32 devices in a mesh: pln: 8 (over y, x, core), pen: 4 (over z).
Axes of the slice: x: 2, y: 2, z: 4, core: 2. Of those that a mesh axis runs over, the one named last changes fastest.
Arguments:
- block_owner: int32 [4096, 1], P(('pln', 'pen')), may hold values from 0 to 31; in each aligned block of 128 rows (0 to 127, 128 to 255, ...) at most 8 rows name the same one
- block_band: int32 [4096], P(('pln', 'pen')), may hold values from 0 to 31
- block_count: int32 [4096], P(('pln', 'pen')), may hold values from 1 to 128
- cells: int32 [4096, 128], P(('pln', 'pen')), may hold values from 0 to 8191
- offsets: float32 [4096, 2, 128], P(('pln', 'pen')), may hold values from 0 to 1
- charges: float32 [4096, 128], P(('pln', 'pen')), may hold values from -5 to 5
Outputs:
- potential: float32 [8, 1024, 1024], P('pln', 'pen')
- forces: float32 [4096, 2, 128], P(('pln', 'pen'))
The draws below stay inside these ranges and needn't reach their ends.
Inputs may be any that keep to these rules, and one draw needn't show every extreme that they name: `block_owner`: among the blocks of one device no owner is named more than 8 times, a bound that some block reaches.
All inputs are finite; a program needn't handle non-finite values.
Results may differ from the reference program's by a relative error of at most 0.0044.
Values sent between devices are 32-bit elements; how exact they have to be, the bound alone decides.
A program may use at most 64 MiB of HBM per device.

```python
import math
import jax
import jax.numpy as jnp
import numpy as np
from jax import lax

NG = 1024
BLK = 128
NB_DEV = 128
PLANES = 8
RY = 256
BANDS = 32
CAP = 8
NB_ALL = 4096
DEVICES = 32


def cell_table(key):
    return jax.random.randint(jax.random.fold_in(key, 11), (NB_ALL, BLK), 0, 8 * NG, dtype=jnp.int32)


def draw_cells(key, part):
    return cell_table(key)


def draw_charges(key, part):
    column = (cell_table(key) % NG).astype(jnp.float32)
    wave_key, angle_key, jitter_key = jax.random.split(jax.random.fold_in(key, 23), 3)
    wavenumber = jax.random.randint(wave_key, (), 9, 13, dtype=jnp.int32).astype(jnp.float32)
    start_angle = jax.random.uniform(angle_key, (), jnp.float32, -math.pi, math.pi)
    jitter = jnp.clip(jax.random.normal(jitter_key, (NB_ALL, BLK), jnp.float32), -4.0, 4.0)
    height = 0.6
    return jitter + height * jnp.cos(2.0 * math.pi * wavenumber * column / NG + start_angle)


def touch_ends(array, own_key, least, top_value):
    shape = array.shape
    place = [jax.random.randint(jax.random.fold_in(own_key, axis), (), 0, shape[axis]) for axis in range(len(shape))]
    array = array.at[tuple(place)].set(least)
    longest = shape.index(max(shape))
    place[longest] = (place[longest] + 1) % shape[longest]
    return array.at[tuple(place)].set(top_value)


def shard_levels(rng, dims, cuts, low, high):
    loudness, own = 1.0, jax.random.fold_in(rng, 6)
    for position, blocks in cuts:
        heights = jnp.exp(jax.random.uniform(jax.random.fold_in(own, position), (blocks,), jnp.float32, low / len(cuts), high / len(cuts)))
        loudness = loudness * jnp.repeat(heights, dims[position] // blocks).reshape([-1 if axis == position else 1 for axis in range(len(dims))])
    return loudness


def assign_block(rng, own, number, rows, count, top, most, lean):
    sequence = jax.random.permutation(rng, count)
    crowded, usual = shares(count, rows * top, most, lean, True), shares(count, rows * top, most, lean, False)
    places = jnp.arange(count)

    def named(sizes, rotation):
        used = int((sizes > 0).sum())
        fixed = max(1, used // 4)
        passed = fixed + (places - fixed + rotation * (used - fixed)) % max(1, count - fixed)
        return jnp.zeros((count,), jnp.int32).at[sequence[jnp.where(places < fixed, places, passed)]].set(jnp.asarray(sizes, jnp.int32))

    sizes = jnp.where(number % 4 == 0, named(crowded, number // 4), named(usual, number - number // 4 - 1))
    mixed = jax.random.permutation(jax.random.fold_in(own, 3), count)
    donor, receiver = mixed[0:count // 2 * 2:2], mixed[1:count // 2 * 2:2]
    margin = jnp.minimum(sizes[donor] - 1, most - sizes[receiver]) // 2
    margin = jnp.where((donor == sequence[0]) | (receiver == sequence[0]) | (sizes[receiver] == 0), 0, jnp.maximum(margin, 0))
    passed = jax.random.randint(jax.random.fold_in(own, 4), (count // 2,), 0, 1 << 20) % (margin + 1)
    sizes = sizes.at[donor].add(-passed).at[receiver].add(passed)
    labels = jnp.searchsorted(jnp.cumsum(sizes), jnp.arange(rows * top), side="right").astype(jnp.int32)
    table = labels.reshape(top, rows).T
    table = table[jax.random.permutation(jax.random.fold_in(own, 1), rows)]
    rotation = jax.random.randint(jax.random.fold_in(own, 2), (rows, 1), 0, top)
    return jnp.take_along_axis(table, (jnp.arange(top)[None, :] + rotation) % top, axis=1)


def shares(number_of, total, reach, lean, full):
    portions = [(1 << 20) // math.isqrt(standing ** lean) + 1 for standing in range(1, number_of + 1)]
    largest = reach if full else min(reach, max(-(-total // number_of), total * portions[0] // sum(portions)))
    least = 1 if total - largest >= number_of - 1 else 0
    given, rest = [largest] + [least] * (number_of - 1), total - largest - least * (number_of - 1)
    while rest > 0:
        free = [i for i in range(1, number_of) if given[i] < largest] or [i for i in range(1, number_of) if given[i] < reach]
        whole, budget = sum([portions[i] for i in free]), rest
        for i in free:
            extra = min(reach - given[i], max(1, budget * portions[i] // whole), rest)
            given[i] = given[i] + extra
            rest = rest - extra
    return np.array(given)


def setup_inputs(seed: int = 0) -> dict:
    keys = jax.random.split(jax.random.key(seed), 7)
    block_owner_keys = jax.random.split(jax.random.fold_in(keys[0], 1), NB_ALL // NB_DEV)
    block_owner_turns = jax.random.permutation(jax.random.fold_in(keys[0], 3), NB_ALL // NB_DEV)
    block_owner = jax.vmap(lambda own, number: assign_block(jax.random.fold_in(keys[0], 2), own, number, NB_DEV, DEVICES, 1, CAP, 2))(block_owner_keys, block_owner_turns).reshape((NB_ALL, 1))
    block_band = touch_ends(jax.random.randint(keys[1], (NB_ALL,), 0, BANDS), jax.random.fold_in(keys[1], 1), 0, BANDS - 1).astype(jnp.int32)
    block_count = touch_ends(jax.random.randint(keys[2], (NB_ALL,), 1, BLK + 1), jax.random.fold_in(keys[2], 1), 1, BLK).astype(jnp.int32)
    cells = draw_cells(jax.random.fold_in(keys[6], 71), 0)
    offsets = jnp.clip(1.0 * jax.random.uniform(keys[4], (NB_ALL, 2, BLK), jnp.float32) ** shard_levels(keys[4], (NB_ALL, 2, BLK), ((0, 32),), -0.2, 0.2), 0.0, 1.0)
    charges = draw_charges(jax.random.fold_in(keys[6], 71), 0)
    return dict(block_owner=block_owner, block_band=block_band, block_count=block_count, cells=cells, offsets=offsets, charges=charges)


screening = 2e-5


def rounded(values):
    return lax.optimization_barrier(values.astype(jnp.bfloat16)).astype(jnp.float32)


def reference(block_owner, block_band, block_count, cells, offsets, charges):
    pencils = NG // RY
    owner = block_owner[:, 0]
    slots = jnp.arange(charges.shape[1], dtype=jnp.int32)
    weight = jnp.where(slots[None, :] < block_count[:, None], charges, jnp.zeros_like(charges))
    plane = (owner // pencils)[:, None]
    row = ((owner % pencils) * RY + 8 * block_band)[:, None] + cells // NG
    column = cells % NG
    next_row = (row + 1) % NG
    next_column = (column + 1) % NG
    frac_x = offsets[:, 0]
    frac_y = offsets[:, 1]
    lower = rounded(weight * (1.0 - frac_y))
    upper = rounded(weight * frac_y)
    left = rounded(1.0 - frac_x)
    right = rounded(frac_x)

    def flat(row_idx, col_idx):
        return (plane * NG * NG + row_idx * NG + col_idx).reshape(-1)

    density = jnp.zeros((PLANES * NG * NG,), jnp.float32)
    density = density.at[flat(row, column)].add((lower * left).reshape(-1))
    density = density.at[flat(row, next_column)].add((lower * right).reshape(-1))
    density = density.at[flat(next_row, column)].add((upper * left).reshape(-1))
    density = density.at[flat(next_row, next_column)].add((upper * right).reshape(-1))
    grid = density.reshape(PLANES, NG, NG)
    freq = jnp.arange(NG).astype(jnp.float32)
    sines = jnp.sin(math.pi * freq / NG)
    green = 1.0 / (4.0 * sines[:, None] ** 2 + 4.0 * sines[None, :] ** 2 + screening)
    potential = jnp.real(jnp.fft.ifft2(jnp.fft.fft2(grid) * green)).astype(jnp.float32)

    def derivative(values, axis):
        return -(8.0 * (jnp.roll(values, -1, axis) - jnp.roll(values, 1, axis))
                 - (jnp.roll(values, -2, axis) - jnp.roll(values, 2, axis))) / 12.0

    field = jnp.stack([derivative(potential, 2), derivative(potential, 1)], axis=1)
    shape = cells.shape
    parts = []
    for comp in range(2):
        flat_field = field[:, comp].reshape(-1)
        near = left * flat_field[flat(row, column)].reshape(shape) + right * flat_field[flat(row, next_column)].reshape(shape)
        far = left * flat_field[flat(next_row, column)].reshape(shape) + right * flat_field[flat(next_row, next_column)].reshape(shape)
        parts.append(weight * ((1.0 - frac_y) * near + frac_y * far))
    forces = jnp.stack(parts, axis=1)
    return potential, forces
```

```python
import functools
import math

import jax
import jax.numpy as jnp
import numpy as np
from jax import lax
from jax.experimental import pallas as pl
from jax.experimental.pallas import tpu as pltpu
from jax.sharding import PartitionSpec as P

NG = 1024
LANES = 128
CHUNKS = NG // LANES
screening = 2e-05
VMEM_LIMIT = 62 * 1024 * 1024
UNROLL = 8


def round_up(value, step):
    return -(-value // step) * step


@functools.lru_cache(None)
def hartley_tables():
    index = np.arange(NG)
    angle = 2.0 * np.pi / NG * (index[:, None] * index[None, :] % NG)
    table = np.cos(angle) + np.sin(angle)
    high = table.astype(jnp.bfloat16)
    low = (table - high.astype(np.float64)).astype(jnp.bfloat16)
    return high, low


@functools.lru_cache(None)
def line_tables(pen_count):
    rows = NG // pen_count
    shift = 4.0 * np.sin(np.pi * np.arange(NG) / NG) ** 2 + screening
    root = 1.0 + shift / 2.0 - np.sqrt(shift + shift * shift / 4.0)
    i = np.arange(8)[:, None]

    def power(exponent):
        return root[None, :] ** (exponent + np.zeros((8, 1)))

    tiles = [
        power(7 - i),
        power(i),
        power(8),
        np.where(i >= 1, power(1), 0.0),
        np.where(i >= 2, power(2), 0.0),
        np.where(i >= 4, power(4), 0.0),
        np.where(i <= 6, power(1), 0.0),
        np.where(i <= 5, power(2), 0.0),
        np.where(i <= 3, power(4), 0.0),
        power(i + 1),
        power(8 - i),
        np.broadcast_to(1.0 / ((1.0 / root - root) * NG), (8, NG)),
        np.broadcast_to(2.0 + shift, (8, NG)),
        power(rows - 1),
    ]
    lags = np.arange(round_up(pen_count, 8))[:, None]
    tiles.append(root[None, :] ** (lags * rows) / (1.0 - root[None, :] ** NG))
    return np.concatenate(tiles, axis=0).astype(np.float32)


T_FEND, T_BEND, T_EIGHT, T_F1, T_F2, T_F4, T_B1, T_B2, T_B4, T_FC, T_BC, T_NORM, T_DIAG, T_LAST, T_LAG = range(15)


def fetch(sources, targets, sems):
    copies = [pltpu.make_async_copy(a, b, sems.at[i]) for i, (a, b) in enumerate(zip(sources, targets))]
    for copy in copies:
        copy.start()
    return copies


def pack_kernel(capacity, owner_h, band_h, count_h, cells_h, offsets_h, charges_h, out, header, target,
                owner, band, count, cells, offsets, charges, used, sems):
    devices = out.shape[0]
    copies = fetch(
        (owner_h, band_h, count_h, cells_h, offsets_h, charges_h),
        (owner, band, count, cells, offsets, charges),
        sems,
    )
    out[...] = jnp.zeros(out.shape, jnp.float32)
    header[...] = jnp.full(header.shape, -1, jnp.int32)

    def clear(i, carry):
        used[i] = 0
        return carry

    lax.fori_loop(0, devices, clear, 0)
    lane = lax.broadcasted_iota(jnp.int32, (1, LANES), 1)
    for copy in copies:
        copy.wait()

    def place(i, carry):
        o = owner[i]
        j = used[o]
        used[o] = j + 1
        target[i] = o * capacity + j
        pair = offsets[i]
        out[o, pl.ds(j, 1), :] = pair[0:1]
        out[o, pl.ds(capacity + j, 1), :] = pair[1:2]
        out[o, pl.ds(2 * capacity + j, 1), :] = jnp.where(lane < count[i], charges[pl.ds(i, 1), :], 0.0)
        out[o, pl.ds(3 * capacity + j, 1), :] = cells[pl.ds(i, 1), :].astype(jnp.float32)
        header[o] = jnp.where(lane == j, band[i], header[o])
        return carry

    lax.fori_loop(0, owner.shape[0], place, 0)


def peer(index, pens):
    return (lax.div(index, pens), lax.rem(index, pens))


def exchange_kernel(planes, pens, arrays, *refs):
    sources, targets = refs[:arrays], refs[arrays : 2 * arrays]
    send_sems, recv_sems, own_sems = refs[2 * arrays :]
    count = planes * pens
    me = lax.axis_index("pln") * pens + lax.axis_index("pen")
    barrier = pltpu.get_barrier_semaphore()

    def greet(k, carry):
        other = peer(lax.rem(me + k, count), pens)
        pl.semaphore_signal(barrier, inc=1, device_id=other, device_id_type=pl.DeviceIdType.MESH)
        return carry

    own = [
        pltpu.make_async_copy(sources[n].at[me], targets[n].at[me], own_sems.at[n]) for n in range(arrays)
    ]
    for copy in own:
        copy.start()
    lax.fori_loop(1, count, greet, 0)
    pl.semaphore_wait(barrier, count - 1)

    def copy_of(n, k, source, target, other):
        return pltpu.make_async_remote_copy(
            src_ref=sources[n].at[source],
            dst_ref=targets[n].at[target],
            send_sem=send_sems.at[n, k],
            recv_sem=recv_sems.at[n, k],
            device_id=peer(other, pens),
            device_id_type=pl.DeviceIdType.MESH,
        )

    def send(k, carry):
        to = lax.rem(me + k, count)
        for n in range(arrays):
            copy_of(n, k, to, me, to).start()
        return carry

    def finish(k, carry):
        to = lax.rem(me + k, count)
        behind = lax.rem(me - k + count, count)
        for n in range(arrays):
            copy_of(n, k, to, me, to).wait_send()
            copy_of(n, k, me, behind, behind).wait_recv()
        return carry

    lax.fori_loop(1, count, send, 0)
    lax.fori_loop(1, count, finish, 0)
    for copy in own:
        copy.wait()


def exchange(values, planes, pens, number):
    place = pl.BlockSpec(memory_space=pl.ANY)
    arrays = len(values)
    return pl.pallas_call(
        functools.partial(exchange_kernel, planes, pens, arrays),
        out_shape=tuple(jax.ShapeDtypeStruct(v.shape, v.dtype) for v in values),
        in_specs=[place] * arrays,
        out_specs=(place,) * arrays,
        scratch_shapes=[
            pltpu.SemaphoreType.DMA((arrays, planes * pens)),
            pltpu.SemaphoreType.DMA((arrays, planes * pens)),
            pltpu.SemaphoreType.DMA((arrays,)),
        ],
        compiler_params=pltpu.CompilerParams(
            collective_id=number, has_side_effects=True, vmem_limit_bytes=VMEM_LIMIT
        ),
        name="exchange",
    )(*values)


def live_list(header, live, capacity):
    def check(d, n):
        for j in range(capacity):
            live[n] = d * capacity + j
            n = n + jnp.where(header[d, 0, j] >= 0, 1, 0)
        return n

    return lax.fori_loop(0, header.shape[0], check, jnp.int32(0))


def particle(recv, capacity, s):
    d = s // capacity
    j = s % capacity

    def spread(which):
        return recv[d, pl.ds(which * capacity + j, 8, stride=0), :]

    return factors(spread(0), spread(1), spread(2), spread(3))


def factors(frac_x, frac_y, weight, cell):
    cell = cell.astype(jnp.int32)
    column = cell & (NG - 1)
    after = (column + 1) & (NG - 1)
    row = cell >> (NG.bit_length() - 1)
    left = (1.0 - frac_x).astype(jnp.bfloat16).astype(jnp.float32)
    right = frac_x.astype(jnp.bfloat16).astype(jnp.float32)
    return frac_y, weight, row, column, after, left, right


def dot3(a_high, a_low, b_high, b_low):
    dot = functools.partial(jnp.dot, preferred_element_type=jnp.float32)
    return dot(a_high, b_high) + (dot(a_high, b_low) + dot(a_low, b_high))


def split(values):
    high = values.astype(jnp.bfloat16)
    return high, (values - high.astype(jnp.float32)).astype(jnp.bfloat16)


def deposit_kernel(capacity, rows, header_h, recv_h, table_high_h, table_low_h, lines_h, spectrum, edges,
                   live, dens, hi, lo, tails, header, recv, table_high, table_low, lines, sems):
    copies = fetch(
        (header_h, recv_h, table_high_h, table_low_h, lines_h),
        (header, recv.at[:, 0 : 4 * capacity], table_high, table_low, lines),
        sems,
    )
    dens[...] = jnp.zeros(dens.shape, jnp.float32)
    tails[...] = jnp.zeros(tails.shape, jnp.float32)
    copies[0].wait()
    n_live = live_list(header, live, capacity)
    copies[1].wait()
    sub8 = lax.broadcasted_iota(jnp.int32, (8, LANES), 0)
    places = [sub8 + 8 * b for b in range(LANES // 8)]

    def one(slot_at):
        alive = slot_at < n_live
        s = live[jnp.where(alive, slot_at, 0)]
        frac_y, weight, row, column, after, left, right = particle(recv, capacity, s)
        weight = jnp.where(alive, weight, 0.0)
        lower = (weight * (1.0 - frac_y)).astype(jnp.bfloat16).astype(jnp.float32)
        upper = (weight * frac_y).astype(jnp.bfloat16).astype(jnp.float32)
        main = jnp.where(row == sub8, lower, jnp.where(row + 1 == sub8, upper, 0.0))
        tail = jnp.where(row == 7, upper, 0.0)

        def row_side(chunk):
            tiles = [jnp.where(chunk == a, main, 0.0) for a in range(CHUNKS)]
            tiles += [jnp.where(chunk == sub8, tail, 0.0), jnp.zeros((8, LANES), jnp.float32)]
            return jnp.concatenate(tiles, axis=0).astype(jnp.bfloat16)

        def column_side(lane, factor):
            return jnp.concatenate([jnp.where(lane == b, factor, 0.0) for b in places], axis=0).astype(jnp.bfloat16)

        lhs = jnp.concatenate([row_side(column >> 7), row_side(after >> 7)], axis=1)
        rhs = jnp.concatenate([column_side(column & 127, left), column_side(after & 127, right)], axis=1)
        values = lax.dot_general(lhs, rhs, (((1,), (1,)), ((), ())), preferred_element_type=jnp.float32)
        return jnp.maximum(header[s // capacity, 0, s % capacity], 0), values

    def group(g, carry):
        results = [one(g * UNROLL + k) for k in range(UNROLL)]
        for band, values in results:
            start = pl.multiple_of(band * 8, 8)
            for a in range(CHUNKS):
                dens[pl.ds(start, 8), a * LANES : (a + 1) * LANES] += values[a * 8 : (a + 1) * 8]
            tails[band] += values[CHUNKS * 8 : CHUNKS * 8 + 8]
        return carry

    lax.fori_loop(0, (n_live + UNROLL - 1) // UNROLL, group, 0)

    def carry_row(t, carry):
        start = pl.multiple_of(t * 8 + 8, 8)
        extra = tails[t]
        for a in range(CHUNKS):
            dens[pl.ds(start, 1), a * LANES : (a + 1) * LANES] += extra[a : a + 1]
        return carry

    lax.fori_loop(0, rows // 8, carry_row, 0)
    high, low = split(dens[...])
    hi[...] = high
    lo[...] = low
    width = 256
    for copy in copies[2:]:
        copy.wait()
    for n in range(NG // width):
        cols = slice(n * width, (n + 1) * width)
        values = dot3(hi[...], lo[...], table_high[:, cols], table_low[:, cols])
        spectrum[:, cols] = values[:rows]
        edges[2:3, cols] = values[rows : rows + 1]
    eight = lines[T_EIGHT * 8 : T_EIGHT * 8 + 8]
    tiles = rows // 8

    def fold(t, carry):
        fwd, bwd = carry
        fwd = eight * fwd + spectrum[pl.ds(pl.multiple_of(t * 8, 8), 8), :]
        bwd = eight * bwd + spectrum[pl.ds(pl.multiple_of((tiles - 1 - t) * 8, 8), 8), :]
        return fwd, bwd

    nothing = jnp.zeros((8, NG), jnp.float32)
    fwd, bwd = lax.fori_loop(0, tiles, fold, (nothing, nothing))
    edges[0:1] = jnp.sum(fwd * lines[T_FEND * 8 : T_FEND * 8 + 8], axis=0, keepdims=True)
    edges[1:2] = jnp.sum(bwd * lines[T_BEND * 8 : T_BEND * 8 + 8], axis=0, keepdims=True)
    edges[3:5] = spectrum[0:2]
    edges[5:6] = spectrum[rows - 1 : rows]
    edges[6:8] = jnp.zeros((2, NG), jnp.float32)


def solve(rows, mine, copies, potential_h, out_sem, rim, wave, hi, lo, field, potential, spectrum, gathered,
          table_high, table_low, lines):
    pens = gathered.shape[0]
    def table(which):
        return lines[which * 8 : which * 8 + 8]

    def row_of(pen, which):
        return gathered[lax.rem(pen + 2 * pens, pens), which : which + 1]

    last_power = table(T_LAST)[0:1]
    before = jnp.zeros((1, NG), jnp.float32)
    beyond = jnp.zeros((1, NG), jnp.float32)
    for j in range(pens):
        lag = lines[T_LAG * 8 + j : T_LAG * 8 + j + 1]
        behind, ahead = mine - 1 - j, mine + 1 + j
        before += lag * (row_of(behind, 0) + last_power * row_of(behind - 1, 2))
        beyond += lag * (row_of(ahead, 1) + row_of(ahead - 1, 2))
    incoming = row_of(mine - 1, 2)
    next_zero = row_of(mine + 1, 3) + row_of(mine, 2)
    next_one = row_of(mine + 1, 4)
    last_before = row_of(mine - 1, 5)
    spectrum_first = spectrum[0:1] + incoming
    first_row = lax.broadcasted_iota(jnp.int32, (8, NG), 0) == 0
    tiles = rows // 8

    def tile_of(t):
        values = spectrum[pl.ds(pl.multiple_of(t * 8, 8), 8), :]
        return values + jnp.where(first_row & (t == 0), incoming, 0.0)

    def backward(i, carry):
        t = tiles - 1 - i
        x = tile_of(t)
        x = x + table(T_B1) * pltpu.roll(x, 7, 0)
        x = x + table(T_B2) * pltpu.roll(x, 6, 0)
        x = x + table(T_B4) * pltpu.roll(x, 4, 0)
        x = x + table(T_BC) * carry
        wave[pl.ds(pl.multiple_of(t * 8 + 8, 8), 8), :] = x
        return x[0:1]

    first_back = lax.fori_loop(0, tiles, backward, beyond)
    norm = table(T_NORM)[0:1]

    def forward(t, carry):
        d = tile_of(t)
        x = d + table(T_F1) * pltpu.roll(d, 1, 0)
        x = x + table(T_F2) * pltpu.roll(x, 2, 0)
        x = x + table(T_F4) * pltpu.roll(x, 4, 0)
        x = x + table(T_FC) * carry
        where = pl.ds(pl.multiple_of(t * 8 + 8, 8), 8)
        wave[where, :] = table(T_NORM) * (x + wave[where, :] - d)
        return x[7:8]

    final = lax.fori_loop(0, tiles, forward, before)
    diagonal = table(T_DIAG)[0:1]
    root = table(T_FC)[0:1]
    scale = 1.0 / NG
    up1 = norm * (before + root * first_back)
    up2 = diagonal * up1 - wave[8:9] - scale * last_before
    down0 = norm * (root * final + beyond)
    down1 = diagonal * down0 - wave[rows + 7 : rows + 8] - scale * next_zero
    down2 = diagonal * down1 - down0 - scale * next_one
    wave[0:6] = jnp.zeros((6, NG), jnp.float32)
    wave[6:7] = up2
    wave[7:8] = up1
    wave[rows + 8 : rows + 9] = down0
    wave[rows + 9 : rows + 10] = down1
    wave[rows + 10 : rows + 11] = down2
    wave[rows + 11 : rows + 16] = jnp.zeros((5, NG), jnp.float32)
    high, low = split(wave[...])
    hi[...] = high
    lo[...] = low
    width = 256
    for copy in copies:
        copy.wait()
    for n in range(NG // width):
        cols = slice(n * width, (n + 1) * width)
        wave[:, cols] = dot3(hi[...], lo[...], table_high[:, cols], table_low[:, cols])
    potential[...] = wave[8 : rows + 8]
    out_copy = pltpu.make_async_copy(potential, potential_h, out_sem)
    out_copy.start()

    def derive(t, carry):
        base = pl.multiple_of(t * 8, 8)
        tall = jnp.concatenate(
            [
                wave[pl.ds(base, 8), :],
                wave[pl.ds(pl.multiple_of(base + 8, 8), 8), :],
                wave[pl.ds(pl.multiple_of(jnp.minimum(base + 16, rows + 8), 8), 8), :],
            ],
            axis=0,
        )
        middle = tall[8:16]
        along_x = (8.0 * (pltpu.roll(middle, NG - 1, 1) - pltpu.roll(middle, 1, 1))
                   - (pltpu.roll(middle, NG - 2, 1) - pltpu.roll(middle, 2, 1))) / -12.0
        along_y = (8.0 * (tall[9:17] - tall[7:15]) - (tall[10:18] - tall[6:14])) / -12.0

        @pl.when(t < tiles)
        def _():
            field[t] = jnp.concatenate([along_x, along_y], axis=0).astype(jnp.bfloat16)

        @pl.when(t > 0)
        def _():
            ends = []
            for a in range(CHUNKS):
                lanes = slice(a * LANES, (a + 1) * LANES)
                ends += [along_x[0:1, lanes], along_y[0:1, lanes]]
            near = jnp.concatenate(ends, axis=0)
            far = jnp.concatenate(ends[2:] + ends[:2], axis=0)
            rim[t - 1] = jnp.concatenate([near, far], axis=1).astype(jnp.bfloat16)

        return carry

    lax.fori_loop(0, tiles + 1, derive, 0)
    return out_copy


def pull_kernel(planes, pens, capacity, rows, target, header_h, recv_h, spectrum_h, edges_h, table_high_h, table_low_h,
                lines_h, potential_h, out, forces, returned, header, recv, field, rim, wave, hi, lo, potential,
                spectrum, edges, gathered, table_high, table_low, lines, sems, send_sems, recv_sems,
                edge_send_sems, edge_recv_sems):
    count = planes * pens
    me = lax.axis_index("pln") * pens + lax.axis_index("pen")
    barrier = pltpu.get_barrier_semaphore()
    copies = fetch(
        (edges_h, lines_h, spectrum_h, table_high_h, table_low_h, header_h, recv_h),
        (edges, lines, spectrum, table_high, table_low, header, recv),
        sems,
    )
    plane = lax.axis_index("pln")
    mine = lax.axis_index("pen")

    def greet(k, carry):
        other = peer(lax.rem(me + k, count), pens)
        pl.semaphore_signal(barrier, inc=1, device_id=other, device_id_type=pl.DeviceIdType.MESH)
        return carry

    lax.fori_loop(1, count, greet, 0)
    for copy in copies[:3]:
        copy.wait()
    gathered[mine] = edges[...]
    pl.semaphore_wait(barrier, count - 1)

    def edge_copy(k, place, other):
        return pltpu.make_async_remote_copy(
            src_ref=edges,
            dst_ref=gathered.at[place],
            send_sem=edge_send_sems.at[k],
            recv_sem=edge_recv_sems.at[k],
            device_id=(plane, other),
            device_id_type=pl.DeviceIdType.MESH,
        )

    for k in range(1, pens):
        edge_copy(k, mine, lax.rem(mine + k, pens)).start()
    for k in range(1, pens):
        behind = lax.rem(mine - k + pens, pens)
        edge_copy(k, mine, lax.rem(mine + k, pens)).wait_send()
        edge_copy(k, behind, behind).wait_recv()
    out_copy = solve(rows, mine, copies[3:5], potential_h, sems.at[7], rim, wave, hi, lo, field, potential, spectrum,
                     gathered, table_high, table_low, lines)
    for copy in copies[5:]:
        copy.wait()
    sub8 = lax.broadcasted_iota(jnp.int32, (8, LANES), 0)
    odd = (sub8 & 1) == 1
    pair = sub8 >> 1
    sub16 = lax.broadcasted_iota(jnp.int32, (16, LANES), 0).astype(jnp.float32).astype(jnp.bfloat16)
    zero16 = jnp.zeros((16, LANES), jnp.bfloat16)

    def doubled(values):
        return jnp.concatenate([values, values], axis=0).astype(jnp.bfloat16)

    def one(d, j):
        def spread(which):
            at = which * capacity + j
            return jnp.broadcast_to(recv[d, at : at + 1, :], (8, LANES))

        band = jnp.maximum(header[d, 0, j], 0)
        frac_y, weight, row, column, after, left, right = factors(
            spread(0), spread(1), spread(2), spread(3)
        )
        chunk = column >> 7
        index = (column & 127).astype(jnp.float32)
        spot, left16, right16 = doubled(index), doubled(left), doubled(right)
        next_spot = doubled(index + 1.0)
        picks = []
        for b in range(LANES // 16 + 1):
            here = sub16 + float(16 * b)
            picks.append(jnp.where(here == spot, left16, jnp.where(here == next_spot, right16, zero16)))
        picks += [zero16] * (2 * LANES // 16 - len(picks))
        rows_of = field[band]
        windows = [
            jnp.concatenate(
                [
                    rows_of[:, a * LANES : (a + 1) * LANES],
                    rows_of[:, (a + 1) % CHUNKS * LANES : ((a + 1) % CHUNKS + 1) * LANES],
                ],
                axis=1,
            )
            for a in range(CHUNKS)
        ]
        values = jnp.dot(
            jnp.concatenate(windows + [rim[band]], axis=0),
            jnp.concatenate(picks, axis=0),
            preferred_element_type=jnp.float32,
        )
        row_weight = weight * jnp.where(row == sub8, 1.0 - frac_y, jnp.where(row + 1 == sub8, frac_y, 0.0))
        mixed = [values[0:8], values[8:16]]
        for a in range(1, CHUNKS):
            held = chunk == a
            mixed = [jnp.where(held, values[a * 16 + c * 8 : a * 16 + c * 8 + 8], mixed[c]) for c in range(2)]
        edge = weight * jnp.where(row == 7, frac_y, 0.0)
        rims = jnp.where(pair == chunk, values[CHUNKS * 16 : CHUNKS * 16 + 8], 0.0)
        rims = edge * jnp.where(pair + 4 == chunk, values[CHUNKS * 16 + 8 : CHUNKS * 16 + 16], rims)
        return [
            jnp.sum(row_weight * mixed[0] + jnp.where(odd, 0.0, rims), axis=0, keepdims=True),
            jnp.sum(row_weight * mixed[1] + jnp.where(odd, rims, 0.0), axis=0, keepdims=True),
        ]

    def pull(d):
        made = [one(d, j) for j in range(capacity)]
        for c in range(2):
            for j in range(capacity):
                forces[d, c * capacity + j : c * capacity + j + 1, :] = made[j][c]
        if forces.shape[1] > 2 * capacity:
            forces[d, 2 * capacity :, :] = jnp.zeros((forces.shape[1] - 2 * capacity, LANES), jnp.float32)

    def copy_of(k, source, place, other):
        return pltpu.make_async_remote_copy(
            src_ref=forces.at[source],
            dst_ref=returned.at[place],
            send_sem=send_sems.at[k],
            recv_sem=recv_sems.at[k],
            device_id=peer(other, pens),
            device_id_type=pl.DeviceIdType.MESH,
        )

    pull(lax.rem(me + 1, count))

    def step(k, carry):
        to = lax.rem(me + k, count)
        copy_of(k, to, me, to).start()
        pull(lax.rem(me + k + 1, count))
        return carry

    lax.fori_loop(1, count, step, 0)
    returned[me] = forces[me]

    def finish(k, carry):
        to = lax.rem(me + k, count)
        behind = lax.rem(me - k + count, count)
        copy_of(k, to, me, to).wait_send()
        copy_of(k, me, behind, behind).wait_recv()
        return carry

    lax.fori_loop(1, count, finish, 0)

    def take(i, carry):
        d = target[i] // capacity
        j = target[i] % capacity
        out[i, 0:1, :] = returned[d, pl.ds(j, 1), :]
        out[i, 1:2, :] = returned[d, pl.ds(capacity + j, 1), :]
        return carry

    lax.fori_loop(0, out.shape[0], take, 0)
    out_copy.wait()


def shards(block_owner, block_band, block_count, cells, offsets, charges):
    plane_count = lax.axis_size("pln")
    pen_count = lax.axis_size("pen")
    devices = plane_count * pen_count
    local_blocks, block_len = charges.shape
    capacity = max(2, 2 * local_blocks // devices)
    total = devices * capacity
    rows = NG // pen_count
    tall = 4 * capacity
    tall_back = round_up(2 * capacity, 8)
    smem = pl.BlockSpec(memory_space=pltpu.SMEM)
    vmem = pl.BlockSpec(memory_space=pltpu.VMEM)
    far = pl.BlockSpec(memory_space=pltpu.HBM)
    params = pltpu.CompilerParams(vmem_limit_bytes=VMEM_LIMIT)
    packed, header, target = pl.pallas_call(
        functools.partial(pack_kernel, capacity),
        out_shape=(
            jax.ShapeDtypeStruct((devices, tall, LANES), jnp.float32),
            jax.ShapeDtypeStruct((devices, 1, LANES), jnp.int32),
            jax.ShapeDtypeStruct((local_blocks,), jnp.int32),
        ),
        in_specs=[far] * 6,
        out_specs=(vmem, vmem, smem),
        scratch_shapes=[pltpu.SMEM((local_blocks,), jnp.int32)] * 3
        + [
            pltpu.VMEM(cells.shape, jnp.int32),
            pltpu.VMEM(offsets.shape, jnp.float32),
            pltpu.VMEM(charges.shape, jnp.float32),
            pltpu.SMEM((devices,), jnp.int32),
            pltpu.SemaphoreType.DMA((6,)),
        ],
        compiler_params=params,
        name="pack",
    )(block_owner[:, 0], block_band, block_count, cells, offsets, charges)
    received, header = exchange((packed, header), plane_count, pen_count, 0)
    table_high, table_low = (jnp.asarray(t) for t in hartley_tables())
    lines = jnp.asarray(line_tables(pen_count))
    arrived = [
        pltpu.SMEM(header.shape, jnp.int32),
        pltpu.VMEM((devices, tall + 8, LANES), jnp.float32),
    ]
    table_scratch = [
        pltpu.VMEM((NG, NG), jnp.bfloat16),
        pltpu.VMEM((NG, NG), jnp.bfloat16),
        pltpu.VMEM(lines.shape, jnp.float32),
        pltpu.SemaphoreType.DMA((8,)),
    ]
    spectrum, edges = pl.pallas_call(
        functools.partial(deposit_kernel, capacity, rows),
        out_shape=(
            jax.ShapeDtypeStruct((rows, NG), jnp.float32),
            jax.ShapeDtypeStruct((8, NG), jnp.float32),
        ),
        in_specs=[far] * 5,
        out_specs=(vmem, vmem),
        scratch_shapes=[
            pltpu.SMEM((total + 8,), jnp.int32),
            pltpu.VMEM((rows + 8, NG), jnp.float32),
            pltpu.VMEM((rows + 8, NG), jnp.bfloat16),
            pltpu.VMEM((rows + 8, NG), jnp.bfloat16),
            pltpu.VMEM((rows // 8, 8, LANES), jnp.float32),
        ]
        + arrived
        + table_scratch,
        compiler_params=params,
        name="deposit",
    )(header, received, table_high, table_low, lines)
    potential, forces = pl.pallas_call(
        functools.partial(pull_kernel, plane_count, pen_count, capacity, rows),
        out_shape=(
            jax.ShapeDtypeStruct((rows, NG), jnp.float32),
            jax.ShapeDtypeStruct((local_blocks, 2, block_len), jnp.float32),
        ),
        in_specs=[smem] + [far] * 7,
        out_specs=(far, vmem),
        scratch_shapes=[
            pltpu.VMEM((devices, tall_back, LANES), jnp.float32),
            pltpu.VMEM((devices, tall_back, LANES), jnp.float32),
            pltpu.SMEM(header.shape, jnp.int32),
            pltpu.VMEM(received.shape, jnp.float32),
            pltpu.VMEM((rows // 8, 16, NG), jnp.bfloat16),
            pltpu.VMEM((rows // 8, 16, 2 * LANES), jnp.bfloat16),
            pltpu.VMEM((rows + 16, NG), jnp.float32),
            pltpu.VMEM((rows + 16, NG), jnp.bfloat16),
            pltpu.VMEM((rows + 16, NG), jnp.bfloat16),
            pltpu.VMEM((rows, NG), jnp.float32),
            pltpu.VMEM((rows, NG), jnp.float32),
            pltpu.VMEM((8, NG), jnp.float32),
            pltpu.VMEM((pen_count, 8, NG), jnp.float32),
        ]
        + table_scratch
        + [
            pltpu.SemaphoreType.DMA((devices,)),
            pltpu.SemaphoreType.DMA((devices,)),
            pltpu.SemaphoreType.DMA((pen_count,)),
            pltpu.SemaphoreType.DMA((pen_count,)),
        ],
        compiler_params=pltpu.CompilerParams(
            collective_id=2, has_side_effects=True, vmem_limit_bytes=VMEM_LIMIT
        ),
        name="pull",
    )(target, header, received, spectrum, edges, table_high, table_low, lines)
    return (potential[None], forces)


def solution(mesh):
    placed = (
        P(("pln", "pen"), None),
        P(("pln", "pen")),
        P(("pln", "pen")),
        P(("pln", "pen"), None),
        P(("pln", "pen"), None, None),
        P(("pln", "pen"), None),
    )
    return jax.shard_map(
        shards,
        mesh=mesh,
        in_specs=placed,
        out_specs=(P("pln", "pen", None), P(("pln", "pen"), None, None)),
        check_vma=False,
    )
```

```python
import functools
import math

import jax
import jax.numpy as jnp
import numpy as np
from jax import lax
from jax.experimental import pallas as pl
from jax.experimental.pallas import tpu as pltpu
from jax.sharding import PartitionSpec as P

NG = 1024
LANES = 128
CHUNKS = NG // LANES
screening = 2e-05
VMEM_LIMIT = 62 * 1024 * 1024
UNROLL = 8


def round_up(value, step):
    return -(-value // step) * step


@functools.lru_cache(None)
def hartley_tables():
    index = np.arange(NG)
    angle = 2.0 * np.pi / NG * (index[:, None] * index[None, :] % NG)
    table = np.cos(angle) + np.sin(angle)
    high = table.astype(jnp.bfloat16)
    low = (table - high.astype(np.float64)).astype(jnp.bfloat16)
    return high, low


@functools.lru_cache(None)
def line_tables(pen_count):
    rows = NG // pen_count
    shift = 4.0 * np.sin(np.pi * np.arange(NG) / NG) ** 2 + screening
    root = 1.0 + shift / 2.0 - np.sqrt(shift + shift * shift / 4.0)
    i = np.arange(8)[:, None]

    def power(exponent):
        return root[None, :] ** (exponent + np.zeros((8, 1)))

    tiles = [
        power(7 - i),
        power(i),
        power(8),
        np.where(i >= 1, power(1), 0.0),
        np.where(i >= 2, power(2), 0.0),
        np.where(i >= 4, power(4), 0.0),
        np.where(i <= 6, power(1), 0.0),
        np.where(i <= 5, power(2), 0.0),
        np.where(i <= 3, power(4), 0.0),
        power(i + 1),
        power(8 - i),
        np.broadcast_to(1.0 / ((1.0 / root - root) * NG), (8, NG)),
        np.broadcast_to(2.0 + shift, (8, NG)),
        power(rows - 1),
    ]
    lags = np.arange(round_up(pen_count, 8))[:, None]
    tiles.append(root[None, :] ** (lags * rows) / (1.0 - root[None, :] ** NG))
    return np.concatenate(tiles, axis=0).astype(np.float32)


T_FEND, T_BEND, T_EIGHT, T_F1, T_F2, T_F4, T_B1, T_B2, T_B4, T_FC, T_BC, T_NORM, T_DIAG, T_LAST, T_LAG = range(15)


def fetch(sources, targets, sems):
    copies = [pltpu.make_async_copy(a, b, sems.at[i]) for i, (a, b) in enumerate(zip(sources, targets))]
    for copy in copies:
        copy.start()
    return copies


def pack_kernel(capacity, planes, pens, owner_h, band_h, count_h, cells_h, offsets_h, charges_h, out, header, target,
                owner, band, count, cells, offsets, charges, used, sems):
    devices = out.shape[0]
    copies = fetch(
        (owner_h, band_h, count_h, cells_h, offsets_h, charges_h),
        (owner, band, count, cells, offsets, charges),
        sems,
    )
    out[...] = jnp.zeros(out.shape, jnp.float32)
    header[...] = jnp.zeros(header.shape, jnp.int32)
    plane = lax.axis_index("pln")
    mine = lax.axis_index("pen")

    def clear(i, carry):
        used[i] = 0
        return carry

    lax.fori_loop(0, devices, clear, 0)
    lane = lax.broadcasted_iota(jnp.int32, (1, LANES), 1)
    for copy in copies:
        copy.wait()

    def place(i, carry):
        o = owner[i]
        step = ((o % pens) ^ mine) * planes + ((o // pens) ^ plane)
        j = used[step]
        used[step] = j + 1
        target[i] = step * capacity + j
        pair = offsets[i]
        out[step, pl.ds(j, 1), :] = pair[0:1]
        out[step, pl.ds(capacity + j, 1), :] = pair[1:2]
        out[step, pl.ds(2 * capacity + j, 1), :] = jnp.where(lane < count[i], charges[pl.ds(i, 1), :], 0.0)
        out[step, pl.ds(3 * capacity + j, 1), :] = cells[pl.ds(i, 1), :].astype(jnp.float32)
        header[step] = jnp.where(lane == j, band[i], header[step])
        return carry

    lax.fori_loop(0, owner.shape[0], place, 0)


def peer(index, pens):
    return (lax.div(index, pens), lax.rem(index, pens))


def exclusive(a, b, size):
    total = 0
    for bit in range(size.bit_length() - 1):
        p = lax.rem(lax.div(a, 1 << bit), 2)
        q = lax.rem(lax.div(b, 1 << bit), 2)
        total = total + (p + q - 2 * p * q) * (1 << bit)
    return total


def factors(frac_x, frac_y, weight, cell):
    cell = cell.astype(jnp.int32)
    column = cell & (NG - 1)
    after = (column + 1) & (NG - 1)
    row = cell >> (NG.bit_length() - 1)
    left = (1.0 - frac_x).astype(jnp.bfloat16).astype(jnp.float32)
    right = frac_x.astype(jnp.bfloat16).astype(jnp.float32)
    return frac_y, weight, row, column, after, left, right


def dot3(a_high, a_low, b_high, b_low):
    dot = functools.partial(jnp.dot, preferred_element_type=jnp.float32)
    return dot(a_high, b_high) + (dot(a_high, b_low) + dot(a_low, b_high))


def split(values):
    high = values.astype(jnp.bfloat16)
    return high, (values - high.astype(jnp.float32)).astype(jnp.bfloat16)


def doubled(values):
    return jnp.concatenate([values, values], axis=0).astype(jnp.bfloat16)


def iota16():
    return lax.broadcasted_iota(jnp.int32, (16, LANES), 0).astype(jnp.float32).astype(jnp.bfloat16)


def link_blocks(heads, links, capacity):
    count = heads.shape[0]
    total = count * capacity
    lane = lax.broadcasted_iota(jnp.int32, (8, LANES), 1)
    slot = lax.broadcasted_iota(jnp.int32, (8, LANES), 0) * LANES + lane

    def collect(s, bands):
        for j in range(capacity):
            bands = jnp.where(slot == s * capacity + j, heads[s, 0, j], bands)
        return bands

    bands = lax.fori_loop(0, count, collect, jnp.full((8, LANES), -1, jnp.int32))

    def link(s, carry):
        earlier, last = carry
        for j in range(capacity):
            here = s * capacity + j
            band = heads[s, 0, j]
            earlier = jnp.where((bands == band) & (slot > here), here, earlier)
            last = jnp.where(lane == band, here, last)
        return earlier, last

    nobody = jnp.full((8, LANES), total, jnp.int32)
    earlier, last = lax.fori_loop(0, count, link, (nobody, nobody))
    links[0:8] = earlier
    links[8:16] = last


def deposit(s, capacity, recv, chain, links):
    sub8 = lax.broadcasted_iota(jnp.int32, (8, LANES), 0)
    sub16 = iota16()
    upper_half = jnp.where(sub16 < 8.0, 0.0, 1.0).astype(jnp.bfloat16)
    zero16 = jnp.zeros((16, LANES), jnp.bfloat16)

    def one(j):
        def spread(which):
            return recv[s, pl.ds(which * capacity + j, 8, stride=0), :]

        frac_y, weight, row, column, after, left, right = factors(spread(0), spread(1), spread(2), spread(3))
        lower = weight * (1.0 - frac_y)
        upper = weight * frac_y
        main = doubled(jnp.where(row == sub8, lower, jnp.where(row + 1 == sub8, upper, 0.0)))
        tail = doubled(jnp.where(row == 7, upper, 0.0))
        chunk = doubled((column >> 7).astype(jnp.float32))
        index = doubled((column & 127).astype(jnp.float32))
        left16, right16 = doubled(left), doubled(right)
        lhs = [jnp.where(chunk == upper_half + float(2 * a), main, zero16) for a in range(CHUNKS // 2)]
        lhs.append(jnp.where(chunk == sub16, tail, zero16))
        here = [index == sub16 + float(16 * b) for b in range(LANES // 16)]
        rhs = [jnp.where(h, left16, zero16) for h in here] + [jnp.where(h, right16, zero16) for h in here]
        values = lax.dot_general(
            jnp.concatenate(lhs, axis=0),
            jnp.concatenate(rhs, axis=0),
            (((1,), (1,)), ((), ())),
            preferred_element_type=jnp.float32,
        )
        return values[0 : CHUNKS * 8 + 8]

    made = [one(j) for j in range(capacity)]
    for j in range(capacity):
        slot = s * capacity + j
        earlier = links[lax.div(slot, LANES), lax.rem(slot, LANES)]
        for side in range(2):
            lanes = slice(side * LANES, (side + 1) * LANES)
            chain[slot, side, 0 : CHUNKS * 8 + 8] = made[j][:, lanes] + chain[earlier, side, 0 : CHUNKS * 8 + 8]


def assemble(bands, total, chain, links, hi, lo):
    first_row = lax.broadcasted_iota(jnp.int32, (8, LANES), 0) == 0

    def last_of(band):
        inside = (band >= 0) & (band < bands)
        return jnp.where(inside, links[8, jnp.clip(band, 0, bands - 1)], total)

    def rows_of(band):
        mine, above = last_of(band), last_of(band - 1)
        sides = []
        for side in range(2):
            tiles = []
            for a in range(CHUNKS):
                extra = chain[above, side, pl.ds(CHUNKS * 8 + a, 8, stride=0)]
                tiles.append(chain[mine, side, a * 8 : a * 8 + 8] + jnp.where(first_row, extra, 0.0))
            sides.append(jnp.concatenate(tiles, axis=1))
        return sides[0] + pltpu.roll(sides[1], 1, 1)

    def pair(q, carry):
        high, low = split(jnp.concatenate([rows_of(2 * q), rows_of(2 * q + 1)], axis=0))
        at = pl.ds(pl.multiple_of(q * 16, 16), 16)
        hi[at, :] = high
        lo[at, :] = low
        return carry

    lax.fori_loop(0, bands // 2 + 1, pair, 0)


def transform(rows, hi, lo, table_high, table_low, lines, spectrum, edges):
    width = 256
    for n in range(NG // width):
        cols = slice(n * width, (n + 1) * width)
        values = dot3(hi[...], lo[...], table_high[:, cols], table_low[:, cols])
        spectrum[:, cols] = values[:rows]
        edges[2:3, cols] = values[rows : rows + 1]
    eight = lines[T_EIGHT * 8 : T_EIGHT * 8 + 8]
    tiles = rows // 8

    def fold(t, carry):
        fwd, bwd = carry
        fwd = eight * fwd + spectrum[pl.ds(pl.multiple_of(t * 8, 8), 8), :]
        bwd = eight * bwd + spectrum[pl.ds(pl.multiple_of((tiles - 1 - t) * 8, 8), 8), :]
        return fwd, bwd

    nothing = jnp.zeros((8, NG), jnp.float32)
    fwd, bwd = lax.fori_loop(0, tiles, fold, (nothing, nothing))
    edges[0:1] = jnp.sum(fwd * lines[T_FEND * 8 : T_FEND * 8 + 8], axis=0, keepdims=True)
    edges[1:2] = jnp.sum(bwd * lines[T_BEND * 8 : T_BEND * 8 + 8], axis=0, keepdims=True)
    edges[3:5] = spectrum[0:2]
    edges[5:6] = spectrum[rows - 1 : rows]
    edges[6:8] = jnp.zeros((2, NG), jnp.float32)


def local_scans(rows, spectrum, lines, wave):
    tiles = rows // 8

    def table(which):
        return lines[which * 8 : which * 8 + 8]

    def backward(i, carry):
        t = tiles - 1 - i
        where = pl.ds(pl.multiple_of(t * 8, 8), 8)
        x = spectrum[where, :]
        x = x + table(T_B1) * pltpu.roll(x, 7, 0)
        x = x + table(T_B2) * pltpu.roll(x, 6, 0)
        x = x + table(T_B4) * pltpu.roll(x, 4, 0)
        x = x + table(T_BC) * carry
        wave[where, :] = x
        return x[0:1]

    nothing = jnp.zeros((1, NG), jnp.float32)
    lax.fori_loop(0, tiles, backward, nothing)

    def forward(t, carry):
        where = pl.ds(pl.multiple_of(t * 8, 8), 8)
        d = spectrum[where, :]
        x = d + table(T_F1) * pltpu.roll(d, 1, 0)
        x = x + table(T_F2) * pltpu.roll(x, 2, 0)
        x = x + table(T_F4) * pltpu.roll(x, 4, 0)
        x = x + table(T_FC) * carry
        wave[where, :] = x + wave[where, :] - d
        return x[7:8]

    lax.fori_loop(0, tiles, forward, nothing)


def finish_solve(rows, mine, gathered, lines, wave, hi, lo):
    pens = gathered.shape[0]
    tiles = rows // 8

    def table(which):
        return lines[which * 8 : which * 8 + 8]

    def row_of(pen, which):
        return gathered[lax.rem(pen + 2 * pens, pens), which : which + 1]

    last_power = table(T_LAST)[0:1]
    before = jnp.zeros((1, NG), jnp.float32)
    beyond = jnp.zeros((1, NG), jnp.float32)
    for j in range(pens):
        lag = lines[T_LAG * 8 + j : T_LAG * 8 + j + 1]
        behind, ahead = mine - 1 - j, mine + 1 + j
        before += lag * (row_of(behind, 0) + last_power * row_of(behind - 1, 2))
        beyond += lag * (row_of(ahead, 1) + row_of(ahead - 1, 2))
    incoming = row_of(mine - 1, 2)
    next_zero = row_of(mine + 1, 3) + row_of(mine, 2)
    next_one = row_of(mine + 1, 4)
    last_before = row_of(mine - 1, 5)
    norm = table(T_NORM)[0:1]
    root = table(T_FC)[0:1]
    eight = table(T_EIGHT)
    ramp_down = norm * (root * before + incoming)
    ramp_up = norm * beyond
    first_back = row_of(mine, 1) + incoming + root * last_power * beyond
    final = row_of(mine, 0) + last_power * incoming + root * last_power * before

    def add_beyond(i, ramp):
        t = tiles - 1 - i
        where = pl.ds(pl.multiple_of(t * 8, 8), 8)
        wave[where, :] = table(T_NORM) * wave[where, :] + ramp
        return ramp * eight

    lax.fori_loop(0, tiles, add_beyond, table(T_BC) * ramp_up)

    def add_before(q, ramp):
        parts = []
        for k in range(2):
            where = pl.ds(pl.multiple_of(q * 16 + k * 8, 8), 8)
            value = wave[where, :] + ramp
            wave[where, :] = value
            parts.append(value)
            ramp = ramp * eight
        high, low = split(jnp.concatenate(parts, axis=0))
        at = pl.ds(pl.multiple_of(q * 16, 16), 16)
        hi[at, :] = high
        lo[at, :] = low
        return ramp

    lax.fori_loop(0, tiles // 2, add_before, table(T_BEND) * ramp_down)
    diagonal = table(T_DIAG)[0:1]
    scale = 1.0 / NG
    up1 = norm * (before + root * first_back)
    up2 = diagonal * up1 - wave[0:1] - scale * last_before
    down0 = norm * (root * final + beyond)
    down1 = diagonal * down0 - wave[rows - 1 : rows] - scale * next_zero
    down2 = diagonal * down1 - down0 - scale * next_one
    halo = jnp.concatenate([down0, down1, down2, jnp.zeros((11, NG), jnp.float32), up2, up1], axis=0)
    high, low = split(halo)
    hi[rows : rows + 16] = high
    lo[rows : rows + 16] = low


def invert(rows, hi, lo, table_high, table_low, wave, potential_h, out_sem, rim, field):
    width = 256
    tiles = rows // 8
    for n in range(NG // width):
        cols = slice(n * width, (n + 1) * width)
        wave[:, cols] = dot3(hi[...], lo[...], table_high[:, cols], table_low[:, cols])
    out_copy = pltpu.make_async_copy(wave.at[0:rows], potential_h, out_sem)
    out_copy.start()

    def derive(t, carry):
        def tile(n):
            return wave[pl.ds(pl.multiple_of(n * 8, 8), 8), :]

        middle = tile(t)
        tall = jnp.concatenate([tile(lax.rem(t + tiles + 1, tiles + 2)), middle, tile(jnp.minimum(t + 1, tiles + 1))], axis=0)
        along_x = (8.0 * (pltpu.roll(middle, NG - 1, 1) - pltpu.roll(middle, 1, 1))
                   - (pltpu.roll(middle, NG - 2, 1) - pltpu.roll(middle, 2, 1))) / -12.0
        along_y = (8.0 * (tall[9:17] - tall[7:15]) - (tall[10:18] - tall[6:14])) / -12.0

        @pl.when(t < tiles)
        def _():
            field[t] = jnp.concatenate([along_x, along_y], axis=0).astype(jnp.bfloat16)

        @pl.when(t > 0)
        def _():
            ends = []
            for a in range(CHUNKS):
                lanes = slice(a * LANES, (a + 1) * LANES)
                ends += [along_x[0:1, lanes], along_y[0:1, lanes]]
            near = jnp.concatenate(ends, axis=0)
            far = jnp.concatenate(ends[2:] + ends[:2], axis=0)
            rim[t - 1] = jnp.concatenate([near, far], axis=1).astype(jnp.bfloat16)

        return carry

    lax.fori_loop(0, tiles + 1, derive, 0)
    return out_copy


def mesh_kernel(planes, pens, capacity, rows, target, packed_h, header_h, table_high_h, table_low_h, lines_h,
                potential_h, out, forces, returned, recv, heads, heads_s, links_v, links, chain, field, rim, wave, hi, lo,
                spectrum, edges, gathered, table_high, table_low, lines, sems, send_sems, recv_sems, head_send_sems,
                head_recv_sems, back_send_sems, back_recv_sems, edge_send_sems, edge_recv_sems):
    count = planes * pens
    total = count * capacity
    tall = 4 * capacity
    plane = lax.axis_index("pln")
    mine = lax.axis_index("pen")
    barrier = pltpu.get_barrier_semaphore()

    def partner(s):
        return (
            exclusive(plane, lax.rem(s, planes), planes),
            exclusive(mine, lax.div(s, planes), pens),
        )

    def greet(s, carry):
        pl.semaphore_signal(barrier, inc=1, device_id=partner(s), device_id_type=pl.DeviceIdType.MESH)
        return carry

    lax.fori_loop(1, count, greet, 0)
    copies = fetch(
        (packed_h.at[0], header_h.at[0], lines_h, table_high_h, table_low_h),
        (recv.at[0, 0:tall], heads.at[0], lines, table_high, table_low),
        sems,
    )
    chain[total] = jnp.zeros(chain.shape[1:], jnp.float32)
    pl.semaphore_wait(barrier, count - 1)

    def remote(s, source, place, send, receive):
        return pltpu.make_async_remote_copy(
            src_ref=source,
            dst_ref=place,
            send_sem=send.at[s],
            recv_sem=receive.at[s],
            device_id=partner(s),
            device_id_type=pl.DeviceIdType.MESH,
        )

    def head_copy(s):
        return remote(s, header_h.at[s], heads.at[s], head_send_sems, head_recv_sems)

    def block_copy(s):
        return remote(s, packed_h.at[s], recv.at[s, 0:tall], send_sems, recv_sems)

    def back_copy(s):
        return remote(s, forces.at[s], returned.at[s], back_send_sems, back_recv_sems)

    def send_heads(s, carry):
        head_copy(s).start()
        return carry

    def send_blocks(s, carry):
        block_copy(s).start()
        return carry

    def take_heads(s, carry):
        head_copy(s).wait_recv()
        return carry

    lax.fori_loop(1, count, send_heads, 0)
    lax.fori_loop(1, count, send_blocks, 0)
    copies[0].wait()
    copies[1].wait()
    lax.fori_loop(1, count, take_heads, 0)
    heads_copy = pltpu.make_async_copy(heads, heads_s, sems.at[5])
    heads_copy.start()
    heads_copy.wait()
    link_blocks(heads_s, links_v, capacity)
    links_copy = pltpu.make_async_copy(links_v, links, sems.at[6])
    links_copy.start()
    links_copy.wait()

    def receive(s, carry):
        @pl.when(s > 0)
        def _():
            block_copy(s).wait_recv()

        deposit(s, capacity, recv, chain, links)
        return carry

    lax.fori_loop(0, count, receive, 0)
    assemble(rows // 8, total, chain, links, hi, lo)
    for copy in copies[2:]:
        copy.wait()
    transform(rows, hi, lo, table_high, table_low, lines, spectrum, edges)
    gathered[mine] = edges[...]

    def edge_copy(k, place, other):
        return pltpu.make_async_remote_copy(
            src_ref=edges,
            dst_ref=gathered.at[place],
            send_sem=edge_send_sems.at[k],
            recv_sem=edge_recv_sems.at[k],
            device_id=(plane, other),
            device_id_type=pl.DeviceIdType.MESH,
        )

    for k in range(1, pens):
        edge_copy(k, mine, lax.rem(mine + k, pens)).start()
    local_scans(rows, spectrum, lines, wave)
    for k in range(1, pens):
        behind = lax.rem(mine - k + pens, pens)
        edge_copy(k, mine, lax.rem(mine + k, pens)).wait_send()
        edge_copy(k, behind, behind).wait_recv()
    finish_solve(rows, mine, gathered, lines, wave, hi, lo)
    out_copy = invert(rows, hi, lo, table_high, table_low, wave, potential_h, sems.at[7], rim, field)
    sub8 = lax.broadcasted_iota(jnp.int32, (8, LANES), 0)
    odd = (sub8 & 1) == 1
    pair = sub8 >> 1
    sub16 = iota16()
    zero16 = jnp.zeros((16, LANES), jnp.bfloat16)

    def one(d, j):
        def spread(which):
            at = which * capacity + j
            return jnp.broadcast_to(recv[d, at : at + 1, :], (8, LANES))

        band = heads_s[d, 0, j]
        frac_y, weight, row, column, after, left, right = factors(
            spread(0), spread(1), spread(2), spread(3)
        )
        chunk = column >> 7
        index = (column & 127).astype(jnp.float32)
        spot, left16, right16 = doubled(index), doubled(left), doubled(right)
        next_spot = doubled(index + 1.0)
        picks = []
        for b in range(LANES // 16 + 1):
            here = sub16 + float(16 * b)
            picks.append(jnp.where(here == spot, left16, jnp.where(here == next_spot, right16, zero16)))
        picks += [zero16] * (2 * LANES // 16 - len(picks))
        rows_of = field[band]
        windows = [
            jnp.concatenate(
                [
                    rows_of[:, a * LANES : (a + 1) * LANES],
                    rows_of[:, (a + 1) % CHUNKS * LANES : ((a + 1) % CHUNKS + 1) * LANES],
                ],
                axis=1,
            )
            for a in range(CHUNKS)
        ]
        values = jnp.dot(
            jnp.concatenate(windows + [rim[band]], axis=0),
            jnp.concatenate(picks, axis=0),
            preferred_element_type=jnp.float32,
        )
        row_weight = weight * jnp.where(row == sub8, 1.0 - frac_y, jnp.where(row + 1 == sub8, frac_y, 0.0))
        mixed = [values[0:8], values[8:16]]
        for a in range(1, CHUNKS):
            held = chunk == a
            mixed = [jnp.where(held, values[a * 16 + c * 8 : a * 16 + c * 8 + 8], mixed[c]) for c in range(2)]
        edge = weight * jnp.where(row == 7, frac_y, 0.0)
        rims = jnp.where(pair == chunk, values[CHUNKS * 16 : CHUNKS * 16 + 8], 0.0)
        rims = edge * jnp.where(pair + 4 == chunk, values[CHUNKS * 16 + 8 : CHUNKS * 16 + 16], rims)
        return [
            jnp.sum(row_weight * mixed[0] + jnp.where(odd, 0.0, rims), axis=0, keepdims=True),
            jnp.sum(row_weight * mixed[1] + jnp.where(odd, rims, 0.0), axis=0, keepdims=True),
        ]

    def pull(d):
        made = [one(d, j) for j in range(capacity)]
        for c in range(2):
            for j in range(capacity):
                forces[d, c * capacity + j : c * capacity + j + 1, :] = made[j][c]
        if forces.shape[1] > 2 * capacity:
            forces[d, 2 * capacity :, :] = jnp.zeros((forces.shape[1] - 2 * capacity, LANES), jnp.float32)

    def step(i, carry):
        s = count - i
        pull(s)
        back_copy(s).start()
        return carry

    lax.fori_loop(1, count, step, 0)
    pull(0)
    returned[0] = forces[0]

    def finish(i, carry):
        s = count - i
        head_copy(s).wait_send()
        block_copy(s).wait_send()
        back_copy(s).wait_send()
        back_copy(s).wait_recv()
        return carry

    lax.fori_loop(1, count, finish, 0)

    def take(i, carry):
        d = target[i] // capacity
        j = target[i] % capacity
        out[i, 0:1, :] = returned[d, pl.ds(j, 1), :]
        out[i, 1:2, :] = returned[d, pl.ds(capacity + j, 1), :]
        return carry

    lax.fori_loop(0, out.shape[0], take, 0)
    out_copy.wait()


def shards(block_owner, block_band, block_count, cells, offsets, charges):
    plane_count = lax.axis_size("pln")
    pen_count = lax.axis_size("pen")
    devices = plane_count * pen_count
    local_blocks, block_len = charges.shape
    capacity = max(2, 2 * local_blocks // devices)
    total = devices * capacity
    rows = NG // pen_count
    tall = 4 * capacity
    tall_back = round_up(2 * capacity, 8)
    smem = pl.BlockSpec(memory_space=pltpu.SMEM)
    vmem = pl.BlockSpec(memory_space=pltpu.VMEM)
    far = pl.BlockSpec(memory_space=pltpu.HBM)
    params = pltpu.CompilerParams(vmem_limit_bytes=VMEM_LIMIT)
    packed, header, target = pl.pallas_call(
        functools.partial(pack_kernel, capacity, plane_count, pen_count),
        out_shape=(
            jax.ShapeDtypeStruct((devices, tall, LANES), jnp.float32),
            jax.ShapeDtypeStruct((devices, 1, LANES), jnp.int32),
            jax.ShapeDtypeStruct((local_blocks,), jnp.int32),
        ),
        in_specs=[far] * 6,
        out_specs=(vmem, vmem, smem),
        scratch_shapes=[pltpu.SMEM((local_blocks,), jnp.int32)] * 3
        + [
            pltpu.VMEM(cells.shape, jnp.int32),
            pltpu.VMEM(offsets.shape, jnp.float32),
            pltpu.VMEM(charges.shape, jnp.float32),
            pltpu.SMEM((devices,), jnp.int32),
            pltpu.SemaphoreType.DMA((6,)),
        ],
        compiler_params=params,
        name="pack",
    )(block_owner[:, 0], block_band, block_count, cells, offsets, charges)
    table_high, table_low = (jnp.asarray(t) for t in hartley_tables())
    lines = jnp.asarray(line_tables(pen_count))
    pairs = pltpu.SemaphoreType.DMA((devices,))
    potential, forces = pl.pallas_call(
        functools.partial(mesh_kernel, plane_count, pen_count, capacity, rows),
        out_shape=(
            jax.ShapeDtypeStruct((rows, NG), jnp.float32),
            jax.ShapeDtypeStruct((local_blocks, 2, block_len), jnp.float32),
        ),
        in_specs=[smem] + [far] * 5,
        out_specs=(far, vmem),
        scratch_shapes=[
            pltpu.VMEM((devices, tall_back, LANES), jnp.float32),
            pltpu.VMEM((devices, tall_back, LANES), jnp.float32),
            pltpu.VMEM((devices, tall + 8, LANES), jnp.float32),
            pltpu.VMEM(header.shape, jnp.int32),
            pltpu.SMEM(header.shape, jnp.int32),
            pltpu.VMEM((16, LANES), jnp.int32),
            pltpu.SMEM((16, LANES), jnp.int32),
            pltpu.VMEM((total + 1, 2, CHUNKS * 8 + 16, LANES), jnp.float32),
            pltpu.VMEM((rows // 8, 16, NG), jnp.bfloat16),
            pltpu.VMEM((rows // 8, 16, 2 * LANES), jnp.bfloat16),
            pltpu.VMEM((rows + 16, NG), jnp.float32),
            pltpu.VMEM((rows + 16, NG), jnp.bfloat16),
            pltpu.VMEM((rows + 16, NG), jnp.bfloat16),
            pltpu.VMEM((rows, NG), jnp.float32),
            pltpu.VMEM((8, NG), jnp.float32),
            pltpu.VMEM((pen_count, 8, NG), jnp.float32),
            pltpu.VMEM((NG, NG), jnp.bfloat16),
            pltpu.VMEM((NG, NG), jnp.bfloat16),
            pltpu.VMEM(lines.shape, jnp.float32),
            pltpu.SemaphoreType.DMA((8,)),
            pairs,
            pairs,
            pairs,
            pairs,
            pairs,
            pairs,
            pltpu.SemaphoreType.DMA((pen_count,)),
            pltpu.SemaphoreType.DMA((pen_count,)),
        ],
        compiler_params=pltpu.CompilerParams(
            collective_id=0, has_side_effects=True, vmem_limit_bytes=VMEM_LIMIT
        ),
        name="mesh",
    )(target, packed, header, table_high, table_low, lines)
    return (potential[None], forces)


def solution(mesh):
    placed = (
        P(("pln", "pen"), None),
        P(("pln", "pen")),
        P(("pln", "pen")),
        P(("pln", "pen"), None),
        P(("pln", "pen"), None, None),
        P(("pln", "pen"), None),
    )
    return jax.shard_map(
        shards,
        mesh=mesh,
        in_specs=placed,
        out_specs=(P("pln", "pen", None), P(("pln", "pen"), None, None)),
        check_vma=False,
    )
```

```python
import functools
import math

import jax
import jax.numpy as jnp
import numpy as np
from jax import lax
from jax.experimental import pallas as pl
from jax.experimental.pallas import tpu as pltpu
from jax.sharding import PartitionSpec as P

NG = 1024
LANES = 128
CHUNKS = NG // LANES
screening = 2e-05
VMEM_LIMIT = 62 * 1024 * 1024
UNROLL = 8


def round_up(value, step):
    return -(-value // step) * step


@functools.lru_cache(None)
def hartley_tables():
    index = np.arange(NG)
    angle = 2.0 * np.pi / NG * (index[:, None] * index[None, :] % NG)
    table = np.cos(angle) + np.sin(angle)
    high = table.astype(jnp.bfloat16)
    low = (table - high.astype(np.float64)).astype(jnp.bfloat16)
    return high, low


@functools.lru_cache(None)
def line_tables(pen_count):
    rows = NG // pen_count
    shift = 4.0 * np.sin(np.pi * np.arange(NG) / NG) ** 2 + screening
    root = 1.0 + shift / 2.0 - np.sqrt(shift + shift * shift / 4.0)
    i = np.arange(8)[:, None]

    def power(exponent):
        return root[None, :] ** (exponent + np.zeros((8, 1)))

    tiles = [
        power(7 - i),
        power(i),
        power(8),
        np.where(i >= 1, power(1), 0.0),
        np.where(i >= 2, power(2), 0.0),
        np.where(i >= 4, power(4), 0.0),
        np.where(i <= 6, power(1), 0.0),
        np.where(i <= 5, power(2), 0.0),
        np.where(i <= 3, power(4), 0.0),
        power(i + 1),
        power(8 - i),
        np.broadcast_to(1.0 / ((1.0 / root - root) * NG), (8, NG)),
        np.broadcast_to(2.0 + shift, (8, NG)),
        power(rows - 1),
    ]
    lags = np.arange(round_up(pen_count, 8))[:, None]
    tiles.append(root[None, :] ** (lags * rows) / (1.0 - root[None, :] ** NG))
    return np.concatenate(tiles, axis=0).astype(np.float32)


T_FEND, T_BEND, T_EIGHT, T_F1, T_F2, T_F4, T_B1, T_B2, T_B4, T_FC, T_BC, T_NORM, T_DIAG, T_LAST, T_LAG = range(15)


def fetch(sources, targets, sems):
    copies = [pltpu.make_async_copy(a, b, sems.at[i]) for i, (a, b) in enumerate(zip(sources, targets))]
    for copy in copies:
        copy.start()
    return copies


def list_blocks(capacity, owner, owner_row, tables):
    blocks = owner.shape[0]
    lane = lax.broadcasted_iota(jnp.int32, (8, LANES), 1)
    place = lax.broadcasted_iota(jnp.int32, (8, LANES), 0)
    owners = jnp.broadcast_to(owner_row[...], (8, LANES))
    unroll = 8

    def look(n, carry):
        block_at, used, rank = carry
        for k in range(unroll):
            i = n * unroll + k
            o = owner[i]
            named = lane == o
            block_at = jnp.where(named & (place == used), i, block_at)
            used = used + jnp.where(named, 1, 0)
            rank = rank + jnp.where((owners == o) & (lane > i), 1, 0)
        return block_at, used, rank

    nothing = jnp.zeros((8, LANES), jnp.int32)
    block_at, used, rank = lax.fori_loop(
        0, blocks // unroll, look, (jnp.full((8, LANES), blocks, jnp.int32), nothing, nothing)
    )
    tables[0:8] = block_at
    tables[8:16] = jnp.minimum(rank, capacity - 1)


def pack(s, other, capacity, tables, band, count, cells, offsets, charges, packed, heads_out):
    lane = lax.broadcasted_iota(jnp.int32, (1, LANES), 1)
    head = jnp.zeros((1, LANES), jnp.int32)
    rows = [[], [], [], []]
    for j in range(capacity):
        i = tables[j, other]
        pair = offsets[i]
        rows[0].append(pair[0:1])
        rows[1].append(pair[1:2])
        rows[2].append(jnp.where(lane < count[i], charges[pl.ds(i, 1), :], 0.0))
        rows[3].append(cells[pl.ds(i, 1), :].astype(jnp.float32))
        head = jnp.where(lane == j, band[i], head)
    for part in range(4):
        for j in range(capacity):
            packed[s, part * capacity + j : part * capacity + j + 1, :] = rows[part][j]
    heads_out[s] = head


def peer(index, pens):
    return (lax.div(index, pens), lax.rem(index, pens))


def exclusive(a, b, size):
    total = 0
    for bit in range(size.bit_length() - 1):
        p = lax.rem(lax.div(a, 1 << bit), 2)
        q = lax.rem(lax.div(b, 1 << bit), 2)
        total = total + (p + q - 2 * p * q) * (1 << bit)
    return total


def factors(frac_x, frac_y, weight, cell):
    cell = cell.astype(jnp.int32)
    column = cell & (NG - 1)
    after = (column + 1) & (NG - 1)
    row = cell >> (NG.bit_length() - 1)
    left = (1.0 - frac_x).astype(jnp.bfloat16).astype(jnp.float32)
    right = frac_x.astype(jnp.bfloat16).astype(jnp.float32)
    return frac_y, weight, row, column, after, left, right


def dot3(a_high, a_low, b_high, b_low):
    dot = functools.partial(jnp.dot, preferred_element_type=jnp.float32)
    return dot(a_high, b_high) + (dot(a_high, b_low) + dot(a_low, b_high))


def split(values):
    high = values.astype(jnp.bfloat16)
    return high, (values - high.astype(jnp.float32)).astype(jnp.bfloat16)


def doubled(values):
    return jnp.concatenate([values, values], axis=0).astype(jnp.bfloat16)


def iota16():
    return lax.broadcasted_iota(jnp.int32, (16, LANES), 0).astype(jnp.float32).astype(jnp.bfloat16)


def link_blocks(heads, links, capacity):
    count = heads.shape[0]
    total = count * capacity
    lane = lax.broadcasted_iota(jnp.int32, (8, LANES), 1)
    slot = lax.broadcasted_iota(jnp.int32, (8, LANES), 0) * LANES + lane

    def collect(s, bands):
        for j in range(capacity):
            bands = jnp.where(slot == s * capacity + j, heads[s, 0, j], bands)
        return bands

    bands = lax.fori_loop(0, count, collect, jnp.full((8, LANES), -1, jnp.int32))

    def link(s, carry):
        earlier, last = carry
        for j in range(capacity):
            here = s * capacity + j
            band = heads[s, 0, j]
            earlier = jnp.where((bands == band) & (slot > here), here, earlier)
            last = jnp.where(lane == band, here, last)
        return earlier, last

    nobody = jnp.full((8, LANES), total, jnp.int32)
    earlier, last = lax.fori_loop(0, count, link, (nobody, nobody))
    links[0:8] = earlier
    links[8:16] = last


def deposit(s, capacity, recv, chain, links):
    sub8 = lax.broadcasted_iota(jnp.int32, (8, LANES), 0)
    sub16 = iota16()
    upper_half = jnp.where(sub16 < 8.0, 0.0, 1.0).astype(jnp.bfloat16)
    zero16 = jnp.zeros((16, LANES), jnp.bfloat16)

    def one(j):
        def spread(which):
            return recv[s, pl.ds(which * capacity + j, 8, stride=0), :]

        frac_y, weight, row, column, after, left, right = factors(spread(0), spread(1), spread(2), spread(3))
        lower = weight * (1.0 - frac_y)
        upper = weight * frac_y
        main = doubled(jnp.where(row == sub8, lower, jnp.where(row + 1 == sub8, upper, 0.0)))
        tail = doubled(jnp.where(row == 7, upper, 0.0))
        chunk = doubled((column >> 7).astype(jnp.float32))
        index = doubled((column & 127).astype(jnp.float32))
        left16, right16 = doubled(left), doubled(right)
        lhs = [jnp.where(chunk == upper_half + float(2 * a), main, zero16) for a in range(CHUNKS // 2)]
        lhs.append(jnp.where(chunk == sub16, tail, zero16))
        here = [index == sub16 + float(16 * b) for b in range(LANES // 16)]
        rhs = [jnp.where(h, left16, zero16) for h in here] + [jnp.where(h, right16, zero16) for h in here]
        values = lax.dot_general(
            jnp.concatenate(lhs, axis=0),
            jnp.concatenate(rhs, axis=0),
            (((1,), (1,)), ((), ())),
            preferred_element_type=jnp.float32,
        )
        return values[0 : CHUNKS * 8 + 8]

    made = [one(j) for j in range(capacity)]
    for j in range(capacity):
        slot = s * capacity + j
        earlier = links[lax.div(slot, LANES), lax.rem(slot, LANES)]
        for side in range(2):
            lanes = slice(side * LANES, (side + 1) * LANES)
            chain[slot, side, 0 : CHUNKS * 8 + 8] = made[j][:, lanes] + chain[earlier, side, 0 : CHUNKS * 8 + 8]


def assemble(bands, total, chain, links, hi, lo):
    first_row = lax.broadcasted_iota(jnp.int32, (8, LANES), 0) == 0

    def last_of(band):
        inside = (band >= 0) & (band < bands)
        return jnp.where(inside, links[8, jnp.clip(band, 0, bands - 1)], total)

    def rows_of(band):
        mine, above = last_of(band), last_of(band - 1)
        sides = []
        for side in range(2):
            tiles = []
            for a in range(CHUNKS):
                extra = chain[above, side, pl.ds(CHUNKS * 8 + a, 8, stride=0)]
                tiles.append(chain[mine, side, a * 8 : a * 8 + 8] + jnp.where(first_row, extra, 0.0))
            sides.append(jnp.concatenate(tiles, axis=1))
        return sides[0] + pltpu.roll(sides[1], 1, 1)

    def pair(q, carry):
        high, low = split(jnp.concatenate([rows_of(2 * q), rows_of(2 * q + 1)], axis=0))
        at = pl.ds(pl.multiple_of(q * 16, 16), 16)
        hi[at, :] = high
        lo[at, :] = low
        return carry

    lax.fori_loop(0, bands // 2 + 1, pair, 0)


def transform(rows, hi, lo, table_high, table_low, lines, spectrum, edges):
    width = 256
    for n in range(NG // width):
        cols = slice(n * width, (n + 1) * width)
        values = dot3(hi[...], lo[...], table_high[:, cols], table_low[:, cols])
        spectrum[:, cols] = values[:rows]
        edges[2:3, cols] = values[rows : rows + 1]
    eight = lines[T_EIGHT * 8 : T_EIGHT * 8 + 8]
    tiles = rows // 8

    def fold(t, carry):
        fwd, bwd = carry
        fwd = eight * fwd + spectrum[pl.ds(pl.multiple_of(t * 8, 8), 8), :]
        bwd = eight * bwd + spectrum[pl.ds(pl.multiple_of((tiles - 1 - t) * 8, 8), 8), :]
        return fwd, bwd

    nothing = jnp.zeros((8, NG), jnp.float32)
    fwd, bwd = lax.fori_loop(0, tiles, fold, (nothing, nothing))
    edges[0:1] = jnp.sum(fwd * lines[T_FEND * 8 : T_FEND * 8 + 8], axis=0, keepdims=True)
    edges[1:2] = jnp.sum(bwd * lines[T_BEND * 8 : T_BEND * 8 + 8], axis=0, keepdims=True)
    edges[3:5] = spectrum[0:2]
    edges[5:6] = spectrum[rows - 1 : rows]
    edges[6:8] = jnp.zeros((2, NG), jnp.float32)


def local_scans(rows, spectrum, lines, wave):
    tiles = rows // 8

    def table(which):
        return lines[which * 8 : which * 8 + 8]

    def backward(i, carry):
        t = tiles - 1 - i
        where = pl.ds(pl.multiple_of(t * 8, 8), 8)
        x = spectrum[where, :]
        x = x + table(T_B1) * pltpu.roll(x, 7, 0)
        x = x + table(T_B2) * pltpu.roll(x, 6, 0)
        x = x + table(T_B4) * pltpu.roll(x, 4, 0)
        x = x + table(T_BC) * carry
        wave[where, :] = x
        return x[0:1]

    nothing = jnp.zeros((1, NG), jnp.float32)
    lax.fori_loop(0, tiles, backward, nothing)

    def forward(t, carry):
        where = pl.ds(pl.multiple_of(t * 8, 8), 8)
        d = spectrum[where, :]
        x = d + table(T_F1) * pltpu.roll(d, 1, 0)
        x = x + table(T_F2) * pltpu.roll(x, 2, 0)
        x = x + table(T_F4) * pltpu.roll(x, 4, 0)
        x = x + table(T_FC) * carry
        wave[where, :] = x + wave[where, :] - d
        return x[7:8]

    lax.fori_loop(0, tiles, forward, nothing)


def finish_solve(rows, mine, gathered, lines, wave, hi, lo):
    pens = gathered.shape[0]
    tiles = rows // 8

    def table(which):
        return lines[which * 8 : which * 8 + 8]

    def row_of(pen, which):
        return gathered[lax.rem(pen + 2 * pens, pens), which : which + 1]

    last_power = table(T_LAST)[0:1]
    before = jnp.zeros((1, NG), jnp.float32)
    beyond = jnp.zeros((1, NG), jnp.float32)
    for j in range(pens):
        lag = lines[T_LAG * 8 + j : T_LAG * 8 + j + 1]
        behind, ahead = mine - 1 - j, mine + 1 + j
        before += lag * (row_of(behind, 0) + last_power * row_of(behind - 1, 2))
        beyond += lag * (row_of(ahead, 1) + row_of(ahead - 1, 2))
    incoming = row_of(mine - 1, 2)
    next_zero = row_of(mine + 1, 3) + row_of(mine, 2)
    next_one = row_of(mine + 1, 4)
    last_before = row_of(mine - 1, 5)
    norm = table(T_NORM)[0:1]
    root = table(T_FC)[0:1]
    eight = table(T_EIGHT)
    ramp_down = norm * (root * before + incoming)
    ramp_up = norm * beyond
    first_back = row_of(mine, 1) + incoming + root * last_power * beyond
    final = row_of(mine, 0) + last_power * incoming + root * last_power * before

    def add_beyond(i, ramp):
        t = tiles - 1 - i
        where = pl.ds(pl.multiple_of(t * 8, 8), 8)
        wave[where, :] = table(T_NORM) * wave[where, :] + ramp
        return ramp * eight

    lax.fori_loop(0, tiles, add_beyond, table(T_BC) * ramp_up)

    def add_before(q, ramp):
        parts = []
        for k in range(2):
            where = pl.ds(pl.multiple_of(q * 16 + k * 8, 8), 8)
            value = wave[where, :] + ramp
            wave[where, :] = value
            parts.append(value)
            ramp = ramp * eight
        high, low = split(jnp.concatenate(parts, axis=0))
        at = pl.ds(pl.multiple_of(q * 16, 16), 16)
        hi[at, :] = high
        lo[at, :] = low
        return ramp

    lax.fori_loop(0, tiles // 2, add_before, table(T_BEND) * ramp_down)
    diagonal = table(T_DIAG)[0:1]
    scale = 1.0 / NG
    up1 = norm * (before + root * first_back)
    up2 = diagonal * up1 - wave[0:1] - scale * last_before
    down0 = norm * (root * final + beyond)
    down1 = diagonal * down0 - wave[rows - 1 : rows] - scale * next_zero
    down2 = diagonal * down1 - down0 - scale * next_one
    halo = jnp.concatenate([down0, down1, down2, jnp.zeros((11, NG), jnp.float32), up2, up1], axis=0)
    high, low = split(halo)
    hi[rows : rows + 16] = high
    lo[rows : rows + 16] = low


def invert(rows, hi, lo, table_high, table_low, wave, potential_h, out_sem, rim, field):
    width = 256
    tiles = rows // 8
    for n in range(NG // width):
        cols = slice(n * width, (n + 1) * width)
        wave[:, cols] = dot3(hi[...], lo[...], table_high[:, cols], table_low[:, cols])
    out_copy = pltpu.make_async_copy(wave.at[0:rows], potential_h, out_sem)
    out_copy.start()

    def derive(t, carry):
        def tile(n):
            return wave[pl.ds(pl.multiple_of(n * 8, 8), 8), :]

        middle = tile(t)
        tall = jnp.concatenate([tile(lax.rem(t + tiles + 1, tiles + 2)), middle, tile(jnp.minimum(t + 1, tiles + 1))], axis=0)
        along_x = (8.0 * (pltpu.roll(middle, NG - 1, 1) - pltpu.roll(middle, 1, 1))
                   - (pltpu.roll(middle, NG - 2, 1) - pltpu.roll(middle, 2, 1))) / -12.0
        along_y = (8.0 * (tall[9:17] - tall[7:15]) - (tall[10:18] - tall[6:14])) / -12.0

        @pl.when(t < tiles)
        def _():
            field[t] = jnp.concatenate([along_x, along_y], axis=0).astype(jnp.bfloat16)

        @pl.when(t > 0)
        def _():
            ends = []
            for a in range(CHUNKS):
                lanes = slice(a * LANES, (a + 1) * LANES)
                ends += [along_x[0:1, lanes], along_y[0:1, lanes]]
            near = jnp.concatenate(ends, axis=0)
            far = jnp.concatenate(ends[2:] + ends[:2], axis=0)
            rim[t - 1] = jnp.concatenate([near, far], axis=1).astype(jnp.bfloat16)

        return carry

    lax.fori_loop(0, tiles + 1, derive, 0)
    return out_copy


def mesh_kernel(planes, pens, capacity, rows, owner_h, owner_row_h, band_h, count_h, cells_h, offsets_h, charges_h,
                table_high_h, table_low_h, lines_h, potential_h, out, forces, returned, packed, recv, heads_out, heads,
                heads_s, ids, owner, owner_row, band, block_count, cells, offsets, charges, tables_v, tables, links_v,
                links, chain, field, rim, wave, hi, lo, spectrum, edges, gathered, table_high, table_low, lines, sems,
                send_sems, recv_sems, head_send_sems, head_recv_sems, back_send_sems, back_recv_sems, edge_send_sems,
                edge_recv_sems):
    count = planes * pens
    total = count * capacity
    tall = 4 * capacity
    blocks = owner.shape[0]
    plane = lax.axis_index("pln")
    mine = lax.axis_index("pen")
    me = plane * pens + mine
    barrier = pltpu.get_barrier_semaphore()
    copies = fetch(
        (owner_h, owner_row_h, band_h, count_h, cells_h, offsets_h, charges_h, lines_h, table_high_h, table_low_h),
        (owner, owner_row, band.at[0:blocks], block_count.at[0:blocks], cells.at[0:blocks], offsets.at[0:blocks],
         charges.at[0:blocks], lines, table_high, table_low),
        sems,
    )

    def greet(s, carry):
        other = (
            exclusive(plane, lax.rem(s, planes), planes),
            exclusive(mine, lax.div(s, planes), pens),
        )
        ids[s] = other[0] * pens + other[1]
        pl.semaphore_signal(barrier, inc=1, device_id=other, device_id_type=pl.DeviceIdType.MESH)
        return carry

    ids[0] = me
    lax.fori_loop(1, count, greet, 0)
    copies[0].wait()
    copies[1].wait()
    list_blocks(capacity, owner, owner_row, tables_v)
    tables_copy = pltpu.make_async_copy(tables_v, tables, sems.at[10])
    tables_copy.start()
    cells[blocks : blocks + 8] = jnp.zeros((8, LANES), jnp.int32)
    charges[blocks : blocks + 8] = jnp.zeros((8, LANES), jnp.float32)
    offsets[blocks] = jnp.zeros((2, LANES), jnp.float32)
    for copy in copies[2:7]:
        copy.wait()
    band[blocks] = 0
    block_count[blocks] = 0
    tables_copy.wait()

    def fill(s, carry):
        pack(s, ids[s], capacity, tables, band, block_count, cells, offsets, charges, packed, heads_out)
        return carry

    lax.fori_loop(0, count, fill, 0)
    recv[0, 0:tall] = packed[0]
    heads[0] = heads_out[0]
    chain[total] = jnp.zeros(chain.shape[1:], jnp.float32)
    pl.semaphore_wait(barrier, count - 1)

    def remote(s, source, place, send, receive):
        return pltpu.make_async_remote_copy(
            src_ref=source,
            dst_ref=place,
            send_sem=send.at[s],
            recv_sem=receive.at[s],
            device_id=peer(ids[s], pens),
            device_id_type=pl.DeviceIdType.MESH,
        )

    def head_copy(s):
        return remote(s, heads_out.at[s], heads.at[s], head_send_sems, head_recv_sems)

    def block_copy(s):
        return remote(s, packed.at[s], recv.at[s, 0:tall], send_sems, recv_sems)

    def back_copy(s):
        return remote(s, forces.at[s], returned.at[me], back_send_sems, back_recv_sems)

    def send_heads(s, carry):
        head_copy(s).start()
        return carry

    def send_blocks(s, carry):
        block_copy(s).start()
        return carry

    def take_heads(s, carry):
        head_copy(s).wait_recv()
        return carry

    lax.fori_loop(1, count, send_heads, 0)
    lax.fori_loop(1, count, send_blocks, 0)
    lax.fori_loop(1, count, take_heads, 0)
    heads_copy = pltpu.make_async_copy(heads, heads_s, sems.at[10])
    heads_copy.start()
    heads_copy.wait()
    link_blocks(heads_s, links_v, capacity)
    links_copy = pltpu.make_async_copy(links_v, links, sems.at[10])
    links_copy.start()
    links_copy.wait()

    def receive(s, carry):
        @pl.when(s > 0)
        def _():
            block_copy(s).wait_recv()

        deposit(s, capacity, recv, chain, links)
        return carry

    lax.fori_loop(0, count, receive, 0)
    assemble(rows // 8, total, chain, links, hi, lo)
    for copy in copies[7:]:
        copy.wait()
    transform(rows, hi, lo, table_high, table_low, lines, spectrum, edges)
    gathered[mine] = edges[...]

    def edge_copy(k, place, other):
        return pltpu.make_async_remote_copy(
            src_ref=edges,
            dst_ref=gathered.at[place],
            send_sem=edge_send_sems.at[k],
            recv_sem=edge_recv_sems.at[k],
            device_id=(plane, other),
            device_id_type=pl.DeviceIdType.MESH,
        )

    for k in range(1, pens):
        edge_copy(k, mine, lax.rem(mine + k, pens)).start()
    local_scans(rows, spectrum, lines, wave)
    for k in range(1, pens):
        behind = lax.rem(mine - k + pens, pens)
        edge_copy(k, mine, lax.rem(mine + k, pens)).wait_send()
        edge_copy(k, behind, behind).wait_recv()
    finish_solve(rows, mine, gathered, lines, wave, hi, lo)
    out_copy = invert(rows, hi, lo, table_high, table_low, wave, potential_h, sems.at[11], rim, field)
    sub8 = lax.broadcasted_iota(jnp.int32, (8, LANES), 0)
    odd = (sub8 & 1) == 1
    pair = sub8 >> 1
    sub16 = iota16()
    zero16 = jnp.zeros((16, LANES), jnp.bfloat16)

    def one(d, j):
        def spread(which):
            at = which * capacity + j
            return jnp.broadcast_to(recv[d, at : at + 1, :], (8, LANES))

        band = heads_s[d, 0, j]
        frac_y, weight, row, column, after, left, right = factors(
            spread(0), spread(1), spread(2), spread(3)
        )
        chunk = column >> 7
        index = (column & 127).astype(jnp.float32)
        spot, left16, right16 = doubled(index), doubled(left), doubled(right)
        next_spot = doubled(index + 1.0)
        picks = []
        for b in range(LANES // 16 + 1):
            here = sub16 + float(16 * b)
            picks.append(jnp.where(here == spot, left16, jnp.where(here == next_spot, right16, zero16)))
        picks += [zero16] * (2 * LANES // 16 - len(picks))
        rows_of = field[band]
        windows = [
            jnp.concatenate(
                [
                    rows_of[:, a * LANES : (a + 1) * LANES],
                    rows_of[:, (a + 1) % CHUNKS * LANES : ((a + 1) % CHUNKS + 1) * LANES],
                ],
                axis=1,
            )
            for a in range(CHUNKS)
        ]
        values = jnp.dot(
            jnp.concatenate(windows + [rim[band]], axis=0),
            jnp.concatenate(picks, axis=0),
            preferred_element_type=jnp.float32,
        )
        row_weight = weight * jnp.where(row == sub8, 1.0 - frac_y, jnp.where(row + 1 == sub8, frac_y, 0.0))
        mixed = [values[0:8], values[8:16]]
        for a in range(1, CHUNKS):
            held = chunk == a
            mixed = [jnp.where(held, values[a * 16 + c * 8 : a * 16 + c * 8 + 8], mixed[c]) for c in range(2)]
        edge = weight * jnp.where(row == 7, frac_y, 0.0)
        rims = jnp.where(pair == chunk, values[CHUNKS * 16 : CHUNKS * 16 + 8], 0.0)
        rims = edge * jnp.where(pair + 4 == chunk, values[CHUNKS * 16 + 8 : CHUNKS * 16 + 16], rims)
        return [
            jnp.sum(row_weight * mixed[0] + jnp.where(odd, 0.0, rims), axis=0, keepdims=True),
            jnp.sum(row_weight * mixed[1] + jnp.where(odd, rims, 0.0), axis=0, keepdims=True),
        ]

    def pull(d):
        made = [one(d, j) for j in range(capacity)]
        for c in range(2):
            for j in range(capacity):
                forces[d, c * capacity + j : c * capacity + j + 1, :] = made[j][c]
        if forces.shape[1] > 2 * capacity:
            forces[d, 2 * capacity :, :] = jnp.zeros((forces.shape[1] - 2 * capacity, LANES), jnp.float32)

    def step(i, carry):
        s = count - i
        pull(s)
        back_copy(s).start()
        return carry

    lax.fori_loop(1, count, step, 0)
    pull(0)
    returned[me] = forces[0]

    def finish(i, carry):
        s = count - i
        head_copy(s).wait_send()
        block_copy(s).wait_send()
        back_copy(s).wait_send()
        back_copy(s).wait_recv()
        return carry

    lax.fori_loop(1, count, finish, 0)

    def take(n, carry):
        for k in range(8):
            i = n * 8 + k
            d, j = owner[i], tables[8, i]
            out[i, 0:1, :] = returned[d, pl.ds(j, 1), :]
            out[i, 1:2, :] = returned[d, pl.ds(capacity + j, 1), :]
        return carry

    lax.fori_loop(0, blocks // 8, take, 0)
    out_copy.wait()


def shards(block_owner, block_band, block_count, cells, offsets, charges):
    plane_count = lax.axis_size("pln")
    pen_count = lax.axis_size("pen")
    devices = plane_count * pen_count
    local_blocks, block_len = charges.shape
    capacity = max(2, 2 * local_blocks // devices)
    total = devices * capacity
    rows = NG // pen_count
    tall = 4 * capacity
    tall_back = round_up(2 * capacity, 8)
    vmem = pl.BlockSpec(memory_space=pltpu.VMEM)
    far = pl.BlockSpec(memory_space=pltpu.HBM)
    table_high, table_low = (jnp.asarray(t) for t in hartley_tables())
    lines = jnp.asarray(line_tables(pen_count))
    pairs = pltpu.SemaphoreType.DMA((devices,))
    potential, forces = pl.pallas_call(
        functools.partial(mesh_kernel, plane_count, pen_count, capacity, rows),
        out_shape=(
            jax.ShapeDtypeStruct((rows, NG), jnp.float32),
            jax.ShapeDtypeStruct((local_blocks, 2, block_len), jnp.float32),
        ),
        in_specs=[far] * 10,
        out_specs=(far, vmem),
        scratch_shapes=[
            pltpu.VMEM((devices, tall_back, LANES), jnp.float32),
            pltpu.VMEM((devices, tall_back, LANES), jnp.float32),
            pltpu.VMEM((devices, tall, LANES), jnp.float32),
            pltpu.VMEM((devices, tall + 8, LANES), jnp.float32),
            pltpu.VMEM((devices, 1, LANES), jnp.int32),
            pltpu.VMEM((devices, 1, LANES), jnp.int32),
            pltpu.SMEM((devices, 1, LANES), jnp.int32),
            pltpu.SMEM((devices,), jnp.int32),
            pltpu.SMEM((local_blocks,), jnp.int32),
            pltpu.VMEM((1, local_blocks), jnp.int32),
            pltpu.SMEM((local_blocks + 8,), jnp.int32),
            pltpu.SMEM((local_blocks + 8,), jnp.int32),
            pltpu.VMEM((local_blocks + 8, block_len), jnp.int32),
            pltpu.VMEM((local_blocks + 8, 2, block_len), jnp.float32),
            pltpu.VMEM((local_blocks + 8, block_len), jnp.float32),
            pltpu.VMEM((16, LANES), jnp.int32),
            pltpu.SMEM((16, LANES), jnp.int32),
            pltpu.VMEM((16, LANES), jnp.int32),
            pltpu.SMEM((16, LANES), jnp.int32),
            pltpu.VMEM((total + 1, 2, CHUNKS * 8 + 16, LANES), jnp.float32),
            pltpu.VMEM((rows // 8, 16, NG), jnp.bfloat16),
            pltpu.VMEM((rows // 8, 16, 2 * LANES), jnp.bfloat16),
            pltpu.VMEM((rows + 16, NG), jnp.float32),
            pltpu.VMEM((rows + 16, NG), jnp.bfloat16),
            pltpu.VMEM((rows + 16, NG), jnp.bfloat16),
            pltpu.VMEM((rows, NG), jnp.float32),
            pltpu.VMEM((8, NG), jnp.float32),
            pltpu.VMEM((pen_count, 8, NG), jnp.float32),
            pltpu.VMEM((NG, NG), jnp.bfloat16),
            pltpu.VMEM((NG, NG), jnp.bfloat16),
            pltpu.VMEM(lines.shape, jnp.float32),
            pltpu.SemaphoreType.DMA((12,)),
            pairs,
            pairs,
            pairs,
            pairs,
            pairs,
            pairs,
            pltpu.SemaphoreType.DMA((pen_count,)),
            pltpu.SemaphoreType.DMA((pen_count,)),
        ],
        compiler_params=pltpu.CompilerParams(
            collective_id=0, has_side_effects=True, vmem_limit_bytes=VMEM_LIMIT
        ),
        name="mesh",
    )(
        block_owner[:, 0],
        block_owner.reshape(1, local_blocks),
        block_band,
        block_count,
        cells,
        offsets,
        charges,
        table_high,
        table_low,
        lines,
    )
    return (potential[None], forces)


def solution(mesh):
    placed = (
        P(("pln", "pen"), None),
        P(("pln", "pen")),
        P(("pln", "pen")),
        P(("pln", "pen"), None),
        P(("pln", "pen"), None, None),
        P(("pln", "pen"), None),
    )
    return jax.shard_map(
        shards,
        mesh=mesh,
        in_specs=placed,
        out_specs=(P("pln", "pen", None), P(("pln", "pen"), None, None)),
        check_vma=False,
    )
```

```python
import functools
import math

import jax
import jax.numpy as jnp
import numpy as np
from jax import lax
from jax.experimental import pallas as pl
from jax.experimental.pallas import tpu as pltpu
from jax.sharding import PartitionSpec as P

NG = 1024
LANES = 128
CHUNKS = NG // LANES
screening = 2e-05
VMEM_LIMIT = 62 * 1024 * 1024
UNROLL = 8


def round_up(value, step):
    return -(-value // step) * step


@functools.lru_cache(None)
def hartley_tables():
    index = np.arange(NG)
    angle = 2.0 * np.pi / NG * (index[:, None] * index[None, :] % NG)
    table = np.cos(angle) + np.sin(angle)
    high = table.astype(jnp.bfloat16)
    low = (table - high.astype(np.float64)).astype(jnp.bfloat16)
    turn = 2.0 * np.pi / NG * np.arange(NG)
    slope = (2.0 * np.sin(2.0 * turn) - 16.0 * np.sin(turn)) / 12.0
    along = (slope[:, None] * (np.cos(angle) - np.sin(angle))).astype(jnp.bfloat16)
    return high, low, along


@functools.lru_cache(None)
def line_tables(pen_count):
    rows = NG // pen_count
    shift = 4.0 * np.sin(np.pi * np.arange(NG) / NG) ** 2 + screening
    root = 1.0 + shift / 2.0 - np.sqrt(shift + shift * shift / 4.0)
    i = np.arange(8)[:, None]

    def power(exponent):
        return root[None, :] ** (exponent + np.zeros((8, 1)))

    tiles = [
        power(7 - i),
        power(i),
        power(8),
        np.where(i >= 1, power(1), 0.0),
        np.where(i >= 2, power(2), 0.0),
        np.where(i >= 4, power(4), 0.0),
        np.where(i <= 6, power(1), 0.0),
        np.where(i <= 5, power(2), 0.0),
        np.where(i <= 3, power(4), 0.0),
        power(i + 1),
        power(8 - i),
        np.broadcast_to(1.0 / ((1.0 / root - root) * NG), (8, NG)),
        np.broadcast_to(2.0 + shift, (8, NG)),
        power(rows - 1),
    ]
    lags = np.arange(round_up(pen_count, 8))[:, None]
    tiles.append(root[None, :] ** (lags * rows) / (1.0 - root[None, :] ** NG))
    return np.concatenate(tiles, axis=0).astype(np.float32)


T_FEND, T_BEND, T_EIGHT, T_F1, T_F2, T_F4, T_B1, T_B2, T_B4, T_FC, T_BC, T_NORM, T_DIAG, T_LAST, T_LAG = range(15)


def fetch(sources, targets, sems):
    copies = [pltpu.make_async_copy(a, b, sems.at[i]) for i, (a, b) in enumerate(zip(sources, targets))]
    for copy in copies:
        copy.start()
    return copies


def list_blocks(capacity, owner, owner_row, tables):
    blocks = owner.shape[0]
    lane = lax.broadcasted_iota(jnp.int32, (8, LANES), 1)
    place = lax.broadcasted_iota(jnp.int32, (8, LANES), 0)
    owners = jnp.broadcast_to(owner_row[...], (8, LANES))
    unroll = 8

    def look(n, carry):
        block_at, used, rank = carry
        for k in range(unroll):
            i = n * unroll + k
            o = owner[i]
            named = lane == o
            block_at = jnp.where(named & (place == used), i, block_at)
            used = used + jnp.where(named, 1, 0)
            rank = rank + jnp.where((owners == o) & (lane > i), 1, 0)
        return block_at, used, rank

    nothing = jnp.zeros((8, LANES), jnp.int32)
    block_at, used, rank = lax.fori_loop(
        0, blocks // unroll, look, (jnp.full((8, LANES), blocks, jnp.int32), nothing, nothing)
    )
    tables[0:8] = block_at
    tables[8:16] = jnp.minimum(rank, capacity - 1)


def pack(s, other, capacity, tables, band, count, cells, offsets, charges, packed, heads_out):
    lane = lax.broadcasted_iota(jnp.int32, (1, LANES), 1)
    head = jnp.zeros((1, LANES), jnp.int32)
    rows = [[], [], [], []]
    for j in range(capacity):
        i = tables[j, other]
        pair = offsets[i]
        rows[0].append(pair[0:1])
        rows[1].append(pair[1:2])
        rows[2].append(jnp.where(lane < count[i], charges[pl.ds(i, 1), :], 0.0))
        rows[3].append(cells[pl.ds(i, 1), :].astype(jnp.float32))
        head = jnp.where(lane == j, band[i], head)
    for part in range(4):
        for j in range(capacity):
            packed[s, part * capacity + j : part * capacity + j + 1, :] = rows[part][j]
    heads_out[s] = head


def peer(index, pens):
    return (lax.div(index, pens), lax.rem(index, pens))


def exclusive(a, b, size):
    total = 0
    for bit in range(size.bit_length() - 1):
        p = lax.rem(lax.div(a, 1 << bit), 2)
        q = lax.rem(lax.div(b, 1 << bit), 2)
        total = total + (p + q - 2 * p * q) * (1 << bit)
    return total


def factors(frac_x, frac_y, weight, cell):
    cell = cell.astype(jnp.int32)
    column = cell & (NG - 1)
    after = (column + 1) & (NG - 1)
    row = cell >> (NG.bit_length() - 1)
    left = (1.0 - frac_x).astype(jnp.bfloat16).astype(jnp.float32)
    right = frac_x.astype(jnp.bfloat16).astype(jnp.float32)
    return frac_y, weight, row, column, after, left, right


def dot3(a_high, a_low, b_high, b_low):
    dot = functools.partial(jnp.dot, preferred_element_type=jnp.float32)
    return dot(a_high, b_high) + (dot(a_high, b_low) + dot(a_low, b_high))


def split(values):
    high = values.astype(jnp.bfloat16)
    return high, (values - high.astype(jnp.float32)).astype(jnp.bfloat16)


def doubled(values):
    return jnp.concatenate([values, values], axis=0).astype(jnp.bfloat16)


def iota16():
    return lax.broadcasted_iota(jnp.int32, (16, LANES), 0).astype(jnp.float32).astype(jnp.bfloat16)


def link_blocks(heads, links, capacity):
    count = heads.shape[0]
    total = count * capacity
    lane = lax.broadcasted_iota(jnp.int32, (8, LANES), 1)
    slot = lax.broadcasted_iota(jnp.int32, (8, LANES), 0) * LANES + lane

    def collect(s, bands):
        for j in range(capacity):
            bands = jnp.where(slot == s * capacity + j, heads[s, 0, j], bands)
        return bands

    bands = lax.fori_loop(0, count, collect, jnp.full((8, LANES), -1, jnp.int32))

    def link(s, carry):
        earlier, last = carry
        for j in range(capacity):
            here = s * capacity + j
            band = heads[s, 0, j]
            earlier = jnp.where((bands == band) & (slot > here), here, earlier)
            last = jnp.where(lane == band, here, last)
        return earlier, last

    nobody = jnp.full((8, LANES), total, jnp.int32)
    earlier, last = lax.fori_loop(0, count, link, (nobody, nobody))
    links[0:8] = earlier
    links[8:16] = last


def deposit(s, capacity, recv, chain, links):
    sub8 = lax.broadcasted_iota(jnp.int32, (8, LANES), 0)
    sub16 = iota16()
    upper_half = jnp.where(sub16 < 8.0, 0.0, 1.0).astype(jnp.bfloat16)
    zero16 = jnp.zeros((16, LANES), jnp.bfloat16)

    def one(j):
        def spread(which):
            return recv[s, pl.ds(which * capacity + j, 8, stride=0), :]

        frac_y, weight, row, column, after, left, right = factors(spread(0), spread(1), spread(2), spread(3))
        lower = weight * (1.0 - frac_y)
        upper = weight * frac_y
        main = doubled(jnp.where(row == sub8, lower, jnp.where(row + 1 == sub8, upper, 0.0)))
        tail = doubled(jnp.where(row == 7, upper, 0.0))
        chunk = doubled((column >> 7).astype(jnp.float32))
        index = doubled((column & 127).astype(jnp.float32))
        left16, right16 = doubled(left), doubled(right)
        lhs = [jnp.where(chunk == upper_half + float(2 * a), main, zero16) for a in range(CHUNKS // 2)]
        lhs.append(jnp.where(chunk == sub16, tail, zero16))
        here = [index == sub16 + float(16 * b) for b in range(LANES // 16)]
        rhs = [jnp.where(h, left16, zero16) for h in here] + [jnp.where(h, right16, zero16) for h in here]
        values = lax.dot_general(
            jnp.concatenate(lhs, axis=0),
            jnp.concatenate(rhs, axis=0),
            (((1,), (1,)), ((), ())),
            preferred_element_type=jnp.float32,
        )
        return values[0 : CHUNKS * 8 + 8]

    made = [one(j) for j in range(capacity)]
    for j in range(capacity):
        slot = s * capacity + j
        earlier = links[lax.div(slot, LANES), lax.rem(slot, LANES)]
        for side in range(2):
            lanes = slice(side * LANES, (side + 1) * LANES)
            chain[slot, side, 0 : CHUNKS * 8 + 8] = made[j][:, lanes] + chain[earlier, side, 0 : CHUNKS * 8 + 8]


def assemble(bands, total, chain, links, hi, lo):
    first_row = lax.broadcasted_iota(jnp.int32, (8, LANES), 0) == 0

    def last_of(band):
        inside = (band >= 0) & (band < bands)
        return jnp.where(inside, links[8, jnp.clip(band, 0, bands - 1)], total)

    def rows_of(band):
        mine, above = last_of(band), last_of(band - 1)
        sides = []
        for side in range(2):
            tiles = []
            for a in range(CHUNKS):
                extra = chain[above, side, pl.ds(CHUNKS * 8 + a, 8, stride=0)]
                tiles.append(chain[mine, side, a * 8 : a * 8 + 8] + jnp.where(first_row, extra, 0.0))
            sides.append(jnp.concatenate(tiles, axis=1))
        return sides[0] + pltpu.roll(sides[1], 1, 1)

    def pair(q, carry):
        high, low = split(jnp.concatenate([rows_of(2 * q), rows_of(2 * q + 1)], axis=0))
        at = pl.ds(pl.multiple_of(q * 16, 16), 16)
        hi[at, :] = high
        lo[at, :] = low
        return carry

    lax.fori_loop(0, bands // 2 + 1, pair, 0)


def transform(rows, hi, lo, table_high, table_low, lines, spectrum, sums, nexts, lasts):
    width = 256
    for n in range(NG // width):
        cols = slice(n * width, (n + 1) * width)
        values = dot3(hi[...], lo[...], table_high[:, cols], table_low[:, cols])
        spectrum[:, cols] = values[:rows]
        sums[2, 0:1, cols] = values[rows : rows + 1]
    eight = lines[T_EIGHT * 8 : T_EIGHT * 8 + 8]
    tiles = rows // 8

    def fold(t, carry):
        fwd, bwd = carry
        fwd = eight * fwd + spectrum[pl.ds(pl.multiple_of(t * 8, 8), 8), :]
        bwd = eight * bwd + spectrum[pl.ds(pl.multiple_of((tiles - 1 - t) * 8, 8), 8), :]
        return fwd, bwd

    nothing = jnp.zeros((8, NG), jnp.float32)
    fwd, bwd = lax.fori_loop(0, tiles, fold, (nothing, nothing))
    sums[0] = jnp.sum(fwd * lines[T_FEND * 8 : T_FEND * 8 + 8], axis=0, keepdims=True)
    sums[1] = jnp.sum(bwd * lines[T_BEND * 8 : T_BEND * 8 + 8], axis=0, keepdims=True)
    nexts[0] = spectrum[0:1]
    nexts[1] = spectrum[1:2]
    lasts[0] = spectrum[rows - 1 : rows]


def wave_tile(wave, row, height=8):
    return jnp.concatenate([wave[a, pl.ds(row, height), :] for a in range(CHUNKS)], axis=1)


def put_wave(wave, row, values):
    for a in range(CHUNKS):
        wave[a, pl.ds(row, values.shape[0]), :] = values[:, a * LANES : (a + 1) * LANES]


def local_scans(rows, spectrum, lines, wave):
    tiles = rows // 8

    def table(which):
        return lines[which * 8 : which * 8 + 8]

    def backward(i, carry):
        t = tiles - 1 - i
        where = pl.ds(pl.multiple_of(t * 8, 8), 8)
        x = spectrum[where, :]
        x = x + table(T_B1) * pltpu.roll(x, 7, 0)
        x = x + table(T_B2) * pltpu.roll(x, 6, 0)
        x = x + table(T_B4) * pltpu.roll(x, 4, 0)
        x = x + table(T_BC) * carry
        put_wave(wave, pl.multiple_of(t * 8 + 8, 8), x)
        return x[0:1]

    nothing = jnp.zeros((1, NG), jnp.float32)
    lax.fori_loop(0, tiles, backward, nothing)

    def forward(t, carry):
        where = pl.ds(pl.multiple_of(t * 8, 8), 8)
        d = spectrum[where, :]
        x = d + table(T_F1) * pltpu.roll(d, 1, 0)
        x = x + table(T_F2) * pltpu.roll(x, 2, 0)
        x = x + table(T_F4) * pltpu.roll(x, 4, 0)
        x = x + table(T_FC) * carry
        row = pl.multiple_of(t * 8 + 8, 8)
        put_wave(wave, row, x + wave_tile(wave, row) - d)
        return x[7:8]

    lax.fori_loop(0, tiles, forward, nothing)


def finish_solve(rows, mine, sums_of, nexts_of, lasts_of, lines, wave, stack):
    pens = sums_of.shape[0]
    tiles = rows // 8

    def table(which):
        return lines[which * 8 : which * 8 + 8]

    def row_of(pen, which):
        return sums_of[lax.rem(pen + 2 * pens, pens), which]

    last_power = table(T_LAST)[0:1]
    before = jnp.zeros((1, NG), jnp.float32)
    beyond = jnp.zeros((1, NG), jnp.float32)
    for j in range(pens):
        lag = lines[T_LAG * 8 + j : T_LAG * 8 + j + 1]
        behind, ahead = mine - 1 - j, mine + 1 + j
        before += lag * (row_of(behind, 0) + last_power * row_of(behind - 1, 2))
        beyond += lag * (row_of(ahead, 1) + row_of(ahead - 1, 2))
    incoming = row_of(mine - 1, 2)
    next_zero = nexts_of[0] + row_of(mine, 2)
    next_one = nexts_of[1]
    last_before = lasts_of[0]
    norm = table(T_NORM)[0:1]
    root = table(T_FC)[0:1]
    eight = table(T_EIGHT)
    ramp_down = norm * (root * before + incoming)
    ramp_up = norm * beyond
    first_back = row_of(mine, 1) + incoming + root * last_power * beyond
    final = row_of(mine, 0) + last_power * incoming + root * last_power * before

    def add_beyond(i, ramp):
        row = pl.multiple_of((tiles - 1 - i) * 8 + 8, 8)
        put_wave(wave, row, table(T_NORM) * wave_tile(wave, row) + ramp)
        return ramp * eight

    lax.fori_loop(0, tiles, add_beyond, table(T_BC) * ramp_up)

    def add_before(q, ramp):
        row = pl.multiple_of(q * 16 + 8, 8)
        then = ramp * eight
        values = wave_tile(wave, row, 16) + jnp.concatenate([ramp, then], axis=0)
        put_wave(wave, row, values)
        stack[pl.ds(pl.multiple_of(q * 16, 16), 16), :] = values.astype(jnp.bfloat16)
        return then * eight

    lax.fori_loop(0, tiles // 2, add_before, table(T_BEND) * ramp_down)
    diagonal = table(T_DIAG)[0:1]
    scale = 1.0 / NG
    up1 = norm * (before + root * first_back)
    up2 = diagonal * up1 - wave_tile(wave, 8, 1) - scale * last_before
    down0 = norm * (root * final + beyond)
    down1 = diagonal * down0 - wave_tile(wave, rows + 7, 1) - scale * next_zero
    down2 = diagonal * down1 - down0 - scale * next_one
    put_wave(wave, 0, jnp.concatenate([jnp.zeros((6, NG), jnp.float32), up2, up1], axis=0))
    below = jnp.concatenate([down0, down1, down2, jnp.zeros((21, NG), jnp.float32)], axis=0)
    put_wave(wave, rows + 8, below)
    stack[rows : rows + 16] = below[0:16].astype(jnp.bfloat16)

    def slope(q, carry):
        row = q * 16 + 8

        def at(shift):
            return wave_tile(wave, row + shift, 16)

        along_y = (8.0 * (at(1) - at(-1)) - (at(2) - at(-2))) * (-1.0 / 12.0)
        stack[pl.ds(pl.multiple_of(rows + 16 + q * 16, 16), 16), :] = along_y.astype(jnp.bfloat16)
        return carry

    lax.fori_loop(0, tiles // 2 + 1, slope, 0)


def invert(rows, stack, table_high, table_along, potential, potential_h, out_sem, forms, rim, field):
    width = 256
    tiles = rows // 8
    tall = rows + 16
    dot = functools.partial(jnp.dot, preferred_element_type=jnp.float32)
    for n in range(NG // width):
        cols = slice(n * width, (n + 1) * width)
        values = dot(stack[...], table_high[:, cols])
        potential[:, cols] = values[:rows]
        along = dot(stack[0:tall], table_along[:, cols])
        for k in range(width // LANES):
            a = n * (width // LANES) + k
            lanes = slice(k * LANES, (k + 1) * LANES)
            forms[a * tall : (a + 1) * tall] = along[:, lanes]
            forms[(CHUNKS + a) * tall : (CHUNKS + a + 1) * tall] = values[tall:, lanes]
    out_copy = pltpu.make_async_copy(potential, potential_h, out_sem)
    out_copy.start()

    def gather_tile(t, carry):
        row = pl.multiple_of(t * 8, 8)
        for a in range(CHUNKS):
            both = [forms[pl.ds(pl.multiple_of((c * CHUNKS + a) * tall + row, 8), 8), :] for c in range(2)]
            field[t, :, a * LANES : (a + 1) * LANES] = jnp.concatenate(both, axis=0).astype(jnp.bfloat16)
        ends = [forms[pl.ds(c * CHUNKS * tall + row + 8, CHUNKS, stride=tall), :] for c in range(2)]
        rim[t, :, 0:LANES] = jnp.concatenate(ends, axis=0).astype(jnp.bfloat16)
        ends = [pltpu.roll(e, CHUNKS - 1, 0) for e in ends]
        rim[t, :, LANES : 2 * LANES] = jnp.concatenate(ends, axis=0).astype(jnp.bfloat16)
        return carry

    lax.fori_loop(0, tiles, gather_tile, 0)
    return out_copy


def mesh_kernel(planes, pens, capacity, rows, owner_h, owner_row_h, band_h, count_h, cells_h, offsets_h, charges_h,
                table_high_h, table_low_h, table_along_h, lines_h, potential_h, out, forces, returned, packed, recv, heads_out, heads,
                heads_s, ids, owner, owner_row, band, block_count, cells, offsets, charges, tables_v, tables, links_v,
                links, chain, field, rim, wave, hi, lo, stack, forms, potential, spectrum, sums, nexts, lasts, sums_of,
                nexts_of, lasts_of, table_high, table_low, table_along, lines, sems,
                send_sems, recv_sems, head_send_sems, head_recv_sems, back_send_sems, back_recv_sems, edge_send_sems,
                edge_recv_sems, side_send_sems, side_recv_sems):
    count = planes * pens
    total = count * capacity
    tall = 4 * capacity
    blocks = owner.shape[0]
    plane = lax.axis_index("pln")
    mine = lax.axis_index("pen")
    me = plane * pens + mine
    barrier = pltpu.get_barrier_semaphore()
    copies = fetch(
        (owner_h, owner_row_h, band_h, count_h, cells_h, offsets_h, charges_h, lines_h, table_high_h, table_low_h,
         table_along_h),
        (owner, owner_row, band.at[0:blocks], block_count.at[0:blocks], cells.at[0:blocks], offsets.at[0:blocks],
         charges.at[0:blocks], lines, table_high, table_low, table_along),
        sems,
    )

    def greet(s, carry):
        other = (
            exclusive(plane, lax.rem(s, planes), planes),
            exclusive(mine, lax.div(s, planes), pens),
        )
        ids[s] = other[0] * pens + other[1]
        pl.semaphore_signal(barrier, inc=1, device_id=other, device_id_type=pl.DeviceIdType.MESH)
        return carry

    ids[0] = me
    lax.fori_loop(1, count, greet, 0)
    copies[0].wait()
    copies[1].wait()
    list_blocks(capacity, owner, owner_row, tables_v)
    tables_copy = pltpu.make_async_copy(tables_v, tables, sems.at[11])
    tables_copy.start()
    cells[blocks : blocks + 8] = jnp.zeros((8, LANES), jnp.int32)
    charges[blocks : blocks + 8] = jnp.zeros((8, LANES), jnp.float32)
    offsets[blocks] = jnp.zeros((2, LANES), jnp.float32)
    for copy in copies[2:7]:
        copy.wait()
    band[blocks] = 0
    block_count[blocks] = 0
    tables_copy.wait()

    def fill(s, carry):
        pack(s, ids[s], capacity, tables, band, block_count, cells, offsets, charges, packed, heads_out)
        return carry

    lax.fori_loop(0, count, fill, 0)
    recv[0, 0:tall] = packed[0]
    heads[0] = heads_out[0]
    chain[total] = jnp.zeros(chain.shape[1:], jnp.float32)
    pl.semaphore_wait(barrier, count - 1)

    def remote(s, source, place, send, receive):
        return pltpu.make_async_remote_copy(
            src_ref=source,
            dst_ref=place,
            send_sem=send.at[s],
            recv_sem=receive.at[s],
            device_id=peer(ids[s], pens),
            device_id_type=pl.DeviceIdType.MESH,
        )

    def head_copy(s):
        return remote(s, heads_out.at[s], heads.at[s], head_send_sems, head_recv_sems)

    def block_copy(s):
        return remote(s, packed.at[s], recv.at[s, 0:tall], send_sems, recv_sems)

    def back_copy(s):
        return remote(s, forces.at[s], returned.at[me], back_send_sems, back_recv_sems)

    def send_heads(s, carry):
        head_copy(s).start()
        return carry

    def send_blocks(s, carry):
        block_copy(s).start()
        return carry

    def take_heads(s, carry):
        head_copy(s).wait_recv()
        return carry

    lax.fori_loop(1, count, send_heads, 0)
    lax.fori_loop(1, count, send_blocks, 0)
    lax.fori_loop(1, count, take_heads, 0)
    heads_copy = pltpu.make_async_copy(heads, heads_s, sems.at[11])
    heads_copy.start()
    heads_copy.wait()
    link_blocks(heads_s, links_v, capacity)
    links_copy = pltpu.make_async_copy(links_v, links, sems.at[11])
    links_copy.start()
    links_copy.wait()

    def receive(s, carry):
        @pl.when(s > 0)
        def _():
            block_copy(s).wait_recv()

        deposit(s, capacity, recv, chain, links)
        return carry

    lax.fori_loop(0, count, receive, 0)
    assemble(rows // 8, total, chain, links, hi, lo)
    for copy in copies[7:]:
        copy.wait()
    transform(rows, hi, lo, table_high, table_low, lines, spectrum, sums, nexts, lasts)
    sums_of[mine] = sums[...]

    def edge_copy(k, place, other):
        return pltpu.make_async_remote_copy(
            src_ref=sums,
            dst_ref=sums_of.at[place],
            send_sem=edge_send_sems.at[k],
            recv_sem=edge_recv_sems.at[k],
            device_id=(plane, other),
            device_id_type=pl.DeviceIdType.MESH,
        )

    def side_copy(n, source, place, other):
        return pltpu.make_async_remote_copy(
            src_ref=source,
            dst_ref=place,
            send_sem=side_send_sems.at[n],
            recv_sem=side_recv_sems.at[n],
            device_id=(plane, other),
            device_id_type=pl.DeviceIdType.MESH,
        )

    up_copy = side_copy(0, nexts, nexts_of, lax.rem(mine + pens - 1, pens))
    down_copy = side_copy(1, lasts, lasts_of, lax.rem(mine + 1, pens))
    for k in range(1, pens):
        edge_copy(k, mine, lax.rem(mine + k, pens)).start()
    up_copy.start()
    down_copy.start()
    local_scans(rows, spectrum, lines, wave)
    for k in range(1, pens):
        behind = lax.rem(mine - k + pens, pens)
        edge_copy(k, mine, lax.rem(mine + k, pens)).wait_send()
        edge_copy(k, behind, behind).wait_recv()
    up_copy.wait()
    down_copy.wait()
    finish_solve(rows, mine, sums_of, nexts_of, lasts_of, lines, wave, stack)
    out_copy = invert(rows, stack, table_high, table_along, potential, potential_h, sems.at[12], forms, rim, field)
    sub8 = lax.broadcasted_iota(jnp.int32, (8, LANES), 0)
    sub16 = iota16()
    zero16 = jnp.zeros((16, LANES), jnp.bfloat16)

    def one(d, j):
        def spread(which):
            return recv[d, pl.ds(which * capacity + j, 8, stride=0), :]

        band = heads_s[d, 0, j]
        frac_y, weight, row, column, after, left, right = factors(
            spread(0), spread(1), spread(2), spread(3)
        )
        chunk = column >> 7
        index = (column & 127).astype(jnp.float32)
        spot, left16, right16 = doubled(index), doubled(left), doubled(right)
        next_spot = doubled(index + 1.0)
        picks = []
        for b in range(LANES // 16 + 1):
            here = sub16 + float(16 * b)
            picks.append(jnp.where(here == spot, left16, jnp.where(here == next_spot, right16, zero16)))
        picks += [zero16] * (2 * LANES // 16 - len(picks))
        rows_of = field[band]
        windows = [
            jnp.concatenate(
                [
                    rows_of[:, a * LANES : (a + 1) * LANES],
                    rows_of[:, (a + 1) % CHUNKS * LANES : ((a + 1) % CHUNKS + 1) * LANES],
                ],
                axis=1,
            )
            for a in range(CHUNKS)
        ]
        values = jnp.dot(
            jnp.concatenate(windows + [rim[band]], axis=0),
            jnp.concatenate(picks, axis=0),
            preferred_element_type=jnp.float32,
        )
        row_weight = weight * jnp.where(row == sub8, 1.0 - frac_y, jnp.where(row + 1 == sub8, frac_y, 0.0))
        mixed = [values[0:8], values[8:16]]
        for a in range(1, CHUNKS):
            held = chunk == a
            mixed = [jnp.where(held, values[a * 16 + c * 8 : a * 16 + c * 8 + 8], mixed[c]) for c in range(2)]
        edge = weight * jnp.where(row == 7, frac_y, 0.0)
        at_edge = sub8 == chunk
        rims = [jnp.where(at_edge, values[CHUNKS * 16 + c * 8 : CHUNKS * 16 + c * 8 + 8], 0.0) for c in range(2)]
        return [jnp.sum(row_weight * mixed[c] + edge * rims[c], axis=0, keepdims=True) for c in range(2)]

    def pull(d):
        made = [one(d, j) for j in range(capacity)]
        for c in range(2):
            for j in range(capacity):
                forces[d, c * capacity + j : c * capacity + j + 1, :] = made[j][c]
        if forces.shape[1] > 2 * capacity:
            forces[d, 2 * capacity :, :] = jnp.zeros((forces.shape[1] - 2 * capacity, LANES), jnp.float32)

    def step(i, carry):
        s = count - i
        pull(s)
        back_copy(s).start()
        return carry

    lax.fori_loop(1, count, step, 0)
    pull(0)
    returned[me] = forces[0]

    def finish(i, carry):
        s = count - i
        head_copy(s).wait_send()
        block_copy(s).wait_send()
        back_copy(s).wait_send()
        back_copy(s).wait_recv()
        return carry

    lax.fori_loop(1, count, finish, 0)

    def take(n, carry):
        for k in range(8):
            i = n * 8 + k
            d, j = owner[i], tables[8, i]
            out[i, 0:1, :] = returned[d, pl.ds(j, 1), :]
            out[i, 1:2, :] = returned[d, pl.ds(capacity + j, 1), :]
        return carry

    lax.fori_loop(0, blocks // 8, take, 0)
    out_copy.wait()


def shards(block_owner, block_band, block_count, cells, offsets, charges):
    plane_count = lax.axis_size("pln")
    pen_count = lax.axis_size("pen")
    devices = plane_count * pen_count
    local_blocks, block_len = charges.shape
    capacity = max(2, 2 * local_blocks // devices)
    total = devices * capacity
    rows = NG // pen_count
    tall = 4 * capacity
    tall_back = round_up(2 * capacity, 8)
    vmem = pl.BlockSpec(memory_space=pltpu.VMEM)
    far = pl.BlockSpec(memory_space=pltpu.HBM)
    table_high, table_low, table_along = (jnp.asarray(t) for t in hartley_tables())
    lines = jnp.asarray(line_tables(pen_count))
    pairs = pltpu.SemaphoreType.DMA((devices,))
    potential, forces = pl.pallas_call(
        functools.partial(mesh_kernel, plane_count, pen_count, capacity, rows),
        out_shape=(
            jax.ShapeDtypeStruct((rows, NG), jnp.float32),
            jax.ShapeDtypeStruct((local_blocks, 2, block_len), jnp.float32),
        ),
        in_specs=[far] * 11,
        out_specs=(far, vmem),
        scratch_shapes=[
            pltpu.VMEM((devices, tall_back, LANES), jnp.float32),
            pltpu.VMEM((devices, tall_back, LANES), jnp.float32),
            pltpu.VMEM((devices, tall, LANES), jnp.float32),
            pltpu.VMEM((devices, tall + 8, LANES), jnp.float32),
            pltpu.VMEM((devices, 1, LANES), jnp.int32),
            pltpu.VMEM((devices, 1, LANES), jnp.int32),
            pltpu.SMEM((devices, 1, LANES), jnp.int32),
            pltpu.SMEM((devices,), jnp.int32),
            pltpu.SMEM((local_blocks,), jnp.int32),
            pltpu.VMEM((1, local_blocks), jnp.int32),
            pltpu.SMEM((local_blocks + 8,), jnp.int32),
            pltpu.SMEM((local_blocks + 8,), jnp.int32),
            pltpu.VMEM((local_blocks + 8, block_len), jnp.int32),
            pltpu.VMEM((local_blocks + 8, 2, block_len), jnp.float32),
            pltpu.VMEM((local_blocks + 8, block_len), jnp.float32),
            pltpu.VMEM((16, LANES), jnp.int32),
            pltpu.SMEM((16, LANES), jnp.int32),
            pltpu.VMEM((16, LANES), jnp.int32),
            pltpu.SMEM((16, LANES), jnp.int32),
            pltpu.VMEM((total + 1, 2, CHUNKS * 8 + 16, LANES), jnp.float32),
            pltpu.VMEM((rows // 8, 16, NG), jnp.bfloat16),
            pltpu.VMEM((rows // 8, 16, 2 * LANES), jnp.bfloat16),
            pltpu.VMEM((CHUNKS, rows + 32, LANES), jnp.float32),
            pltpu.VMEM((rows + 16, NG), jnp.bfloat16),
            pltpu.VMEM((rows + 16, NG), jnp.bfloat16),
            pltpu.VMEM((2 * rows + 32, NG), jnp.bfloat16),
            pltpu.VMEM((2 * CHUNKS * (rows + 16), LANES), jnp.float32),
            pltpu.VMEM((rows, NG), jnp.float32),
            pltpu.VMEM((rows, NG), jnp.float32),
            pltpu.VMEM((3, 1, NG), jnp.float32),
            pltpu.VMEM((2, 1, NG), jnp.float32),
            pltpu.VMEM((1, 1, NG), jnp.float32),
            pltpu.VMEM((pen_count, 3, 1, NG), jnp.float32),
            pltpu.VMEM((2, 1, NG), jnp.float32),
            pltpu.VMEM((1, 1, NG), jnp.float32),
            pltpu.VMEM((NG, NG), jnp.bfloat16),
            pltpu.VMEM((NG, NG), jnp.bfloat16),
            pltpu.VMEM((NG, NG), jnp.bfloat16),
            pltpu.VMEM(lines.shape, jnp.float32),
            pltpu.SemaphoreType.DMA((13,)),
            pairs,
            pairs,
            pairs,
            pairs,
            pairs,
            pairs,
            pltpu.SemaphoreType.DMA((pen_count,)),
            pltpu.SemaphoreType.DMA((pen_count,)),
            pltpu.SemaphoreType.DMA((2,)),
            pltpu.SemaphoreType.DMA((2,)),
        ],
        compiler_params=pltpu.CompilerParams(
            collective_id=0, has_side_effects=True, vmem_limit_bytes=VMEM_LIMIT
        ),
        name="mesh",
    )(
        block_owner[:, 0],
        block_owner.reshape(1, local_blocks),
        block_band,
        block_count,
        cells,
        offsets,
        charges,
        table_high,
        table_low,
        table_along,
        lines,
    )
    return (potential[None], forces)


def solution(mesh):
    placed = (
        P(("pln", "pen"), None),
        P(("pln", "pen")),
        P(("pln", "pen")),
        P(("pln", "pen"), None),
        P(("pln", "pen"), None, None),
        P(("pln", "pen"), None),
    )
    return jax.shard_map(
        shards,
        mesh=mesh,
        in_specs=placed,
        out_specs=(P("pln", "pen", None), P(("pln", "pen"), None, None)),
        check_vma=False,
    )
```

```python
import functools
import math

import jax
import jax.numpy as jnp
import numpy as np
from jax import lax
from jax.experimental import pallas as pl
from jax.experimental.pallas import tpu as pltpu
from jax.sharding import PartitionSpec as P

NG = 1024
LANES = 128
CHUNKS = NG // LANES
screening = 2e-05
VMEM_LIMIT = 62 * 1024 * 1024
UNROLL = 8


def round_up(value, step):
    return -(-value // step) * step


@functools.lru_cache(None)
def hartley_tables():
    index = np.arange(NG)
    angle = 2.0 * np.pi / NG * (index[:, None] * index[None, :] % NG)
    table = np.cos(angle) + np.sin(angle)
    high = table.astype(jnp.bfloat16)
    low = (table - high.astype(np.float64)).astype(jnp.bfloat16)
    turn = 2.0 * np.pi / NG * np.arange(NG)
    slope = (2.0 * np.sin(2.0 * turn) - 16.0 * np.sin(turn)) / 12.0
    along = (slope[:, None] * (np.cos(angle) - np.sin(angle))).astype(jnp.bfloat16)
    return high, low, along


@functools.lru_cache(None)
def line_tables(pen_count):
    rows = NG // pen_count
    shift = 4.0 * np.sin(np.pi * np.arange(NG) / NG) ** 2 + screening
    root = 1.0 + shift / 2.0 - np.sqrt(shift + shift * shift / 4.0)
    i = np.arange(8)[:, None]

    def power(exponent):
        return root[None, :] ** (exponent + np.zeros((8, 1)))

    tiles = [
        power(7 - i),
        power(i),
        power(8),
        np.where(i >= 1, power(1), 0.0),
        np.where(i >= 2, power(2), 0.0),
        np.where(i >= 4, power(4), 0.0),
        np.where(i <= 6, power(1), 0.0),
        np.where(i <= 5, power(2), 0.0),
        np.where(i <= 3, power(4), 0.0),
        power(i + 1),
        power(8 - i),
        np.broadcast_to(1.0 / ((1.0 / root - root) * NG), (8, NG)),
        np.broadcast_to(2.0 + shift, (8, NG)),
        power(rows - 1),
    ]
    lags = np.arange(round_up(pen_count, 8))[:, None]
    tiles.append(root[None, :] ** (lags * rows) / (1.0 - root[None, :] ** NG))
    return np.concatenate(tiles, axis=0).astype(np.float32)


T_FEND, T_BEND, T_EIGHT, T_F1, T_F2, T_F4, T_B1, T_B2, T_B4, T_FC, T_BC, T_NORM, T_DIAG, T_LAST, T_LAG = range(15)


def fetch(sources, targets, sems):
    copies = [pltpu.make_async_copy(a, b, sems.at[i]) for i, (a, b) in enumerate(zip(sources, targets))]
    for copy in copies:
        copy.start()
    return copies


def list_blocks(capacity, owner, owner_row, tables):
    blocks = owner.shape[0]
    lane = lax.broadcasted_iota(jnp.int32, (8, LANES), 1)
    place = lax.broadcasted_iota(jnp.int32, (8, LANES), 0)
    owners = jnp.broadcast_to(owner_row[...], (8, LANES))
    unroll = 8

    def look(n, carry):
        block_at, used, rank = carry
        for k in range(unroll):
            i = n * unroll + k
            o = owner[i]
            named = lane == o
            block_at = jnp.where(named & (place == used), i, block_at)
            used = used + jnp.where(named, 1, 0)
            rank = rank + jnp.where((owners == o) & (lane > i), 1, 0)
        return block_at, used, rank

    nothing = jnp.zeros((8, LANES), jnp.int32)
    block_at, used, rank = lax.fori_loop(
        0, blocks // unroll, look, (jnp.full((8, LANES), blocks, jnp.int32), nothing, nothing)
    )
    tables[0:8] = block_at
    tables[8:16] = jnp.minimum(rank, capacity - 1)


def pack(s, other, capacity, tables, band, count, cells, offsets, charges, packed, heads_out):
    lane = lax.broadcasted_iota(jnp.int32, (1, LANES), 1)
    head = jnp.zeros((1, LANES), jnp.int32)
    rows = [[], [], [], []]
    for j in range(capacity):
        i = tables[j, other]
        pair = offsets[i]
        rows[0].append(pair[0:1])
        rows[1].append(pair[1:2])
        rows[2].append(jnp.where(lane < count[i], charges[pl.ds(i, 1), :], 0.0))
        rows[3].append(cells[pl.ds(i, 1), :].astype(jnp.float32))
        head = jnp.where(lane == j, band[i], head)
    for part in range(4):
        for j in range(capacity):
            packed[s, part * capacity + j : part * capacity + j + 1, :] = rows[part][j]
    heads_out[s] = head


def peer(index, pens):
    return (lax.div(index, pens), lax.rem(index, pens))


def exclusive(a, b, size):
    total = 0
    for bit in range(size.bit_length() - 1):
        p = lax.rem(lax.div(a, 1 << bit), 2)
        q = lax.rem(lax.div(b, 1 << bit), 2)
        total = total + (p + q - 2 * p * q) * (1 << bit)
    return total


def factors(frac_x, frac_y, weight, cell):
    cell = cell.astype(jnp.int32)
    column = cell & (NG - 1)
    after = (column + 1) & (NG - 1)
    row = cell >> (NG.bit_length() - 1)
    left = (1.0 - frac_x).astype(jnp.bfloat16).astype(jnp.float32)
    right = frac_x.astype(jnp.bfloat16).astype(jnp.float32)
    return frac_y, weight, row, column, after, left, right


def dot3(a_high, a_low, b_high, b_low):
    dot = functools.partial(jnp.dot, preferred_element_type=jnp.float32)
    return dot(a_high, b_high) + (dot(a_high, b_low) + dot(a_low, b_high))


def split(values):
    high = values.astype(jnp.bfloat16)
    return high, (values - high.astype(jnp.float32)).astype(jnp.bfloat16)


def doubled(values):
    return jnp.concatenate([values, values], axis=0).astype(jnp.bfloat16)


def iota16():
    return lax.broadcasted_iota(jnp.int32, (16, LANES), 0).astype(jnp.float32).astype(jnp.bfloat16)


def link_blocks(heads, links, capacity):
    count = heads.shape[0]
    total = count * capacity
    lane = lax.broadcasted_iota(jnp.int32, (8, LANES), 1)
    slot = lax.broadcasted_iota(jnp.int32, (8, LANES), 0) * LANES + lane

    def collect(s, bands):
        for j in range(capacity):
            bands = jnp.where(slot == s * capacity + j, heads[s, 0, j], bands)
        return bands

    bands = lax.fori_loop(0, count, collect, jnp.full((8, LANES), -1, jnp.int32))

    def link(s, carry):
        earlier, last = carry
        for j in range(capacity):
            here = s * capacity + j
            band = heads[s, 0, j]
            earlier = jnp.where((bands == band) & (slot > here), here, earlier)
            last = jnp.where(lane == band, here, last)
        return earlier, last

    nobody = jnp.full((8, LANES), total, jnp.int32)
    earlier, last = lax.fori_loop(0, count, link, (nobody, nobody))
    links[0:8] = earlier
    links[8:16] = last


def deposit(sources, capacity, recv, chain, links):
    sub8 = lax.broadcasted_iota(jnp.int32, (8, LANES), 0)
    sub16 = iota16()
    upper_half = jnp.where(sub16 < 8.0, 0.0, 1.0).astype(jnp.bfloat16)
    zero16 = jnp.zeros((16, LANES), jnp.bfloat16)

    def one(s, j):
        def spread(which):
            return recv[s, pl.ds(which * capacity + j, 8, stride=0), :]

        frac_y, weight, row, column, after, left, right = factors(spread(0), spread(1), spread(2), spread(3))
        lower = weight * (1.0 - frac_y)
        upper = weight * frac_y
        main = doubled(jnp.where(row == sub8, lower, jnp.where(row + 1 == sub8, upper, 0.0)))
        tail = doubled(jnp.where(row == 7, upper, 0.0))
        lhs, rhs = [], []
        for place, factor in ((column, left), (after, right)):
            chunk = doubled((place >> 7).astype(jnp.float32))
            index, factor = doubled((place & 127).astype(jnp.float32)), doubled(factor)
            tiles = [jnp.where(chunk == upper_half + float(2 * a), main, zero16) for a in range(CHUNKS // 2)]
            lhs.append(tiles + [jnp.where(chunk == sub16, tail, zero16)])
            rhs.append([jnp.where(index == sub16 + float(16 * b), factor, zero16) for b in range(LANES // 16)])
        lhs = [jnp.concatenate(both, axis=1) for both in zip(*lhs)]
        rhs = [jnp.concatenate(both, axis=1) for both in zip(*rhs)]
        values = lax.dot_general(
            jnp.concatenate(lhs, axis=0),
            jnp.concatenate(rhs, axis=0),
            (((1,), (1,)), ((), ())),
            preferred_element_type=jnp.float32,
        )
        return values[0 : CHUNKS * 8 + 8]

    places = [(s, j) for s in sources for j in range(capacity)]
    made = [one(s, j) for s, j in places]
    for (s, j), values in zip(places, made):
        slot = s * capacity + j
        earlier = links[lax.div(slot, LANES), lax.rem(slot, LANES)]
        chain[slot, 0 : CHUNKS * 8 + 8] = values + chain[earlier, 0 : CHUNKS * 8 + 8]


def assemble(bands, total, chain, links, hi, lo):
    first_row = lax.broadcasted_iota(jnp.int32, (8, LANES), 0) == 0

    def last_of(band):
        inside = (band >= 0) & (band < bands)
        return jnp.where(inside, links[8, jnp.clip(band, 0, bands - 1)], total)

    def rows_of(band):
        mine, above = last_of(band), last_of(band - 1)
        tiles = []
        for a in range(CHUNKS):
            extra = chain[above, pl.ds(CHUNKS * 8 + a, 8, stride=0)]
            tiles.append(chain[mine, a * 8 : a * 8 + 8] + jnp.where(first_row, extra, 0.0))
        return jnp.concatenate(tiles, axis=1)

    def pair(q, carry):
        high, low = split(jnp.concatenate([rows_of(2 * q), rows_of(2 * q + 1)], axis=0))
        at = pl.ds(pl.multiple_of(q * 16, 16), 16)
        hi[at, :] = high
        lo[at, :] = low
        return carry

    lax.fori_loop(0, bands // 2 + 1, pair, 0)


def transform(rows, hi, lo, table_high, table_low, lines, spectrum, sums, nexts, lasts):
    width = 256
    for n in range(NG // width):
        cols = slice(n * width, (n + 1) * width)
        values = dot3(hi[...], lo[...], table_high[:, cols], table_low[:, cols])
        spectrum[:, cols] = values[:rows]
        sums[2, 0:1, cols] = values[rows : rows + 1]
    eight = lines[T_EIGHT * 8 : T_EIGHT * 8 + 8]
    tiles = rows // 8

    def fold(t, carry):
        fwd, bwd = carry
        fwd = eight * fwd + spectrum[pl.ds(pl.multiple_of(t * 8, 8), 8), :]
        bwd = eight * bwd + spectrum[pl.ds(pl.multiple_of((tiles - 1 - t) * 8, 8), 8), :]
        return fwd, bwd

    nothing = jnp.zeros((8, NG), jnp.float32)
    fwd, bwd = lax.fori_loop(0, tiles, fold, (nothing, nothing))
    sums[0] = jnp.sum(fwd * lines[T_FEND * 8 : T_FEND * 8 + 8], axis=0, keepdims=True)
    sums[1] = jnp.sum(bwd * lines[T_BEND * 8 : T_BEND * 8 + 8], axis=0, keepdims=True)
    nexts[0] = spectrum[0:1]
    nexts[1] = spectrum[1:2]
    lasts[0] = spectrum[rows - 1 : rows]


def wave_tile(wave, row, height=8):
    return jnp.concatenate([wave[a, pl.ds(row, height), :] for a in range(CHUNKS)], axis=1)


def put_wave(wave, row, values):
    for a in range(CHUNKS):
        wave[a, pl.ds(row, values.shape[0]), :] = values[:, a * LANES : (a + 1) * LANES]


def local_scans(rows, spectrum, lines, wave):
    tiles = rows // 8

    def table(which):
        return lines[which * 8 : which * 8 + 8]

    def backward(i, carry):
        t = tiles - 1 - i
        where = pl.ds(pl.multiple_of(t * 8, 8), 8)
        x = spectrum[where, :]
        x = x + table(T_B1) * pltpu.roll(x, 7, 0)
        x = x + table(T_B2) * pltpu.roll(x, 6, 0)
        x = x + table(T_B4) * pltpu.roll(x, 4, 0)
        x = x + table(T_BC) * carry
        put_wave(wave, pl.multiple_of(t * 8 + 8, 8), x)
        return x[0:1]

    nothing = jnp.zeros((1, NG), jnp.float32)
    lax.fori_loop(0, tiles, backward, nothing)

    def forward(t, carry):
        where = pl.ds(pl.multiple_of(t * 8, 8), 8)
        d = spectrum[where, :]
        x = d + table(T_F1) * pltpu.roll(d, 1, 0)
        x = x + table(T_F2) * pltpu.roll(x, 2, 0)
        x = x + table(T_F4) * pltpu.roll(x, 4, 0)
        x = x + table(T_FC) * carry
        row = pl.multiple_of(t * 8 + 8, 8)
        put_wave(wave, row, x + wave_tile(wave, row) - d)
        return x[7:8]

    lax.fori_loop(0, tiles, forward, nothing)


def finish_solve(rows, mine, sums_of, nexts_of, lasts_of, lines, wave, stack):
    pens = sums_of.shape[0]
    tiles = rows // 8

    def table(which):
        return lines[which * 8 : which * 8 + 8]

    def row_of(pen, which):
        return sums_of[lax.rem(pen + 2 * pens, pens), which]

    last_power = table(T_LAST)[0:1]
    before = jnp.zeros((1, NG), jnp.float32)
    beyond = jnp.zeros((1, NG), jnp.float32)
    for j in range(pens):
        lag = lines[T_LAG * 8 + j : T_LAG * 8 + j + 1]
        behind, ahead = mine - 1 - j, mine + 1 + j
        before += lag * (row_of(behind, 0) + last_power * row_of(behind - 1, 2))
        beyond += lag * (row_of(ahead, 1) + row_of(ahead - 1, 2))
    incoming = row_of(mine - 1, 2)
    next_zero = nexts_of[0] + row_of(mine, 2)
    next_one = nexts_of[1]
    last_before = lasts_of[0]
    norm = table(T_NORM)[0:1]
    root = table(T_FC)[0:1]
    eight = table(T_EIGHT)
    ramp_down = norm * (root * before + incoming)
    ramp_up = norm * beyond
    first_back = row_of(mine, 1) + incoming + root * last_power * beyond
    final = row_of(mine, 0) + last_power * incoming + root * last_power * before

    def add_beyond(i, ramp):
        row = pl.multiple_of((tiles - 1 - i) * 8 + 8, 8)
        put_wave(wave, row, table(T_NORM) * wave_tile(wave, row) + ramp)
        return ramp * eight

    lax.fori_loop(0, tiles, add_beyond, table(T_BC) * ramp_up)

    def add_before(q, ramp):
        row = pl.multiple_of(q * 16 + 8, 8)
        then = ramp * eight
        values = wave_tile(wave, row, 16) + jnp.concatenate([ramp, then], axis=0)
        put_wave(wave, row, values)
        stack[pl.ds(pl.multiple_of(q * 16, 16), 16), :] = values.astype(jnp.bfloat16)
        return then * eight

    lax.fori_loop(0, tiles // 2, add_before, table(T_BEND) * ramp_down)
    diagonal = table(T_DIAG)[0:1]
    scale = 1.0 / NG
    up1 = norm * (before + root * first_back)
    up2 = diagonal * up1 - wave_tile(wave, 8, 1) - scale * last_before
    down0 = norm * (root * final + beyond)
    down1 = diagonal * down0 - wave_tile(wave, rows + 7, 1) - scale * next_zero
    down2 = diagonal * down1 - down0 - scale * next_one
    put_wave(wave, 0, jnp.concatenate([jnp.zeros((6, NG), jnp.float32), up2, up1], axis=0))
    below = jnp.concatenate([down0, down1, down2, jnp.zeros((21, NG), jnp.float32)], axis=0)
    put_wave(wave, rows + 8, below)
    stack[rows : rows + 16] = below[0:16].astype(jnp.bfloat16)

    def slope(q, carry):
        row = q * 16 + 8

        def at(shift):
            return wave_tile(wave, row + shift, 16)

        along_y = (8.0 * (at(1) - at(-1)) - (at(2) - at(-2))) * (-1.0 / 12.0)
        stack[pl.ds(pl.multiple_of(rows + 16 + q * 16, 16), 16), :] = along_y.astype(jnp.bfloat16)
        return carry

    lax.fori_loop(0, tiles // 2 + 1, slope, 0)


def invert(rows, stack, table_high, table_along, potential, potential_h, out_sem, forms, rim, field):
    width = 256
    tiles = rows // 8
    tall = rows + 16
    dot = functools.partial(jnp.dot, preferred_element_type=jnp.float32)
    for n in range(NG // width):
        cols = slice(n * width, (n + 1) * width)
        values = dot(stack[...], table_high[:, cols])
        potential[:, cols] = values[:rows]
        along = dot(stack[0:tall], table_along[:, cols])
        for k in range(width // LANES):
            a = n * (width // LANES) + k
            lanes = slice(k * LANES, (k + 1) * LANES)
            forms[a * tall : (a + 1) * tall] = along[:, lanes]
            forms[(CHUNKS + a) * tall : (CHUNKS + a + 1) * tall] = values[tall:, lanes]
    out_copy = pltpu.make_async_copy(potential, potential_h, out_sem)
    out_copy.start()

    def gather_tile(t, carry):
        row = pl.multiple_of(t * 8, 8)
        for a in range(CHUNKS):
            both = [forms[pl.ds(pl.multiple_of((c * CHUNKS + a) * tall + row, 8), 8), :] for c in range(2)]
            field[t, :, a * LANES : (a + 1) * LANES] = jnp.concatenate(both, axis=0).astype(jnp.bfloat16)
        ends = [forms[pl.ds(c * CHUNKS * tall + row + 8, CHUNKS, stride=tall), :] for c in range(2)]
        rim[t, :, 0:LANES] = jnp.concatenate(ends, axis=0).astype(jnp.bfloat16)
        ends = [pltpu.roll(e, CHUNKS - 1, 0) for e in ends]
        rim[t, :, LANES : 2 * LANES] = jnp.concatenate(ends, axis=0).astype(jnp.bfloat16)
        return carry

    lax.fori_loop(0, tiles, gather_tile, 0)
    return out_copy


def mesh_kernel(planes, pens, capacity, rows, owner_h, owner_row_h, band_h, count_h, cells_h, offsets_h, charges_h,
                table_high_h, table_low_h, table_along_h, lines_h, potential_h, out, forces, returned, packed, recv, heads_out, heads,
                heads_s, ids, owner, owner_row, band, block_count, cells, offsets, charges, tables_v, tables, links_v,
                links, chain, field, rim, wave, hi, lo, stack, forms, potential, spectrum, sums, nexts, lasts, sums_of,
                nexts_of, lasts_of, table_high, table_low, table_along, lines, sems,
                send_sems, recv_sems, head_send_sems, head_recv_sems, back_send_sems, back_recv_sems, edge_send_sems,
                edge_recv_sems, side_send_sems, side_recv_sems):
    count = planes * pens
    total = count * capacity
    tall = 4 * capacity
    blocks = owner.shape[0]
    plane = lax.axis_index("pln")
    mine = lax.axis_index("pen")
    me = plane * pens + mine
    barrier = pltpu.get_barrier_semaphore()
    copies = fetch(
        (owner_h, owner_row_h, band_h, count_h, cells_h, offsets_h, charges_h, lines_h, table_high_h, table_low_h,
         table_along_h),
        (owner, owner_row, band.at[0:blocks], block_count.at[0:blocks], cells.at[0:blocks], offsets.at[0:blocks],
         charges.at[0:blocks], lines, table_high, table_low, table_along),
        sems,
    )

    def greet(s, carry):
        other = (
            exclusive(plane, lax.rem(s, planes), planes),
            exclusive(mine, lax.div(s, planes), pens),
        )
        ids[s] = other[0] * pens + other[1]
        pl.semaphore_signal(barrier, inc=1, device_id=other, device_id_type=pl.DeviceIdType.MESH)
        return carry

    ids[0] = me
    lax.fori_loop(1, count, greet, 0)
    copies[0].wait()
    copies[1].wait()
    list_blocks(capacity, owner, owner_row, tables_v)
    tables_copy = pltpu.make_async_copy(tables_v, tables, sems.at[11])
    tables_copy.start()
    cells[blocks : blocks + 8] = jnp.zeros((8, LANES), jnp.int32)
    charges[blocks : blocks + 8] = jnp.zeros((8, LANES), jnp.float32)
    offsets[blocks] = jnp.zeros((2, LANES), jnp.float32)
    for copy in copies[2:7]:
        copy.wait()
    band[blocks] = 0
    block_count[blocks] = 0
    tables_copy.wait()

    def fill(s, carry):
        pack(s, ids[s], capacity, tables, band, block_count, cells, offsets, charges, packed, heads_out)
        return carry

    lax.fori_loop(0, count, fill, 0)
    recv[0, 0:tall] = packed[0]
    heads[0] = heads_out[0]
    chain[total] = jnp.zeros(chain.shape[1:], jnp.float32)
    pl.semaphore_wait(barrier, count - 1)

    def remote(s, source, place, send, receive):
        return pltpu.make_async_remote_copy(
            src_ref=source,
            dst_ref=place,
            send_sem=send.at[s],
            recv_sem=receive.at[s],
            device_id=peer(ids[s], pens),
            device_id_type=pl.DeviceIdType.MESH,
        )

    def head_copy(s):
        return remote(s, heads_out.at[s], heads.at[s], head_send_sems, head_recv_sems)

    def block_copy(s):
        return remote(s, packed.at[s], recv.at[s, 0:tall], send_sems, recv_sems)

    def back_copy(s):
        return remote(s, forces.at[s], returned.at[me], back_send_sems, back_recv_sems)

    def send_heads(s, carry):
        head_copy(s).start()
        return carry

    def send_blocks(s, carry):
        block_copy(s).start()
        return carry

    def take_heads(s, carry):
        head_copy(s).wait_recv()
        return carry

    lax.fori_loop(1, count, send_heads, 0)
    lax.fori_loop(1, count, send_blocks, 0)
    lax.fori_loop(1, count, take_heads, 0)
    heads_copy = pltpu.make_async_copy(heads, heads_s, sems.at[11])
    heads_copy.start()
    heads_copy.wait()
    link_blocks(heads_s, links_v, capacity)
    links_copy = pltpu.make_async_copy(links_v, links, sems.at[11])
    links_copy.start()
    links_copy.wait()

    bunch = 4

    def receive(i, carry):
        sources = [i * bunch + k for k in range(bunch)]
        for s in sources:
            @pl.when(s > 0)
            def _():
                block_copy(s).wait_recv()

        deposit(sources, capacity, recv, chain, links)
        return carry

    lax.fori_loop(0, count // bunch, receive, 0)
    assemble(rows // 8, total, chain, links, hi, lo)
    for copy in copies[7:]:
        copy.wait()
    transform(rows, hi, lo, table_high, table_low, lines, spectrum, sums, nexts, lasts)
    sums_of[mine] = sums[...]

    def edge_copy(k, place, other):
        return pltpu.make_async_remote_copy(
            src_ref=sums,
            dst_ref=sums_of.at[place],
            send_sem=edge_send_sems.at[k],
            recv_sem=edge_recv_sems.at[k],
            device_id=(plane, other),
            device_id_type=pl.DeviceIdType.MESH,
        )

    def side_copy(n, source, place, other):
        return pltpu.make_async_remote_copy(
            src_ref=source,
            dst_ref=place,
            send_sem=side_send_sems.at[n],
            recv_sem=side_recv_sems.at[n],
            device_id=(plane, other),
            device_id_type=pl.DeviceIdType.MESH,
        )

    up_copy = side_copy(0, nexts, nexts_of, lax.rem(mine + pens - 1, pens))
    down_copy = side_copy(1, lasts, lasts_of, lax.rem(mine + 1, pens))
    for k in range(1, pens):
        edge_copy(k, mine, lax.rem(mine + k, pens)).start()
    up_copy.start()
    down_copy.start()
    local_scans(rows, spectrum, lines, wave)
    for k in range(1, pens):
        behind = lax.rem(mine - k + pens, pens)
        edge_copy(k, mine, lax.rem(mine + k, pens)).wait_send()
        edge_copy(k, behind, behind).wait_recv()
    up_copy.wait()
    down_copy.wait()
    finish_solve(rows, mine, sums_of, nexts_of, lasts_of, lines, wave, stack)
    out_copy = invert(rows, stack, table_high, table_along, potential, potential_h, sems.at[12], forms, rim, field)
    sub8 = lax.broadcasted_iota(jnp.int32, (8, LANES), 0)
    sub16 = iota16()
    zero16 = jnp.zeros((16, LANES), jnp.bfloat16)

    def one(d, j):
        def spread(which):
            return recv[d, pl.ds(which * capacity + j, 8, stride=0), :]

        band = heads_s[d, 0, j]
        frac_y, weight, row, column, after, left, right = factors(
            spread(0), spread(1), spread(2), spread(3)
        )
        chunk = column >> 7
        index = (column & 127).astype(jnp.float32)
        spot, left16, right16 = doubled(index), doubled(left), doubled(right)
        next_spot = doubled(index + 1.0)
        picks = []
        for b in range(LANES // 16 + 1):
            here = sub16 + float(16 * b)
            picks.append(jnp.where(here == spot, left16, jnp.where(here == next_spot, right16, zero16)))
        picks += [zero16] * (2 * LANES // 16 - len(picks))
        rows_of = field[band]
        windows = [
            jnp.concatenate(
                [
                    rows_of[:, a * LANES : (a + 1) * LANES],
                    rows_of[:, (a + 1) % CHUNKS * LANES : ((a + 1) % CHUNKS + 1) * LANES],
                ],
                axis=1,
            )
            for a in range(CHUNKS)
        ]
        values = jnp.dot(
            jnp.concatenate(windows + [rim[band]], axis=0),
            jnp.concatenate(picks, axis=0),
            preferred_element_type=jnp.float32,
        )
        row_weight = weight * jnp.where(row == sub8, 1.0 - frac_y, jnp.where(row + 1 == sub8, frac_y, 0.0))
        mixed = [values[0:8], values[8:16]]
        for a in range(1, CHUNKS):
            held = chunk == a
            mixed = [jnp.where(held, values[a * 16 + c * 8 : a * 16 + c * 8 + 8], mixed[c]) for c in range(2)]
        edge = weight * jnp.where(row == 7, frac_y, 0.0)
        at_edge = sub8 == chunk
        rims = [jnp.where(at_edge, values[CHUNKS * 16 + c * 8 : CHUNKS * 16 + c * 8 + 8], 0.0) for c in range(2)]
        return [jnp.sum(row_weight * mixed[c] + edge * rims[c], axis=0, keepdims=True) for c in range(2)]

    def pull(sources):
        made = [[one(d, j) for j in range(capacity)] for d in sources]
        for d, results in zip(sources, made):
            keep(d, results)

    def keep(d, made):
        for c in range(2):
            for j in range(capacity):
                forces[d, c * capacity + j : c * capacity + j + 1, :] = made[j][c]
        if forces.shape[1] > 2 * capacity:
            forces[d, 2 * capacity :, :] = jnp.zeros((forces.shape[1] - 2 * capacity, LANES), jnp.float32)

    group = 4

    def step(i, carry):
        sources = [count - 1 - i * group - k for k in range(group)]
        pull(sources)
        for s in sources:
            back_copy(s).start()
        return carry

    lax.fori_loop(0, count // group - 1, step, 0)
    pull(list(range(group)))
    for s in range(1, group):
        back_copy(s).start()
    returned[me] = forces[0]

    def finish(i, carry):
        s = count - i
        head_copy(s).wait_send()
        block_copy(s).wait_send()
        back_copy(s).wait_send()
        back_copy(s).wait_recv()
        return carry

    lax.fori_loop(1, count, finish, 0)

    def take(n, carry):
        for k in range(8):
            i = n * 8 + k
            d, j = owner[i], tables[8, i]
            out[i, 0:1, :] = returned[d, pl.ds(j, 1), :]
            out[i, 1:2, :] = returned[d, pl.ds(capacity + j, 1), :]
        return carry

    lax.fori_loop(0, blocks // 8, take, 0)
    out_copy.wait()


def copy_kernel(parts, potential_h, forces_h, potential, forces, rows_held, blocks_held, sems):
    rows, blocks = potential.shape[0] // parts, forces.shape[0] // parts
    reads, writes = [], []
    for n in range(parts):
        part = slice(n * rows, (n + 1) * rows)
        reads.append(pltpu.make_async_copy(potential_h.at[part], rows_held.at[part], sems.at[4 * n]))
        writes.append(pltpu.make_async_copy(rows_held.at[part], potential.at[part], sems.at[4 * n + 1]))
        part = slice(n * blocks, (n + 1) * blocks)
        reads.append(pltpu.make_async_copy(forces_h.at[part], blocks_held.at[part], sems.at[4 * n + 2]))
        writes.append(pltpu.make_async_copy(blocks_held.at[part], forces.at[part], sems.at[4 * n + 3]))
    for read in reads:
        read.start()
    for read, write in zip(reads, writes):
        read.wait()
        write.start()
    for write in writes:
        write.wait()


def shards(block_owner, block_band, block_count, cells, offsets, charges):
    plane_count = lax.axis_size("pln")
    pen_count = lax.axis_size("pen")
    devices = plane_count * pen_count
    local_blocks, block_len = charges.shape
    capacity = max(2, 2 * local_blocks // devices)
    total = devices * capacity
    rows = NG // pen_count
    tall = 4 * capacity
    tall_back = round_up(2 * capacity, 8)
    vmem = pl.BlockSpec(memory_space=pltpu.VMEM)
    far = pl.BlockSpec(memory_space=pltpu.HBM)
    table_high, table_low, table_along = (jnp.asarray(t) for t in hartley_tables())
    lines = jnp.asarray(line_tables(pen_count))
    pairs = pltpu.SemaphoreType.DMA((devices,))
    potential, forces = pl.pallas_call(
        functools.partial(mesh_kernel, plane_count, pen_count, capacity, rows),
        out_shape=(
            jax.ShapeDtypeStruct((rows, NG), jnp.float32),
            jax.ShapeDtypeStruct((local_blocks, 2, block_len), jnp.float32),
        ),
        in_specs=[far] * 11,
        out_specs=(far, vmem),
        scratch_shapes=[
            pltpu.VMEM((devices, tall_back, LANES), jnp.float32),
            pltpu.VMEM((devices, tall_back, LANES), jnp.float32),
            pltpu.VMEM((devices, tall, LANES), jnp.float32),
            pltpu.VMEM((devices, tall + 8, LANES), jnp.float32),
            pltpu.VMEM((devices, 1, LANES), jnp.int32),
            pltpu.VMEM((devices, 1, LANES), jnp.int32),
            pltpu.SMEM((devices, 1, LANES), jnp.int32),
            pltpu.SMEM((devices,), jnp.int32),
            pltpu.SMEM((local_blocks,), jnp.int32),
            pltpu.VMEM((1, local_blocks), jnp.int32),
            pltpu.SMEM((local_blocks + 8,), jnp.int32),
            pltpu.SMEM((local_blocks + 8,), jnp.int32),
            pltpu.VMEM((local_blocks + 8, block_len), jnp.int32),
            pltpu.VMEM((local_blocks + 8, 2, block_len), jnp.float32),
            pltpu.VMEM((local_blocks + 8, block_len), jnp.float32),
            pltpu.VMEM((16, LANES), jnp.int32),
            pltpu.SMEM((16, LANES), jnp.int32),
            pltpu.VMEM((16, LANES), jnp.int32),
            pltpu.SMEM((16, LANES), jnp.int32),
            pltpu.VMEM((total + 1, CHUNKS * 8 + 16, LANES), jnp.float32),
            pltpu.VMEM((rows // 8, 16, NG), jnp.bfloat16),
            pltpu.VMEM((rows // 8, 16, 2 * LANES), jnp.bfloat16),
            pltpu.VMEM((CHUNKS, rows + 32, LANES), jnp.float32),
            pltpu.VMEM((rows + 16, NG), jnp.bfloat16),
            pltpu.VMEM((rows + 16, NG), jnp.bfloat16),
            pltpu.VMEM((2 * rows + 32, NG), jnp.bfloat16),
            pltpu.VMEM((2 * CHUNKS * (rows + 16), LANES), jnp.float32),
            pltpu.VMEM((rows, NG), jnp.float32),
            pltpu.VMEM((rows, NG), jnp.float32),
            pltpu.VMEM((3, 1, NG), jnp.float32),
            pltpu.VMEM((2, 1, NG), jnp.float32),
            pltpu.VMEM((1, 1, NG), jnp.float32),
            pltpu.VMEM((pen_count, 3, 1, NG), jnp.float32),
            pltpu.VMEM((2, 1, NG), jnp.float32),
            pltpu.VMEM((1, 1, NG), jnp.float32),
            pltpu.VMEM((NG, NG), jnp.bfloat16),
            pltpu.VMEM((NG, NG), jnp.bfloat16),
            pltpu.VMEM((NG, NG), jnp.bfloat16),
            pltpu.VMEM(lines.shape, jnp.float32),
            pltpu.SemaphoreType.DMA((13,)),
            pairs,
            pairs,
            pairs,
            pairs,
            pairs,
            pairs,
            pltpu.SemaphoreType.DMA((pen_count,)),
            pltpu.SemaphoreType.DMA((pen_count,)),
            pltpu.SemaphoreType.DMA((2,)),
            pltpu.SemaphoreType.DMA((2,)),
        ],
        compiler_params=pltpu.CompilerParams(
            collective_id=0, has_side_effects=True, vmem_limit_bytes=VMEM_LIMIT
        ),
        name="mesh",
    )(
        block_owner[:, 0],
        block_owner.reshape(1, local_blocks),
        block_band,
        block_count,
        cells,
        offsets,
        charges,
        table_high,
        table_low,
        table_along,
        lines,
    )
    parts = 2
    potential, forces = pl.pallas_call(
        functools.partial(copy_kernel, parts),
        out_shape=(
            jax.ShapeDtypeStruct(potential.shape, jnp.float32),
            jax.ShapeDtypeStruct(forces.shape, jnp.float32),
        ),
        in_specs=[far] * 2,
        out_specs=(far, far),
        scratch_shapes=[
            pltpu.VMEM(potential.shape, jnp.float32),
            pltpu.VMEM(forces.shape, jnp.float32),
            pltpu.SemaphoreType.DMA((4 * parts,)),
        ],
        name="copy",
    )(potential, forces)
    return (potential[None], forces)


def solution(mesh):
    placed = (
        P(("pln", "pen"), None),
        P(("pln", "pen")),
        P(("pln", "pen")),
        P(("pln", "pen"), None),
        P(("pln", "pen"), None, None),
        P(("pln", "pen"), None),
    )
    return jax.shard_map(
        shards,
        mesh=mesh,
        in_specs=placed,
        out_specs=(P("pln", "pen", None), P(("pln", "pen"), None, None)),
        check_vma=False,
    )
```

```python
import functools
import math

import jax
import jax.numpy as jnp
import numpy as np
from jax import lax
from jax.experimental import pallas as pl
from jax.experimental.pallas import tpu as pltpu
from jax.sharding import PartitionSpec as P

NG = 1024
LANES = 128
CHUNKS = NG // LANES
screening = 2e-05
VMEM_LIMIT = 56 * 1024 * 1024
UNROLL = 8


def round_up(value, step):
    return -(-value // step) * step


@functools.lru_cache(None)
def hartley_tables():
    index = np.arange(NG)
    angle = 2.0 * np.pi / NG * (index[:, None] * index[None, :] % NG)
    table = np.cos(angle) + np.sin(angle)
    high = table.astype(jnp.bfloat16)
    turn = 2.0 * np.pi / NG * np.arange(NG)
    slope = (2.0 * np.sin(2.0 * turn) - 16.0 * np.sin(turn)) / 12.0
    along = (slope[:, None] * (np.cos(angle) - np.sin(angle))).astype(jnp.bfloat16)
    return high, along


@functools.lru_cache(None)
def line_tables(pen_count):
    rows = NG // pen_count
    shift = 4.0 * np.sin(np.pi * np.arange(NG) / NG) ** 2 + screening
    root = 1.0 + shift / 2.0 - np.sqrt(shift + shift * shift / 4.0)
    i = np.arange(8)[:, None]

    def power(exponent):
        return root[None, :] ** (exponent + np.zeros((8, 1)))

    tiles = [
        power(7 - i),
        power(i),
        power(8),
        np.where(i >= 1, power(1), 0.0),
        np.where(i >= 2, power(2), 0.0),
        np.where(i >= 4, power(4), 0.0),
        np.where(i <= 6, power(1), 0.0),
        np.where(i <= 5, power(2), 0.0),
        np.where(i <= 3, power(4), 0.0),
        power(i + 1),
        power(8 - i),
        np.broadcast_to(1.0 / ((1.0 / root - root) * NG), (8, NG)),
        np.broadcast_to(2.0 + shift, (8, NG)),
        power(rows - 1),
    ]
    lags = np.arange(round_up(pen_count, 8))[:, None]
    tiles.append(root[None, :] ** (lags * rows) / (1.0 - root[None, :] ** NG))
    return np.concatenate(tiles, axis=0).astype(np.float32)


T_FEND, T_BEND, T_EIGHT, T_F1, T_F2, T_F4, T_B1, T_B2, T_B4, T_FC, T_BC, T_NORM, T_DIAG, T_LAST, T_LAG = range(15)


def fetch(sources, targets, sems):
    copies = [pltpu.make_async_copy(a, b, sems.at[i]) for i, (a, b) in enumerate(zip(sources, targets))]
    for copy in copies:
        copy.start()
    return copies


def list_blocks(capacity, owner, owner_row, tables):
    blocks = owner.shape[0]
    lane = lax.broadcasted_iota(jnp.int32, (8, LANES), 1)
    place = lax.broadcasted_iota(jnp.int32, (8, LANES), 0)
    owners = jnp.broadcast_to(owner_row[...], (8, LANES))
    unroll = 8

    def look(n, carry):
        block_at, used, rank = carry
        for k in range(unroll):
            i = n * unroll + k
            o = owner[i]
            named = lane == o
            block_at = jnp.where(named & (place == used), i, block_at)
            used = used + jnp.where(named, 1, 0)
            rank = rank + jnp.where((owners == o) & (lane > i), 1, 0)
        return block_at, used, rank

    nothing = jnp.zeros((8, LANES), jnp.int32)
    block_at, used, rank = lax.fori_loop(
        0, blocks // unroll, look, (jnp.full((8, LANES), blocks, jnp.int32), nothing, nothing)
    )
    tables[0:8] = block_at
    tables[8:16] = jnp.minimum(rank, capacity - 1)


def pack(s, other, capacity, tables, band, count, cells, offsets, charges, packed, heads_out):
    lane = lax.broadcasted_iota(jnp.int32, (1, LANES), 1)
    head = jnp.zeros((1, LANES), jnp.int32)
    rows = [[], [], [], []]
    for j in range(capacity):
        i = tables[j, other]
        pair = offsets[i]
        rows[0].append(pair[0:1])
        rows[1].append(pair[1:2])
        rows[2].append(jnp.where(lane < count[i], charges[pl.ds(i, 1), :], 0.0))
        rows[3].append(cells[pl.ds(i, 1), :].astype(jnp.float32))
        head = jnp.where(lane == j, band[i], head)
    for part in range(4):
        for j in range(capacity):
            packed[s, part * capacity + j : part * capacity + j + 1, :] = rows[part][j]
    heads_out[s] = head


def peer(index, pens):
    return (lax.div(index, pens), lax.rem(index, pens))


def exclusive(a, b, size):
    total = 0
    for bit in range(size.bit_length() - 1):
        p = lax.rem(lax.div(a, 1 << bit), 2)
        q = lax.rem(lax.div(b, 1 << bit), 2)
        total = total + (p + q - 2 * p * q) * (1 << bit)
    return total


def factors(frac_x, frac_y, weight, cell):
    cell = cell.astype(jnp.int32)
    column = cell & (NG - 1)
    after = (column + 1) & (NG - 1)
    row = cell >> (NG.bit_length() - 1)
    left = (1.0 - frac_x).astype(jnp.bfloat16).astype(jnp.float32)
    right = frac_x.astype(jnp.bfloat16).astype(jnp.float32)
    return frac_y, weight, row, column, after, left, right


def doubled(values):
    return jnp.concatenate([values, values], axis=0).astype(jnp.bfloat16)


def iota16():
    return lax.broadcasted_iota(jnp.int32, (16, LANES), 0).astype(jnp.float32).astype(jnp.bfloat16)


def link_blocks(heads, links, capacity):
    count = heads.shape[0]
    total = count * capacity
    lane = lax.broadcasted_iota(jnp.int32, (8, LANES), 1)
    slot = lax.broadcasted_iota(jnp.int32, (8, LANES), 0) * LANES + lane

    def collect(s, bands):
        for j in range(capacity):
            bands = jnp.where(slot == s * capacity + j, heads[s, 0, j], bands)
        return bands

    bands = lax.fori_loop(0, count, collect, jnp.full((8, LANES), -1, jnp.int32), unroll=4)

    def link(s, carry):
        earlier, last = carry
        for j in range(capacity):
            here = s * capacity + j
            band = heads[s, 0, j]
            earlier = jnp.where((bands == band) & (slot > here), here, earlier)
            last = jnp.where(lane == band, here, last)
        return earlier, last

    nobody = jnp.full((8, LANES), total, jnp.int32)
    earlier, last = lax.fori_loop(0, count, link, (nobody, nobody), unroll=4)
    links[0:8] = earlier
    links[8:16] = last


def deposit(sources, capacity, recv, chain, links):
    sub8 = lax.broadcasted_iota(jnp.int32, (8, LANES), 0)
    sub16 = iota16()
    upper_half = jnp.where(sub16 < 8.0, 0.0, 1.0).astype(jnp.bfloat16)
    zero16 = jnp.zeros((16, LANES), jnp.bfloat16)

    def one(s, j):
        def spread(which):
            return recv[s, pl.ds(which * capacity + j, 8, stride=0), :]

        frac_y, weight, row, column, after, left, right = factors(spread(0), spread(1), spread(2), spread(3))
        lower = weight * (1.0 - frac_y)
        upper = weight * frac_y
        main = doubled(jnp.where(row == sub8, lower, jnp.where(row + 1 == sub8, upper, 0.0)))
        tail = doubled(jnp.where(row == 7, upper, 0.0))
        lhs, rhs = [], []
        for place, factor in ((column, left), (after, right)):
            chunk = doubled((place >> 7).astype(jnp.float32))
            index, factor = doubled((place & 127).astype(jnp.float32)), doubled(factor)
            tiles = [jnp.where(chunk == upper_half + float(2 * a), main, zero16) for a in range(CHUNKS // 2)]
            lhs.append(tiles + [jnp.where(chunk == sub16, tail, zero16)])
            rhs.append([jnp.where(index == sub16 + float(16 * b), factor, zero16) for b in range(LANES // 16)])
        lhs = [jnp.concatenate(both, axis=1) for both in zip(*lhs)]
        rhs = [jnp.concatenate(both, axis=1) for both in zip(*rhs)]
        values = lax.dot_general(
            jnp.concatenate(lhs, axis=0),
            jnp.concatenate(rhs, axis=0),
            (((1,), (1,)), ((), ())),
            preferred_element_type=jnp.float32,
        )
        return values[0 : CHUNKS * 8 + 8]

    places = [(s, j) for s in sources for j in range(capacity)]
    made = [one(s, j) for s, j in places]
    for (s, j), values in zip(places, made):
        slot = s * capacity + j
        earlier = links[lax.div(slot, LANES), lax.rem(slot, LANES)]
        chain[slot, 0 : CHUNKS * 8 + 8] = values + chain[earlier, 0 : CHUNKS * 8 + 8]


def assemble(bands, total, chain, links, hi):
    first_row = lax.broadcasted_iota(jnp.int32, (8, LANES), 0) == 0

    def last_of(band):
        inside = (band >= 0) & (band < bands)
        return jnp.where(inside, links[8, jnp.clip(band, 0, bands - 1)], total)

    def rows_of(band):
        mine, above = last_of(band), last_of(band - 1)
        tiles = []
        for a in range(CHUNKS):
            extra = chain[above, pl.ds(CHUNKS * 8 + a, 8, stride=0)]
            tiles.append(chain[mine, a * 8 : a * 8 + 8] + jnp.where(first_row, extra, 0.0))
        return jnp.concatenate(tiles, axis=1)

    def pair(q, carry):
        both = jnp.concatenate([rows_of(2 * q), rows_of(2 * q + 1)], axis=0)
        hi[pl.ds(pl.multiple_of(q * 16, 16), 16), :] = both.astype(jnp.bfloat16)
        return carry

    lax.fori_loop(0, bands // 2, pair, 0, unroll=4)
    pair(bands // 2, 0)


def transform(rows, hi, table_high, lines, spectrum, sums, nexts, lasts):
    width = 256
    for n in range(NG // width):
        cols = slice(n * width, (n + 1) * width)
        values = jnp.dot(hi[...], table_high[:, cols], preferred_element_type=jnp.float32)
        spectrum[:, cols] = values[:rows]
        sums[2, 0:1, cols] = values[rows : rows + 1]
    eight = lines[T_EIGHT * 8 : T_EIGHT * 8 + 8]
    tiles = rows // 8

    def fold(t, carry):
        fwd, bwd = carry
        fwd = eight * fwd + spectrum[pl.ds(pl.multiple_of(t * 8, 8), 8), :]
        bwd = eight * bwd + spectrum[pl.ds(pl.multiple_of((tiles - 1 - t) * 8, 8), 8), :]
        return fwd, bwd

    nothing = jnp.zeros((8, NG), jnp.float32)
    fwd, bwd = lax.fori_loop(0, tiles, fold, (nothing, nothing), unroll=4)
    sums[0] = jnp.sum(fwd * lines[T_FEND * 8 : T_FEND * 8 + 8], axis=0, keepdims=True)
    sums[1] = jnp.sum(bwd * lines[T_BEND * 8 : T_BEND * 8 + 8], axis=0, keepdims=True)
    nexts[0] = spectrum[0:1]
    nexts[1] = spectrum[1:2]
    lasts[0] = spectrum[rows - 1 : rows]


def wave_tile(wave, row, height=8):
    return jnp.concatenate([wave[a, pl.ds(row, height), :] for a in range(CHUNKS)], axis=1)


def put_wave(wave, row, values):
    for a in range(CHUNKS):
        wave[a, pl.ds(row, values.shape[0]), :] = values[:, a * LANES : (a + 1) * LANES]


def local_scans(rows, spectrum, lines, wave):
    tiles = rows // 8

    def table(which):
        return lines[which * 8 : which * 8 + 8]

    def backward(i, carry):
        t = tiles - 1 - i
        where = pl.ds(pl.multiple_of(t * 8, 8), 8)
        x = spectrum[where, :]
        x = x + table(T_B1) * pltpu.roll(x, 7, 0)
        x = x + table(T_B2) * pltpu.roll(x, 6, 0)
        x = x + table(T_B4) * pltpu.roll(x, 4, 0)
        x = x + table(T_BC) * carry
        put_wave(wave, pl.multiple_of(t * 8 + 8, 8), x)
        return x[0:1]

    nothing = jnp.zeros((1, NG), jnp.float32)
    lax.fori_loop(0, tiles, backward, nothing)

    def forward(t, carry):
        where = pl.ds(pl.multiple_of(t * 8, 8), 8)
        d = spectrum[where, :]
        x = d + table(T_F1) * pltpu.roll(d, 1, 0)
        x = x + table(T_F2) * pltpu.roll(x, 2, 0)
        x = x + table(T_F4) * pltpu.roll(x, 4, 0)
        x = x + table(T_FC) * carry
        row = pl.multiple_of(t * 8 + 8, 8)
        put_wave(wave, row, x + wave_tile(wave, row) - d)
        return x[7:8]

    lax.fori_loop(0, tiles, forward, nothing)


def finish_solve(rows, mine, sums_of, nexts_of, lasts_of, lines, wave, stack):
    pens = sums_of.shape[0]
    tiles = rows // 8

    def table(which):
        return lines[which * 8 : which * 8 + 8]

    def row_of(pen, which):
        return sums_of[lax.rem(pen + 2 * pens, pens), which]

    last_power = table(T_LAST)[0:1]
    before = jnp.zeros((1, NG), jnp.float32)
    beyond = jnp.zeros((1, NG), jnp.float32)
    for j in range(pens):
        lag = lines[T_LAG * 8 + j : T_LAG * 8 + j + 1]
        behind, ahead = mine - 1 - j, mine + 1 + j
        before += lag * (row_of(behind, 0) + last_power * row_of(behind - 1, 2))
        beyond += lag * (row_of(ahead, 1) + row_of(ahead - 1, 2))
    incoming = row_of(mine - 1, 2)
    next_zero = nexts_of[0] + row_of(mine, 2)
    next_one = nexts_of[1]
    last_before = lasts_of[0]
    norm = table(T_NORM)[0:1]
    root = table(T_FC)[0:1]
    eight = table(T_EIGHT)
    ramp_down = norm * (root * before + incoming)
    ramp_up = norm * beyond
    first_back = row_of(mine, 1) + incoming + root * last_power * beyond
    final = row_of(mine, 0) + last_power * incoming + root * last_power * before

    def add_beyond(i, ramp):
        row = pl.multiple_of((tiles - 1 - i) * 8 + 8, 8)
        put_wave(wave, row, table(T_NORM) * wave_tile(wave, row) + ramp)
        return ramp * eight

    lax.fori_loop(0, tiles, add_beyond, table(T_BC) * ramp_up, unroll=4)

    def add_before(q, ramp):
        row = pl.multiple_of(q * 16 + 8, 8)
        then = ramp * eight
        values = wave_tile(wave, row, 16) + jnp.concatenate([ramp, then], axis=0)
        put_wave(wave, row, values)
        stack[pl.ds(pl.multiple_of(q * 16, 16), 16), :] = values.astype(jnp.bfloat16)
        return then * eight

    lax.fori_loop(0, tiles // 2, add_before, table(T_BEND) * ramp_down, unroll=4)
    diagonal = table(T_DIAG)[0:1]
    scale = 1.0 / NG
    up1 = norm * (before + root * first_back)
    up2 = diagonal * up1 - wave_tile(wave, 8, 1) - scale * last_before
    down0 = norm * (root * final + beyond)
    down1 = diagonal * down0 - wave_tile(wave, rows + 7, 1) - scale * next_zero
    down2 = diagonal * down1 - down0 - scale * next_one
    put_wave(wave, 0, jnp.concatenate([jnp.zeros((6, NG), jnp.float32), up2, up1], axis=0))
    below = jnp.concatenate([down0, down1, down2, jnp.zeros((21, NG), jnp.float32)], axis=0)
    put_wave(wave, rows + 8, below)
    stack[rows : rows + 16] = below[0:16].astype(jnp.bfloat16)

    def slope(q, carry):
        row = q * 16 + 8

        def at(shift):
            return wave_tile(wave, row + shift, 16)

        along_y = (8.0 * (at(1) - at(-1)) - (at(2) - at(-2))) * (-1.0 / 12.0)
        stack[pl.ds(pl.multiple_of(rows + 16 + q * 16, 16), 16), :] = along_y.astype(jnp.bfloat16)
        return carry

    lax.fori_loop(0, tiles // 2 + 1, slope, 0)


def invert(rows, stack, table_high, table_along, potential, forms, rim, field):
    width = 256
    tiles = rows // 8
    tall = rows + 16
    dot = functools.partial(jnp.dot, preferred_element_type=jnp.float32)
    for n in range(NG // width):
        cols = slice(n * width, (n + 1) * width)
        values = dot(stack[...], table_high[:, cols])
        potential[:, cols] = values[:rows]
        along = dot(stack[0:tall], table_along[:, cols])
        for k in range(width // LANES):
            a = n * (width // LANES) + k
            lanes = slice(k * LANES, (k + 1) * LANES)
            forms[a * tall : (a + 1) * tall] = along[:, lanes]
            forms[(CHUNKS + a) * tall : (CHUNKS + a + 1) * tall] = values[tall:, lanes]

    def gather_tile(t, carry):
        row = pl.multiple_of(t * 8, 8)
        for a in range(CHUNKS):
            both = [forms[pl.ds(pl.multiple_of((c * CHUNKS + a) * tall + row, 8), 8), :] for c in range(2)]
            field[t, :, a * LANES : (a + 1) * LANES] = jnp.concatenate(both, axis=0).astype(jnp.bfloat16)
        ends = [forms[pl.ds(c * CHUNKS * tall + row + 8, CHUNKS, stride=tall), :] for c in range(2)]
        rim[t, :, 0:LANES] = jnp.concatenate(ends, axis=0).astype(jnp.bfloat16)
        ends = [pltpu.roll(e, CHUNKS - 1, 0) for e in ends]
        rim[t, :, LANES : 2 * LANES] = jnp.concatenate(ends, axis=0).astype(jnp.bfloat16)
        return carry

    lax.fori_loop(0, tiles, gather_tile, 0, unroll=4)


def mesh_kernel(planes, pens, capacity, rows, owner_h, owner_row_h, band_h, count_h, cells_h, offsets_h, charges_h,
                table_high_h, table_along_h, lines_h, potential, out, forces, returned, packed, recv, heads_out, heads,
                heads_s, ids, owner, owner_row, band, block_count, cells, offsets, charges, tables_v, tables, links_v,
                links, chain, field, rim, wave, hi, stack, forms, spectrum, sums, nexts, lasts, sums_of,
                nexts_of, lasts_of, table_high, table_along, lines, sems,
                send_sems, recv_sems, head_send_sems, head_recv_sems, back_send_sems, back_recv_sems, edge_send_sems,
                edge_recv_sems, side_send_sems, side_recv_sems):
    count = planes * pens
    total = count * capacity
    tall = 4 * capacity
    blocks = owner.shape[0]
    plane = lax.axis_index("pln")
    mine = lax.axis_index("pen")
    me = plane * pens + mine
    barrier = pltpu.get_barrier_semaphore()
    copies = fetch(
        (owner_h, owner_row_h, band_h, count_h, cells_h, offsets_h, charges_h, lines_h, table_high_h,
         table_along_h),
        (owner, owner_row, band.at[0:blocks], block_count.at[0:blocks], cells.at[0:blocks], offsets.at[0:blocks],
         charges.at[0:blocks], lines, table_high, table_along),
        sems,
    )

    def greet(s, carry):
        other = (
            exclusive(plane, lax.rem(s, planes), planes),
            exclusive(mine, lax.div(s, planes), pens),
        )
        ids[s] = other[0] * pens + other[1]
        pl.semaphore_signal(barrier, inc=1, device_id=other, device_id_type=pl.DeviceIdType.MESH)
        return carry

    ids[0] = me
    lax.fori_loop(1, count, greet, 0)
    copies[0].wait()
    copies[1].wait()
    list_blocks(capacity, owner, owner_row, tables_v)
    tables_copy = pltpu.make_async_copy(tables_v, tables, sems.at[11])
    tables_copy.start()
    cells[blocks : blocks + 8] = jnp.zeros((8, LANES), jnp.int32)
    charges[blocks : blocks + 8] = jnp.zeros((8, LANES), jnp.float32)
    offsets[blocks] = jnp.zeros((2, LANES), jnp.float32)
    for copy in copies[2:7]:
        copy.wait()
    band[blocks] = 0
    block_count[blocks] = 0
    tables_copy.wait()

    def fill(s, carry):
        pack(s, ids[s], capacity, tables, band, block_count, cells, offsets, charges, packed, heads_out)
        return carry

    lax.fori_loop(0, count, fill, 0, unroll=4)
    recv[0, 0:tall] = packed[0]
    heads[0] = heads_out[0]
    chain[total] = jnp.zeros(chain.shape[1:], jnp.float32)
    pl.semaphore_wait(barrier, count - 1)

    def remote(s, source, place, send, receive):
        return pltpu.make_async_remote_copy(
            src_ref=source,
            dst_ref=place,
            send_sem=send.at[s],
            recv_sem=receive.at[s],
            device_id=peer(ids[s], pens),
            device_id_type=pl.DeviceIdType.MESH,
        )

    def head_copy(s):
        return remote(s, heads_out.at[s], heads.at[s], head_send_sems, head_recv_sems)

    def block_copy(s):
        return remote(s, packed.at[s], recv.at[s, 0:tall], send_sems, recv_sems)

    def back_copy(s):
        return remote(s, forces.at[s], returned.at[me], back_send_sems, back_recv_sems)

    def send_heads(s, carry):
        head_copy(s).start()
        return carry

    def send_blocks(s, carry):
        block_copy(s).start()
        return carry

    def take_heads(s, carry):
        head_copy(s).wait_recv()
        return carry

    lax.fori_loop(1, count, send_heads, 0)
    lax.fori_loop(1, count, send_blocks, 0)
    lax.fori_loop(1, count, take_heads, 0)
    heads_copy = pltpu.make_async_copy(heads, heads_s, sems.at[11])
    heads_copy.start()
    heads_copy.wait()
    link_blocks(heads_s, links_v, capacity)
    links_copy = pltpu.make_async_copy(links_v, links, sems.at[11])
    links_copy.start()
    links_copy.wait()

    bunch = 4

    def receive(i, carry):
        sources = [i * bunch + k for k in range(bunch)]
        for s in sources:
            @pl.when(s > 0)
            def _():
                block_copy(s).wait_recv()

        deposit(sources, capacity, recv, chain, links)
        return carry

    lax.fori_loop(0, count // bunch, receive, 0)
    assemble(rows // 8, total, chain, links, hi)
    for copy in copies[7:]:
        copy.wait()
    transform(rows, hi, table_high, lines, spectrum, sums, nexts, lasts)
    sums_of[mine] = sums[...]

    def edge_copy(k, place, other):
        return pltpu.make_async_remote_copy(
            src_ref=sums,
            dst_ref=sums_of.at[place],
            send_sem=edge_send_sems.at[k],
            recv_sem=edge_recv_sems.at[k],
            device_id=(plane, other),
            device_id_type=pl.DeviceIdType.MESH,
        )

    def side_copy(n, source, place, other):
        return pltpu.make_async_remote_copy(
            src_ref=source,
            dst_ref=place,
            send_sem=side_send_sems.at[n],
            recv_sem=side_recv_sems.at[n],
            device_id=(plane, other),
            device_id_type=pl.DeviceIdType.MESH,
        )

    up_copy = side_copy(0, nexts, nexts_of, lax.rem(mine + pens - 1, pens))
    down_copy = side_copy(1, lasts, lasts_of, lax.rem(mine + 1, pens))
    for k in range(1, pens):
        edge_copy(k, mine, lax.rem(mine + k, pens)).start()
    up_copy.start()
    down_copy.start()
    local_scans(rows, spectrum, lines, wave)
    for k in range(1, pens):
        behind = lax.rem(mine - k + pens, pens)
        edge_copy(k, mine, lax.rem(mine + k, pens)).wait_send()
        edge_copy(k, behind, behind).wait_recv()
    up_copy.wait()
    down_copy.wait()
    finish_solve(rows, mine, sums_of, nexts_of, lasts_of, lines, wave, stack)
    invert(rows, stack, table_high, table_along, potential, forms, rim, field)
    sub8 = lax.broadcasted_iota(jnp.int32, (8, LANES), 0)
    sub16 = iota16()
    zero16 = jnp.zeros((16, LANES), jnp.bfloat16)

    def one(d, j):
        def spread(which):
            return recv[d, pl.ds(which * capacity + j, 8, stride=0), :]

        band = heads_s[d, 0, j]
        frac_y, weight, row, column, after, left, right = factors(
            spread(0), spread(1), spread(2), spread(3)
        )
        chunk = column >> 7
        index = (column & 127).astype(jnp.float32)
        spot, left16, right16 = doubled(index), doubled(left), doubled(right)
        next_spot = doubled(index + 1.0)
        picks = []
        for b in range(LANES // 16 + 1):
            here = sub16 + float(16 * b)
            picks.append(jnp.where(here == spot, left16, jnp.where(here == next_spot, right16, zero16)))
        picks += [zero16] * (2 * LANES // 16 - len(picks))
        rows_of = field[band]
        windows = [
            jnp.concatenate(
                [
                    rows_of[:, a * LANES : (a + 1) * LANES],
                    rows_of[:, (a + 1) % CHUNKS * LANES : ((a + 1) % CHUNKS + 1) * LANES],
                ],
                axis=1,
            )
            for a in range(CHUNKS)
        ]
        values = jnp.dot(
            jnp.concatenate(windows + [rim[band]], axis=0),
            jnp.concatenate(picks, axis=0),
            preferred_element_type=jnp.float32,
        )
        row_weight = weight * jnp.where(row == sub8, 1.0 - frac_y, jnp.where(row + 1 == sub8, frac_y, 0.0))
        mixed = [values[0:8], values[8:16]]
        for a in range(1, CHUNKS):
            held = chunk == a
            mixed = [jnp.where(held, values[a * 16 + c * 8 : a * 16 + c * 8 + 8], mixed[c]) for c in range(2)]
        edge = weight * jnp.where(row == 7, frac_y, 0.0)
        at_edge = sub8 == chunk
        rims = [jnp.where(at_edge, values[CHUNKS * 16 + c * 8 : CHUNKS * 16 + c * 8 + 8], 0.0) for c in range(2)]
        return [jnp.sum(row_weight * mixed[c] + edge * rims[c], axis=0, keepdims=True) for c in range(2)]

    def pull(sources):
        made = [[one(d, j) for j in range(capacity)] for d in sources]
        for d, results in zip(sources, made):
            keep(d, results)

    def keep(d, made):
        for c in range(2):
            for j in range(capacity):
                forces[d, c * capacity + j : c * capacity + j + 1, :] = made[j][c]
        if forces.shape[1] > 2 * capacity:
            forces[d, 2 * capacity :, :] = jnp.zeros((forces.shape[1] - 2 * capacity, LANES), jnp.float32)

    group = 4

    def step(i, carry):
        sources = [count - 1 - i * group - k for k in range(group)]
        pull(sources)
        for s in sources:
            back_copy(s).start()
        return carry

    lax.fori_loop(0, count // group - 1, step, 0)
    pull(list(range(group)))
    for s in range(1, group):
        back_copy(s).start()
    returned[me] = forces[0]

    def finish(i, carry):
        s = count - i
        head_copy(s).wait_send()
        block_copy(s).wait_send()
        back_copy(s).wait_send()
        back_copy(s).wait_recv()
        return carry

    lax.fori_loop(1, count, finish, 0)

    def take(n, carry):
        for k in range(8):
            i = n * 8 + k
            d, j = owner[i], tables[8, i]
            out[i, 0:1, :] = returned[d, pl.ds(j, 1), :]
            out[i, 1:2, :] = returned[d, pl.ds(capacity + j, 1), :]
        return carry

    lax.fori_loop(0, blocks // 8, take, 0, unroll=2)


def copy_kernel(potential_v, forces_v, potential, forces, sems):
    copies = fetch((potential_v, forces_v), (potential, forces), sems)
    for copy in copies:
        copy.wait()


def shards(block_owner, block_band, block_count, cells, offsets, charges):
    plane_count = lax.axis_size("pln")
    pen_count = lax.axis_size("pen")
    devices = plane_count * pen_count
    local_blocks, block_len = charges.shape
    capacity = max(2, 2 * local_blocks // devices)
    total = devices * capacity
    rows = NG // pen_count
    tall = 4 * capacity
    tall_back = round_up(2 * capacity, 8)
    vmem = pl.BlockSpec(memory_space=pltpu.VMEM)
    far = pl.BlockSpec(memory_space=pltpu.HBM)
    table_high, table_along = (jnp.asarray(t) for t in hartley_tables())
    lines = jnp.asarray(line_tables(pen_count))
    pairs = pltpu.SemaphoreType.DMA((devices,))
    potential, forces = pl.pallas_call(
        functools.partial(mesh_kernel, plane_count, pen_count, capacity, rows),
        out_shape=(
            pltpu.VMEM((rows, NG), jnp.float32),
            pltpu.VMEM((local_blocks, 2, block_len), jnp.float32),
        ),
        in_specs=[far] * 10,
        out_specs=(vmem, vmem),
        scratch_shapes=[
            pltpu.VMEM((devices, tall_back, LANES), jnp.float32),
            pltpu.VMEM((devices, tall_back, LANES), jnp.float32),
            pltpu.VMEM((devices, tall, LANES), jnp.float32),
            pltpu.VMEM((devices, tall + 8, LANES), jnp.float32),
            pltpu.VMEM((devices, 1, LANES), jnp.int32),
            pltpu.VMEM((devices, 1, LANES), jnp.int32),
            pltpu.SMEM((devices, 1, LANES), jnp.int32),
            pltpu.SMEM((devices,), jnp.int32),
            pltpu.SMEM((local_blocks,), jnp.int32),
            pltpu.VMEM((1, local_blocks), jnp.int32),
            pltpu.SMEM((local_blocks + 8,), jnp.int32),
            pltpu.SMEM((local_blocks + 8,), jnp.int32),
            pltpu.VMEM((local_blocks + 8, block_len), jnp.int32),
            pltpu.VMEM((local_blocks + 8, 2, block_len), jnp.float32),
            pltpu.VMEM((local_blocks + 8, block_len), jnp.float32),
            pltpu.VMEM((16, LANES), jnp.int32),
            pltpu.SMEM((16, LANES), jnp.int32),
            pltpu.VMEM((16, LANES), jnp.int32),
            pltpu.SMEM((16, LANES), jnp.int32),
            pltpu.VMEM((total + 1, CHUNKS * 8 + 16, LANES), jnp.float32),
            pltpu.VMEM((rows // 8, 16, NG), jnp.bfloat16),
            pltpu.VMEM((rows // 8, 16, 2 * LANES), jnp.bfloat16),
            pltpu.VMEM((CHUNKS, rows + 32, LANES), jnp.float32),
            pltpu.VMEM((rows + 16, NG), jnp.bfloat16),
            pltpu.VMEM((2 * rows + 32, NG), jnp.bfloat16),
            pltpu.VMEM((2 * CHUNKS * (rows + 16), LANES), jnp.float32),
            pltpu.VMEM((rows, NG), jnp.float32),
            pltpu.VMEM((3, 1, NG), jnp.float32),
            pltpu.VMEM((2, 1, NG), jnp.float32),
            pltpu.VMEM((1, 1, NG), jnp.float32),
            pltpu.VMEM((pen_count, 3, 1, NG), jnp.float32),
            pltpu.VMEM((2, 1, NG), jnp.float32),
            pltpu.VMEM((1, 1, NG), jnp.float32),
            pltpu.VMEM((NG, NG), jnp.bfloat16),
            pltpu.VMEM((NG, NG), jnp.bfloat16),
            pltpu.VMEM(lines.shape, jnp.float32),
            pltpu.SemaphoreType.DMA((13,)),
            pairs,
            pairs,
            pairs,
            pairs,
            pairs,
            pairs,
            pltpu.SemaphoreType.DMA((pen_count,)),
            pltpu.SemaphoreType.DMA((pen_count,)),
            pltpu.SemaphoreType.DMA((2,)),
            pltpu.SemaphoreType.DMA((2,)),
        ],
        compiler_params=pltpu.CompilerParams(
            collective_id=0, has_side_effects=True, vmem_limit_bytes=VMEM_LIMIT
        ),
        name="mesh",
    )(
        block_owner[:, 0],
        block_owner.reshape(1, local_blocks),
        block_band,
        block_count,
        cells,
        offsets,
        charges,
        table_high,
        table_along,
        lines,
    )
    potential = pltpu.with_memory_space_constraint(potential, pltpu.VMEM)
    forces = pltpu.with_memory_space_constraint(forces, pltpu.VMEM)
    potential, forces = pl.pallas_call(
        copy_kernel,
        out_shape=(
            jax.ShapeDtypeStruct(potential.shape, jnp.float32),
            jax.ShapeDtypeStruct(forces.shape, jnp.float32),
        ),
        in_specs=[pl.BlockSpec(memory_space=pl.ANY)] * 2,
        out_specs=(far, far),
        scratch_shapes=[pltpu.SemaphoreType.DMA((2,))],
        name="copy",
    )(potential, forces)
    return (potential[None], forces)


def solution(mesh):
    placed = (
        P(("pln", "pen"), None),
        P(("pln", "pen")),
        P(("pln", "pen")),
        P(("pln", "pen"), None),
        P(("pln", "pen"), None, None),
        P(("pln", "pen"), None),
    )
    return jax.shard_map(
        shards,
        mesh=mesh,
        in_specs=placed,
        out_specs=(P("pln", "pen", None), P(("pln", "pen"), None, None)),
        check_vma=False,
    )
```

```python
import functools
import math

import jax
import jax.numpy as jnp
import numpy as np
from jax import lax
from jax.experimental import pallas as pl
from jax.experimental.pallas import tpu as pltpu
from jax.sharding import PartitionSpec as P

NG = 1024
LANES = 128
CHUNKS = NG // LANES
screening = 2e-05
VMEM_LIMIT = 56 * 1024 * 1024
UNROLL = 8


def round_up(value, step):
    return -(-value // step) * step


@functools.lru_cache(None)
def hartley_tables():
    index = np.arange(NG)
    angle = 2.0 * np.pi / NG * (index[:, None] * index[None, :] % NG)
    table = np.cos(angle) + np.sin(angle)
    high = table.astype(jnp.bfloat16)
    low = (table - high.astype(np.float64)).astype(jnp.bfloat16)
    turn = 2.0 * np.pi / NG * np.arange(NG)
    slope = (2.0 * np.sin(2.0 * turn) - 16.0 * np.sin(turn)) / 12.0
    along = (slope[:, None] * (np.cos(angle) - np.sin(angle))).astype(jnp.bfloat16)
    return high, low, along


@functools.lru_cache(None)
def line_tables(pen_count):
    rows = NG // pen_count
    shift = 4.0 * np.sin(np.pi * np.arange(NG) / NG) ** 2 + screening
    root = 1.0 + shift / 2.0 - np.sqrt(shift + shift * shift / 4.0)
    i = np.arange(8)[:, None]

    def power(exponent):
        return root[None, :] ** (exponent + np.zeros((8, 1)))

    tiles = [
        power(7 - i),
        power(i),
        power(8),
        np.where(i >= 1, power(1), 0.0),
        np.where(i >= 2, power(2), 0.0),
        np.where(i >= 4, power(4), 0.0),
        np.where(i <= 6, power(1), 0.0),
        np.where(i <= 5, power(2), 0.0),
        np.where(i <= 3, power(4), 0.0),
        power(i + 1),
        power(8 - i),
        np.broadcast_to(1.0 / ((1.0 / root - root) * NG), (8, NG)),
        np.broadcast_to(2.0 + shift, (8, NG)),
        power(rows - 1),
    ]
    lags = np.arange(round_up(pen_count, 8))[:, None]
    tiles.append(root[None, :] ** (lags * rows) / (1.0 - root[None, :] ** NG))
    return np.concatenate(tiles, axis=0).astype(np.float32)


T_FEND, T_BEND, T_EIGHT, T_F1, T_F2, T_F4, T_B1, T_B2, T_B4, T_FC, T_BC, T_NORM, T_DIAG, T_LAST, T_LAG = range(15)


def fetch(sources, targets, sems):
    copies = [pltpu.make_async_copy(a, b, sems.at[i]) for i, (a, b) in enumerate(zip(sources, targets))]
    for copy in copies:
        copy.start()
    return copies


def list_blocks(capacity, owner, owner_row, tables):
    blocks = owner.shape[0]
    lane = lax.broadcasted_iota(jnp.int32, (8, LANES), 1)
    place = lax.broadcasted_iota(jnp.int32, (8, LANES), 0)
    owners = jnp.broadcast_to(owner_row[...], (8, LANES))
    unroll = 8

    def look(n, carry):
        block_at, used, rank = carry
        for k in range(unroll):
            i = n * unroll + k
            o = owner[i]
            named = lane == o
            block_at = jnp.where(named & (place == used), i, block_at)
            used = used + jnp.where(named, 1, 0)
            rank = rank + jnp.where((owners == o) & (lane > i), 1, 0)
        return block_at, used, rank

    nothing = jnp.zeros((8, LANES), jnp.int32)
    block_at, used, rank = lax.fori_loop(
        0, blocks // unroll, look, (jnp.full((8, LANES), blocks, jnp.int32), nothing, nothing)
    )
    tables[0:8] = block_at
    tables[8:16] = jnp.minimum(rank, capacity - 1)


def pack(s, other, capacity, tables, band, count, cells, offsets, charges, packed, heads_out):
    lane = lax.broadcasted_iota(jnp.int32, (1, LANES), 1)
    head = jnp.zeros((1, LANES), jnp.int32)
    rows = [[], [], [], []]
    for j in range(capacity):
        i = tables[j, other]
        pair = offsets[i]
        rows[0].append(pair[0:1])
        rows[1].append(pair[1:2])
        rows[2].append(jnp.where(lane < count[i], charges[pl.ds(i, 1), :], 0.0))
        rows[3].append(cells[pl.ds(i, 1), :].astype(jnp.float32))
        head = jnp.where(lane == j, band[i], head)
    for part in range(4):
        for j in range(capacity):
            packed[s, part * capacity + j : part * capacity + j + 1, :] = rows[part][j]
    heads_out[s] = head


def peer(index, pens):
    return (lax.div(index, pens), lax.rem(index, pens))


def exclusive(a, b, size):
    total = 0
    for bit in range(size.bit_length() - 1):
        p = lax.rem(lax.div(a, 1 << bit), 2)
        q = lax.rem(lax.div(b, 1 << bit), 2)
        total = total + (p + q - 2 * p * q) * (1 << bit)
    return total


def factors(frac_x, frac_y, weight, cell):
    cell = cell.astype(jnp.int32)
    column = cell & (NG - 1)
    after = (column + 1) & (NG - 1)
    row = cell >> (NG.bit_length() - 1)
    left = (1.0 - frac_x).astype(jnp.bfloat16).astype(jnp.float32)
    right = frac_x.astype(jnp.bfloat16).astype(jnp.float32)
    return frac_y, weight, row, column, after, left, right


def dot3(a_high, a_low, b_high, b_low):
    dot = functools.partial(jnp.dot, preferred_element_type=jnp.float32)
    return dot(a_high, b_high) + (dot(a_high, b_low) + dot(a_low, b_high))


def split(values):
    high = values.astype(jnp.bfloat16)
    return high, (values - high.astype(jnp.float32)).astype(jnp.bfloat16)


def doubled(values):
    return jnp.concatenate([values, values], axis=0).astype(jnp.bfloat16)


def iota16():
    return lax.broadcasted_iota(jnp.int32, (16, LANES), 0).astype(jnp.float32).astype(jnp.bfloat16)


def link_blocks(heads, links, capacity):
    count = heads.shape[0]
    total = count * capacity
    lane = lax.broadcasted_iota(jnp.int32, (8, LANES), 1)
    slot = lax.broadcasted_iota(jnp.int32, (8, LANES), 0) * LANES + lane

    def collect(s, bands):
        for j in range(capacity):
            bands = jnp.where(slot == s * capacity + j, heads[s, 0, j], bands)
        return bands

    bands = lax.fori_loop(0, count, collect, jnp.full((8, LANES), -1, jnp.int32), unroll=4)

    def link(s, carry):
        earlier, last = carry
        for j in range(capacity):
            here = s * capacity + j
            band = heads[s, 0, j]
            earlier = jnp.where((bands == band) & (slot > here), here, earlier)
            last = jnp.where(lane == band, here, last)
        return earlier, last

    nobody = jnp.full((8, LANES), total, jnp.int32)
    earlier, last = lax.fori_loop(0, count, link, (nobody, nobody), unroll=4)
    links[0:8] = earlier
    links[8:16] = last


def deposit(sources, capacity, recv, chain, links):
    sub8 = lax.broadcasted_iota(jnp.int32, (8, LANES), 0)
    sub16 = iota16()
    upper_half = jnp.where(sub16 < 8.0, 0.0, 1.0).astype(jnp.bfloat16)
    zero16 = jnp.zeros((16, LANES), jnp.bfloat16)

    def one(s, j):
        def spread(which):
            return recv[s, pl.ds(which * capacity + j, 8, stride=0), :]

        frac_y, weight, row, column, after, left, right = factors(spread(0), spread(1), spread(2), spread(3))
        lower = weight * (1.0 - frac_y)
        upper = weight * frac_y
        main = doubled(jnp.where(row == sub8, lower, jnp.where(row + 1 == sub8, upper, 0.0)))
        tail = doubled(jnp.where(row == 7, upper, 0.0))
        lhs, rhs = [], []
        for place, factor in ((column, left), (after, right)):
            chunk = doubled((place >> 7).astype(jnp.float32))
            index, factor = doubled((place & 127).astype(jnp.float32)), doubled(factor)
            tiles = [jnp.where(chunk == upper_half + float(2 * a), main, zero16) for a in range(CHUNKS // 2)]
            lhs.append(tiles + [jnp.where(chunk == sub16, tail, zero16)])
            rhs.append([jnp.where(index == sub16 + float(16 * b), factor, zero16) for b in range(LANES // 16)])
        lhs = [jnp.concatenate(both, axis=1) for both in zip(*lhs)]
        rhs = [jnp.concatenate(both, axis=1) for both in zip(*rhs)]
        values = lax.dot_general(
            jnp.concatenate(lhs, axis=0),
            jnp.concatenate(rhs, axis=0),
            (((1,), (1,)), ((), ())),
            preferred_element_type=jnp.float32,
        )
        return values[0 : CHUNKS * 8 + 8]

    places = [(s, j) for s in sources for j in range(capacity)]
    made = [one(s, j) for s, j in places]
    for (s, j), values in zip(places, made):
        slot = s * capacity + j
        earlier = links[lax.div(slot, LANES), lax.rem(slot, LANES)]
        chain[slot, 0 : CHUNKS * 8 + 8] = values + chain[earlier, 0 : CHUNKS * 8 + 8]


def assemble(bands, total, chain, links, hi, lo):
    first_row = lax.broadcasted_iota(jnp.int32, (8, LANES), 0) == 0

    def last_of(band):
        inside = (band >= 0) & (band < bands)
        return jnp.where(inside, links[8, jnp.clip(band, 0, bands - 1)], total)

    def rows_of(band):
        mine, above = last_of(band), last_of(band - 1)
        tiles = []
        for a in range(CHUNKS):
            extra = chain[above, pl.ds(CHUNKS * 8 + a, 8, stride=0)]
            tiles.append(chain[mine, a * 8 : a * 8 + 8] + jnp.where(first_row, extra, 0.0))
        return jnp.concatenate(tiles, axis=1)

    def pair(q, carry):
        high, low = split(jnp.concatenate([rows_of(2 * q), rows_of(2 * q + 1)], axis=0))
        at = pl.ds(pl.multiple_of(q * 16, 16), 16)
        hi[at, :] = high
        lo[at, :] = low
        return carry

    lax.fori_loop(0, bands // 2, pair, 0, unroll=4)
    pair(bands // 2, 0)


def transform(rows, hi, lo, table_high, table_low, lines, spectrum, sums, nexts, lasts):
    width = 256
    for n in range(NG // width):
        cols = slice(n * width, (n + 1) * width)
        values = dot3(hi[...], lo[...], table_high[:, cols], table_low[:, cols])
        spectrum[:, cols] = values[:rows]
        sums[2, 0:1, cols] = values[rows : rows + 1]
    eight = lines[T_EIGHT * 8 : T_EIGHT * 8 + 8]
    tiles = rows // 8

    def fold(t, carry):
        fwd, bwd = carry
        fwd = eight * fwd + spectrum[pl.ds(pl.multiple_of(t * 8, 8), 8), :]
        bwd = eight * bwd + spectrum[pl.ds(pl.multiple_of((tiles - 1 - t) * 8, 8), 8), :]
        return fwd, bwd

    nothing = jnp.zeros((8, NG), jnp.float32)
    fwd, bwd = lax.fori_loop(0, tiles, fold, (nothing, nothing), unroll=4)
    sums[0] = jnp.sum(fwd * lines[T_FEND * 8 : T_FEND * 8 + 8], axis=0, keepdims=True)
    sums[1] = jnp.sum(bwd * lines[T_BEND * 8 : T_BEND * 8 + 8], axis=0, keepdims=True)
    nexts[0] = spectrum[0:1]
    nexts[1] = spectrum[1:2]
    lasts[0] = spectrum[rows - 1 : rows]


def wave_tile(wave, row, height=8):
    return jnp.concatenate([wave[a, pl.ds(row, height), :] for a in range(CHUNKS)], axis=1)


def put_wave(wave, row, values):
    for a in range(CHUNKS):
        wave[a, pl.ds(row, values.shape[0]), :] = values[:, a * LANES : (a + 1) * LANES]


def local_scans(rows, spectrum, lines, wave):
    tiles = rows // 8

    def table(which):
        return lines[which * 8 : which * 8 + 8]

    def backward(i, carry):
        t = tiles - 1 - i
        where = pl.ds(pl.multiple_of(t * 8, 8), 8)
        x = spectrum[where, :]
        x = x + table(T_B1) * pltpu.roll(x, 7, 0)
        x = x + table(T_B2) * pltpu.roll(x, 6, 0)
        x = x + table(T_B4) * pltpu.roll(x, 4, 0)
        x = x + table(T_BC) * carry
        put_wave(wave, pl.multiple_of(t * 8 + 8, 8), x)
        return x[0:1]

    nothing = jnp.zeros((1, NG), jnp.float32)
    lax.fori_loop(0, tiles, backward, nothing)

    def forward(t, carry):
        where = pl.ds(pl.multiple_of(t * 8, 8), 8)
        d = spectrum[where, :]
        x = d + table(T_F1) * pltpu.roll(d, 1, 0)
        x = x + table(T_F2) * pltpu.roll(x, 2, 0)
        x = x + table(T_F4) * pltpu.roll(x, 4, 0)
        x = x + table(T_FC) * carry
        row = pl.multiple_of(t * 8 + 8, 8)
        put_wave(wave, row, x + wave_tile(wave, row) - d)
        return x[7:8]

    lax.fori_loop(0, tiles, forward, nothing)


def finish_solve(rows, mine, sums_of, nexts_of, lasts_of, lines, wave, stack):
    pens = sums_of.shape[0]
    tiles = rows // 8

    def table(which):
        return lines[which * 8 : which * 8 + 8]

    def row_of(pen, which):
        return sums_of[lax.rem(pen + 2 * pens, pens), which]

    last_power = table(T_LAST)[0:1]
    before = jnp.zeros((1, NG), jnp.float32)
    beyond = jnp.zeros((1, NG), jnp.float32)
    for j in range(pens):
        lag = lines[T_LAG * 8 + j : T_LAG * 8 + j + 1]
        behind, ahead = mine - 1 - j, mine + 1 + j
        before += lag * (row_of(behind, 0) + last_power * row_of(behind - 1, 2))
        beyond += lag * (row_of(ahead, 1) + row_of(ahead - 1, 2))
    incoming = row_of(mine - 1, 2)
    next_zero = nexts_of[0] + row_of(mine, 2)
    next_one = nexts_of[1]
    last_before = lasts_of[0]
    norm = table(T_NORM)[0:1]
    root = table(T_FC)[0:1]
    eight = table(T_EIGHT)
    ramp_down = norm * (root * before + incoming)
    ramp_up = norm * beyond
    first_back = row_of(mine, 1) + incoming + root * last_power * beyond
    final = row_of(mine, 0) + last_power * incoming + root * last_power * before

    def add_beyond(i, ramp):
        row = pl.multiple_of((tiles - 1 - i) * 8 + 8, 8)
        put_wave(wave, row, table(T_NORM) * wave_tile(wave, row) + ramp)
        return ramp * eight

    lax.fori_loop(0, tiles, add_beyond, table(T_BC) * ramp_up, unroll=4)

    def add_before(q, ramp):
        row = pl.multiple_of(q * 16 + 8, 8)
        then = ramp * eight
        values = wave_tile(wave, row, 16) + jnp.concatenate([ramp, then], axis=0)
        put_wave(wave, row, values)
        stack[pl.ds(pl.multiple_of(q * 16, 16), 16), :] = values.astype(jnp.bfloat16)
        return then * eight

    lax.fori_loop(0, tiles // 2, add_before, table(T_BEND) * ramp_down, unroll=4)
    diagonal = table(T_DIAG)[0:1]
    scale = 1.0 / NG
    up1 = norm * (before + root * first_back)
    up2 = diagonal * up1 - wave_tile(wave, 8, 1) - scale * last_before
    down0 = norm * (root * final + beyond)
    down1 = diagonal * down0 - wave_tile(wave, rows + 7, 1) - scale * next_zero
    down2 = diagonal * down1 - down0 - scale * next_one
    put_wave(wave, 0, jnp.concatenate([jnp.zeros((6, NG), jnp.float32), up2, up1], axis=0))
    below = jnp.concatenate([down0, down1, down2, jnp.zeros((21, NG), jnp.float32)], axis=0)
    put_wave(wave, rows + 8, below)
    stack[rows : rows + 16] = below[0:16].astype(jnp.bfloat16)

    def slope(q, carry):
        row = q * 16 + 8

        def at(shift):
            return wave_tile(wave, row + shift, 16)

        along_y = (8.0 * (at(1) - at(-1)) - (at(2) - at(-2))) * (-1.0 / 12.0)
        stack[pl.ds(pl.multiple_of(rows + 16 + q * 16, 16), 16), :] = along_y.astype(jnp.bfloat16)
        return carry

    lax.fori_loop(0, tiles // 2 + 1, slope, 0)


def invert(rows, stack, table_high, table_along, potential, forms, rim, field):
    width = 256
    tiles = rows // 8
    tall = rows + 16
    dot = functools.partial(jnp.dot, preferred_element_type=jnp.float32)
    for n in range(NG // width):
        cols = slice(n * width, (n + 1) * width)
        values = dot(stack[...], table_high[:, cols])
        potential[:, cols] = values[:rows]
        along = dot(stack[0:tall], table_along[:, cols])
        for k in range(width // LANES):
            a = n * (width // LANES) + k
            lanes = slice(k * LANES, (k + 1) * LANES)
            forms[a * tall : (a + 1) * tall] = along[:, lanes]
            forms[(CHUNKS + a) * tall : (CHUNKS + a + 1) * tall] = values[tall:, lanes]

    def gather_tile(t, carry):
        row = pl.multiple_of(t * 8, 8)
        for a in range(CHUNKS):
            both = [forms[pl.ds(pl.multiple_of((c * CHUNKS + a) * tall + row, 8), 8), :] for c in range(2)]
            field[t, :, a * LANES : (a + 1) * LANES] = jnp.concatenate(both, axis=0).astype(jnp.bfloat16)
        ends = [forms[pl.ds(c * CHUNKS * tall + row + 8, CHUNKS, stride=tall), :] for c in range(2)]
        rim[t, :, 0:LANES] = jnp.concatenate(ends, axis=0).astype(jnp.bfloat16)
        ends = [pltpu.roll(e, CHUNKS - 1, 0) for e in ends]
        rim[t, :, LANES : 2 * LANES] = jnp.concatenate(ends, axis=0).astype(jnp.bfloat16)
        return carry

    lax.fori_loop(0, tiles, gather_tile, 0, unroll=4)


def mesh_kernel(planes, pens, capacity, rows, owner_h, owner_row_h, band_h, count_h, cells_h, offsets_h, charges_h,
                table_high_h, table_low_h, table_along_h, lines_h, potential, out, forces, returned, packed, recv, heads_out, heads,
                heads_s, ids, owner, owner_row, band, block_count, cells, offsets, charges, tables_v, tables, links_v,
                links, chain, field, rim, wave, hi, lo, stack, forms, spectrum, sums, nexts, lasts, sums_of,
                nexts_of, lasts_of, table_high, table_low, table_along, lines, sems,
                send_sems, recv_sems, head_send_sems, head_recv_sems, back_send_sems, back_recv_sems, edge_send_sems,
                edge_recv_sems, side_send_sems, side_recv_sems):
    count = planes * pens
    total = count * capacity
    tall = 4 * capacity
    blocks = owner.shape[0]
    plane = lax.axis_index("pln")
    mine = lax.axis_index("pen")
    me = plane * pens + mine
    barrier = pltpu.get_barrier_semaphore()
    copies = fetch(
        (owner_h, owner_row_h, band_h, count_h, cells_h, offsets_h, charges_h, lines_h, table_high_h, table_low_h,
         table_along_h),
        (owner, owner_row, band.at[0:blocks], block_count.at[0:blocks], cells.at[0:blocks], offsets.at[0:blocks],
         charges.at[0:blocks], lines, table_high, table_low, table_along),
        sems,
    )

    def greet(k, carry):
        other = peer(lax.rem(me + k, count), pens)
        pl.semaphore_signal(barrier, inc=1, device_id=other, device_id_type=pl.DeviceIdType.MESH)
        return carry

    def note(s, carry):
        column = exclusive(plane, lax.rem(s, planes), planes)
        ids[s] = column * pens + exclusive(mine, lax.div(s, planes), pens)
        return carry

    lax.fori_loop(1, count, greet, 0, unroll=8)
    lax.fori_loop(0, count, note, 0, unroll=4)
    copies[0].wait()
    copies[1].wait()
    list_blocks(capacity, owner, owner_row, tables_v)
    tables_copy = pltpu.make_async_copy(tables_v, tables, sems.at[11])
    tables_copy.start()
    cells[blocks : blocks + 8] = jnp.zeros((8, LANES), jnp.int32)
    charges[blocks : blocks + 8] = jnp.zeros((8, LANES), jnp.float32)
    offsets[blocks] = jnp.zeros((2, LANES), jnp.float32)
    for copy in copies[2:7]:
        copy.wait()
    band[blocks] = 0
    block_count[blocks] = 0
    tables_copy.wait()

    def fill(s, carry):
        pack(s, ids[s], capacity, tables, band, block_count, cells, offsets, charges, packed, heads_out)
        return carry

    lax.fori_loop(0, count, fill, 0, unroll=4)
    recv[0, 0:tall] = packed[0]
    heads[0] = heads_out[0]
    chain[total] = jnp.zeros(chain.shape[1:], jnp.float32)
    pl.semaphore_wait(barrier, count - 1)

    def remote(s, source, place, send, receive):
        return pltpu.make_async_remote_copy(
            src_ref=source,
            dst_ref=place,
            send_sem=send.at[s],
            recv_sem=receive.at[s],
            device_id=peer(ids[s], pens),
            device_id_type=pl.DeviceIdType.MESH,
        )

    def head_copy(s):
        return remote(s, heads_out.at[s], heads.at[s], head_send_sems, head_recv_sems)

    def block_copy(s):
        return remote(s, packed.at[s], recv.at[s, 0:tall], send_sems, recv_sems)

    def back_copy(s):
        return remote(s, forces.at[s], returned.at[me], back_send_sems, back_recv_sems)

    def send_heads(s, carry):
        head_copy(s).start()
        return carry

    def send_blocks(s, carry):
        block_copy(s).start()
        return carry

    def take_heads(s, carry):
        head_copy(s).wait_recv()
        return carry

    lax.fori_loop(1, count, send_heads, 0)
    lax.fori_loop(1, count, send_blocks, 0)
    lax.fori_loop(1, count, take_heads, 0)
    heads_copy = pltpu.make_async_copy(heads, heads_s, sems.at[11])
    heads_copy.start()
    heads_copy.wait()
    link_blocks(heads_s, links_v, capacity)
    links_copy = pltpu.make_async_copy(links_v, links, sems.at[11])
    links_copy.start()
    links_copy.wait()

    bunch = 4

    def receive(i, carry):
        sources = [i * bunch + k for k in range(bunch)]
        for s in sources:
            @pl.when(s > 0)
            def _():
                block_copy(s).wait_recv()

        deposit(sources, capacity, recv, chain, links)
        return carry

    lax.fori_loop(0, count // bunch, receive, 0)
    assemble(rows // 8, total, chain, links, hi, lo)
    for copy in copies[7:]:
        copy.wait()
    transform(rows, hi, lo, table_high, table_low, lines, spectrum, sums, nexts, lasts)
    sums_of[mine] = sums[...]

    def edge_copy(k, place, other):
        return pltpu.make_async_remote_copy(
            src_ref=sums,
            dst_ref=sums_of.at[place],
            send_sem=edge_send_sems.at[k],
            recv_sem=edge_recv_sems.at[k],
            device_id=(plane, other),
            device_id_type=pl.DeviceIdType.MESH,
        )

    def side_copy(n, source, place, other):
        return pltpu.make_async_remote_copy(
            src_ref=source,
            dst_ref=place,
            send_sem=side_send_sems.at[n],
            recv_sem=side_recv_sems.at[n],
            device_id=(plane, other),
            device_id_type=pl.DeviceIdType.MESH,
        )

    up_copy = side_copy(0, nexts, nexts_of, lax.rem(mine + pens - 1, pens))
    down_copy = side_copy(1, lasts, lasts_of, lax.rem(mine + 1, pens))
    for k in range(1, pens):
        edge_copy(k, mine, lax.rem(mine + k, pens)).start()
    up_copy.start()
    down_copy.start()
    local_scans(rows, spectrum, lines, wave)
    for k in range(1, pens):
        behind = lax.rem(mine - k + pens, pens)
        edge_copy(k, mine, lax.rem(mine + k, pens)).wait_send()
        edge_copy(k, behind, behind).wait_recv()
    up_copy.wait()
    down_copy.wait()
    finish_solve(rows, mine, sums_of, nexts_of, lasts_of, lines, wave, stack)
    invert(rows, stack, table_high, table_along, potential, forms, rim, field)
    sub8 = lax.broadcasted_iota(jnp.int32, (8, LANES), 0)
    sub16 = iota16()
    zero16 = jnp.zeros((16, LANES), jnp.bfloat16)

    def one(d, j):
        def spread(which):
            return recv[d, pl.ds(which * capacity + j, 8, stride=0), :]

        band = heads_s[d, 0, j]
        frac_y, weight, row, column, after, left, right = factors(
            spread(0), spread(1), spread(2), spread(3)
        )
        chunk = column >> 7
        index = (column & 127).astype(jnp.float32)
        spot, left16, right16 = doubled(index), doubled(left), doubled(right)
        next_spot = doubled(index + 1.0)
        picks = []
        for b in range(LANES // 16 + 1):
            here = sub16 + float(16 * b)
            picks.append(jnp.where(here == spot, left16, jnp.where(here == next_spot, right16, zero16)))
        picks += [zero16] * (2 * LANES // 16 - len(picks))
        rows_of = field[band]
        windows = [
            jnp.concatenate(
                [
                    rows_of[:, a * LANES : (a + 1) * LANES],
                    rows_of[:, (a + 1) % CHUNKS * LANES : ((a + 1) % CHUNKS + 1) * LANES],
                ],
                axis=1,
            )
            for a in range(CHUNKS)
        ]
        values = jnp.dot(
            jnp.concatenate(windows + [rim[band]], axis=0),
            jnp.concatenate(picks, axis=0),
            preferred_element_type=jnp.float32,
        )
        row_weight = weight * jnp.where(row == sub8, 1.0 - frac_y, jnp.where(row + 1 == sub8, frac_y, 0.0))
        mixed = [values[0:8], values[8:16]]
        for a in range(1, CHUNKS):
            held = chunk == a
            mixed = [jnp.where(held, values[a * 16 + c * 8 : a * 16 + c * 8 + 8], mixed[c]) for c in range(2)]
        edge = weight * jnp.where(row == 7, frac_y, 0.0)
        at_edge = sub8 == chunk
        rims = [jnp.where(at_edge, values[CHUNKS * 16 + c * 8 : CHUNKS * 16 + c * 8 + 8], 0.0) for c in range(2)]
        return [jnp.sum(row_weight * mixed[c] + edge * rims[c], axis=0, keepdims=True) for c in range(2)]

    def pull(sources):
        made = [[one(d, j) for j in range(capacity)] for d in sources]
        for d, results in zip(sources, made):
            keep(d, results)

    def keep(d, made):
        for c in range(2):
            for j in range(capacity):
                forces[d, c * capacity + j : c * capacity + j + 1, :] = made[j][c]
        if forces.shape[1] > 2 * capacity:
            forces[d, 2 * capacity :, :] = jnp.zeros((forces.shape[1] - 2 * capacity, LANES), jnp.float32)

    group = 4

    def step(i, carry):
        sources = [count - 1 - i * group - k for k in range(group)]
        pull(sources)
        for s in sources:
            back_copy(s).start()
        return carry

    lax.fori_loop(0, count // group - 1, step, 0)
    pull(list(range(group)))
    for s in range(1, group):
        back_copy(s).start()
    returned[me] = forces[0]

    def finish(i, carry):
        s = count - i
        head_copy(s).wait_send()
        block_copy(s).wait_send()
        back_copy(s).wait_send()
        back_copy(s).wait_recv()
        return carry

    lax.fori_loop(1, count, finish, 0)

    def take(n, carry):
        for k in range(8):
            i = n * 8 + k
            d, j = owner[i], tables[8, i]
            out[i, 0:1, :] = returned[d, pl.ds(j, 1), :]
            out[i, 1:2, :] = returned[d, pl.ds(capacity + j, 1), :]
        return carry

    lax.fori_loop(0, blocks // 8, take, 0, unroll=2)


def copy_kernel(potential_v, forces_v, potential, forces, sems):
    copies = fetch((potential_v, forces_v), (potential, forces), sems)
    for copy in copies:
        copy.wait()


def shards(block_owner, block_band, block_count, cells, offsets, charges):
    plane_count = lax.axis_size("pln")
    pen_count = lax.axis_size("pen")
    devices = plane_count * pen_count
    local_blocks, block_len = charges.shape
    capacity = max(2, 2 * local_blocks // devices)
    total = devices * capacity
    rows = NG // pen_count
    tall = 4 * capacity
    tall_back = round_up(2 * capacity, 8)
    vmem = pl.BlockSpec(memory_space=pltpu.VMEM)
    far = pl.BlockSpec(memory_space=pltpu.HBM)
    table_high, table_low, table_along = (jnp.asarray(t) for t in hartley_tables())
    lines = jnp.asarray(line_tables(pen_count))
    pairs = pltpu.SemaphoreType.DMA((devices,))
    potential, forces = pl.pallas_call(
        functools.partial(mesh_kernel, plane_count, pen_count, capacity, rows),
        out_shape=(
            pltpu.VMEM((rows, NG), jnp.float32),
            pltpu.VMEM((local_blocks, 2, block_len), jnp.float32),
        ),
        in_specs=[far] * 11,
        out_specs=(vmem, vmem),
        scratch_shapes=[
            pltpu.VMEM((devices, tall_back, LANES), jnp.float32),
            pltpu.VMEM((devices, tall_back, LANES), jnp.float32),
            pltpu.VMEM((devices, tall, LANES), jnp.float32),
            pltpu.VMEM((devices, tall + 8, LANES), jnp.float32),
            pltpu.VMEM((devices, 1, LANES), jnp.int32),
            pltpu.VMEM((devices, 1, LANES), jnp.int32),
            pltpu.SMEM((devices, 1, LANES), jnp.int32),
            pltpu.SMEM((devices,), jnp.int32),
            pltpu.SMEM((local_blocks,), jnp.int32),
            pltpu.VMEM((1, local_blocks), jnp.int32),
            pltpu.SMEM((local_blocks + 8,), jnp.int32),
            pltpu.SMEM((local_blocks + 8,), jnp.int32),
            pltpu.VMEM((local_blocks + 8, block_len), jnp.int32),
            pltpu.VMEM((local_blocks + 8, 2, block_len), jnp.float32),
            pltpu.VMEM((local_blocks + 8, block_len), jnp.float32),
            pltpu.VMEM((16, LANES), jnp.int32),
            pltpu.SMEM((16, LANES), jnp.int32),
            pltpu.VMEM((16, LANES), jnp.int32),
            pltpu.SMEM((16, LANES), jnp.int32),
            pltpu.VMEM((total + 1, CHUNKS * 8 + 16, LANES), jnp.float32),
            pltpu.VMEM((rows // 8, 16, NG), jnp.bfloat16),
            pltpu.VMEM((rows // 8, 16, 2 * LANES), jnp.bfloat16),
            pltpu.VMEM((CHUNKS, rows + 32, LANES), jnp.float32),
            pltpu.VMEM((rows + 16, NG), jnp.bfloat16),
            pltpu.VMEM((rows + 16, NG), jnp.bfloat16),
            pltpu.VMEM((2 * rows + 32, NG), jnp.bfloat16),
            pltpu.VMEM((2 * CHUNKS * (rows + 16), LANES), jnp.float32),
            pltpu.VMEM((rows, NG), jnp.float32),
            pltpu.VMEM((3, 1, NG), jnp.float32),
            pltpu.VMEM((2, 1, NG), jnp.float32),
            pltpu.VMEM((1, 1, NG), jnp.float32),
            pltpu.VMEM((pen_count, 3, 1, NG), jnp.float32),
            pltpu.VMEM((2, 1, NG), jnp.float32),
            pltpu.VMEM((1, 1, NG), jnp.float32),
            pltpu.VMEM((NG, NG), jnp.bfloat16),
            pltpu.VMEM((NG, NG), jnp.bfloat16),
            pltpu.VMEM((NG, NG), jnp.bfloat16),
            pltpu.VMEM(lines.shape, jnp.float32),
            pltpu.SemaphoreType.DMA((13,)),
            pairs,
            pairs,
            pairs,
            pairs,
            pairs,
            pairs,
            pltpu.SemaphoreType.DMA((pen_count,)),
            pltpu.SemaphoreType.DMA((pen_count,)),
            pltpu.SemaphoreType.DMA((2,)),
            pltpu.SemaphoreType.DMA((2,)),
        ],
        compiler_params=pltpu.CompilerParams(
            collective_id=0, has_side_effects=True, vmem_limit_bytes=VMEM_LIMIT
        ),
        name="mesh",
    )(
        block_owner[:, 0],
        block_owner.reshape(1, local_blocks),
        block_band,
        block_count,
        cells,
        offsets,
        charges,
        table_high,
        table_low,
        table_along,
        lines,
    )
    potential = pltpu.with_memory_space_constraint(potential, pltpu.VMEM)
    forces = pltpu.with_memory_space_constraint(forces, pltpu.VMEM)
    potential, forces = pl.pallas_call(
        copy_kernel,
        out_shape=(
            jax.ShapeDtypeStruct(potential.shape, jnp.float32),
            jax.ShapeDtypeStruct(forces.shape, jnp.float32),
        ),
        in_specs=[pl.BlockSpec(memory_space=pl.ANY)] * 2,
        out_specs=(far, far),
        scratch_shapes=[pltpu.SemaphoreType.DMA((2,))],
        name="copy",
    )(potential, forces)
    return (potential[None], forces)


def solution(mesh):
    placed = (
        P(("pln", "pen"), None),
        P(("pln", "pen")),
        P(("pln", "pen")),
        P(("pln", "pen"), None),
        P(("pln", "pen"), None, None),
        P(("pln", "pen"), None),
    )
    return jax.shard_map(
        shards,
        mesh=mesh,
        in_specs=placed,
        out_specs=(P("pln", "pen", None), P(("pln", "pen"), None, None)),
        check_vma=False,
    )
```

```python
import functools
import math

import jax
import jax.numpy as jnp
import numpy as np
from jax import lax
from jax.experimental import pallas as pl
from jax.experimental.pallas import tpu as pltpu
from jax.sharding import PartitionSpec as P

NG = 1024
LANES = 128
CHUNKS = NG // LANES
screening = 2e-05
VMEM_LIMIT = 56 * 1024 * 1024
UNROLL = 8


def round_up(value, step):
    return -(-value // step) * step


@functools.lru_cache(None)
def hartley_tables():
    index = np.arange(NG)
    angle = 2.0 * np.pi / NG * (index[:, None] * index[None, :] % NG)
    table = np.cos(angle) + np.sin(angle)
    high = table.astype(jnp.bfloat16)
    low = (table - high.astype(np.float64)).astype(jnp.bfloat16)
    turn = 2.0 * np.pi / NG * np.arange(NG)
    slope = (2.0 * np.sin(2.0 * turn) - 16.0 * np.sin(turn)) / 12.0
    along = (slope[:, None] * (np.cos(angle) - np.sin(angle))).astype(jnp.bfloat16)
    return high, low, along


@functools.lru_cache(None)
def line_tables(pen_count):
    rows = NG // pen_count
    shift = 4.0 * np.sin(np.pi * np.arange(NG) / NG) ** 2 + screening
    root = 1.0 + shift / 2.0 - np.sqrt(shift + shift * shift / 4.0)
    i = np.arange(8)[:, None]

    def power(exponent):
        return root[None, :] ** (exponent + np.zeros((8, 1)))

    tiles = [
        power(7 - i),
        power(i),
        power(8),
        np.where(i >= 1, power(1), 0.0),
        np.where(i >= 2, power(2), 0.0),
        np.where(i >= 4, power(4), 0.0),
        np.where(i <= 6, power(1), 0.0),
        np.where(i <= 5, power(2), 0.0),
        np.where(i <= 3, power(4), 0.0),
        power(i + 1),
        power(8 - i),
        np.broadcast_to(1.0 / ((1.0 / root - root) * NG), (8, NG)),
        np.broadcast_to(2.0 + shift, (8, NG)),
        power(rows - 1),
    ]
    lags = np.arange(round_up(pen_count, 8))[:, None]
    tiles.append(root[None, :] ** (lags * rows) / (1.0 - root[None, :] ** NG))
    return np.concatenate(tiles, axis=0).astype(np.float32)


T_FEND, T_BEND, T_EIGHT, T_F1, T_F2, T_F4, T_B1, T_B2, T_B4, T_FC, T_BC, T_NORM, T_DIAG, T_LAST, T_LAG = range(15)


def fetch(sources, targets, sems):
    copies = [pltpu.make_async_copy(a, b, sems.at[i]) for i, (a, b) in enumerate(zip(sources, targets))]
    for copy in copies:
        copy.start()
    return copies


def list_blocks(capacity, owner, owner_row, tables):
    blocks = owner.shape[0]
    lane = lax.broadcasted_iota(jnp.int32, (8, LANES), 1)
    place = lax.broadcasted_iota(jnp.int32, (8, LANES), 0)
    owners = jnp.broadcast_to(owner_row[...], (8, LANES))
    unroll = 8

    def look(n, carry):
        block_at, used, rank = carry
        for k in range(unroll):
            i = n * unroll + k
            o = owner[i]
            named = lane == o
            block_at = jnp.where(named & (place == used), i, block_at)
            used = used + jnp.where(named, 1, 0)
            rank = rank + jnp.where((owners == o) & (lane > i), 1, 0)
        return block_at, used, rank

    nothing = jnp.zeros((8, LANES), jnp.int32)
    block_at, used, rank = lax.fori_loop(
        0, blocks // unroll, look, (jnp.full((8, LANES), blocks, jnp.int32), nothing, nothing)
    )
    tables[0:8] = block_at
    tables[8:16] = jnp.minimum(rank, capacity - 1)


def pack(s, other, capacity, tables, band, count, cells, offsets, charges, packed, heads_out):
    lane = lax.broadcasted_iota(jnp.int32, (1, LANES), 1)
    head = jnp.zeros((1, LANES), jnp.int32)
    rows = [[], [], [], []]
    for j in range(capacity):
        i = tables[j, other]
        pair = offsets[i]
        rows[0].append(pair[0:1])
        rows[1].append(pair[1:2])
        rows[2].append(jnp.where(lane < count[i], charges[pl.ds(i, 1), :], 0.0))
        rows[3].append(cells[pl.ds(i, 1), :].astype(jnp.float32))
        head = jnp.where(lane == j, band[i], head)
    for part in range(4):
        for j in range(capacity):
            packed[s, part * capacity + j : part * capacity + j + 1, :] = rows[part][j]
    heads_out[s] = head


def peer(index, pens):
    return (lax.div(index, pens), lax.rem(index, pens))


def exclusive(a, b, size):
    total = 0
    for bit in range(size.bit_length() - 1):
        p = lax.rem(lax.div(a, 1 << bit), 2)
        q = lax.rem(lax.div(b, 1 << bit), 2)
        total = total + (p + q - 2 * p * q) * (1 << bit)
    return total


def factors(frac_x, frac_y, weight, cell):
    cell = cell.astype(jnp.int32)
    column = cell & (NG - 1)
    after = (column + 1) & (NG - 1)
    row = cell >> (NG.bit_length() - 1)
    left = (1.0 - frac_x).astype(jnp.bfloat16).astype(jnp.float32)
    right = frac_x.astype(jnp.bfloat16).astype(jnp.float32)
    return frac_y, weight, row, column, after, left, right


def dot3(a_high, a_low, b_high, b_low):
    dot = functools.partial(jnp.dot, preferred_element_type=jnp.float32)
    return dot(a_high, b_high) + (dot(a_high, b_low) + dot(a_low, b_high))


def split(values):
    high = values.astype(jnp.bfloat16)
    return high, (values - high.astype(jnp.float32)).astype(jnp.bfloat16)


def doubled(values):
    return jnp.concatenate([values, values], axis=0).astype(jnp.bfloat16)


def iota16():
    return lax.broadcasted_iota(jnp.int32, (16, LANES), 0).astype(jnp.float32).astype(jnp.bfloat16)


def link_blocks(heads, links, capacity):
    count = heads.shape[0]
    total = count * capacity
    lane = lax.broadcasted_iota(jnp.int32, (8, LANES), 1)
    slot = lax.broadcasted_iota(jnp.int32, (8, LANES), 0) * LANES + lane

    def collect(s, bands):
        for j in range(capacity):
            bands = jnp.where(slot == s * capacity + j, heads[s, 0, j], bands)
        return bands

    bands = lax.fori_loop(0, count, collect, jnp.full((8, LANES), -1, jnp.int32), unroll=4)

    def link(s, carry):
        earlier, last = carry
        for j in range(capacity):
            here = s * capacity + j
            band = heads[s, 0, j]
            earlier = jnp.where((bands == band) & (slot > here), here, earlier)
            last = jnp.where(lane == band, here, last)
        return earlier, last

    nobody = jnp.full((8, LANES), total, jnp.int32)
    earlier, last = lax.fori_loop(0, count, link, (nobody, nobody), unroll=4)
    links[0:8] = earlier
    links[8:16] = last


def deposit(sources, capacity, recv, chain, links):
    sub8 = lax.broadcasted_iota(jnp.int32, (8, LANES), 0)
    sub16 = iota16()
    upper_half = jnp.where(sub16 < 8.0, 0.0, 1.0).astype(jnp.bfloat16)
    zero16 = jnp.zeros((16, LANES), jnp.bfloat16)

    def one(s, j):
        def spread(which):
            return recv[s, pl.ds(which * capacity + j, 8, stride=0), :]

        frac_y, weight, row, column, after, left, right = factors(spread(0), spread(1), spread(2), spread(3))
        lower = weight * (1.0 - frac_y)
        upper = weight * frac_y
        main = doubled(jnp.where(row == sub8, lower, jnp.where(row + 1 == sub8, upper, 0.0)))
        tail = doubled(jnp.where(row == 7, upper, 0.0))
        lhs, rhs = [], []
        for place, factor in ((column, left), (after, right)):
            chunk = doubled((place >> 7).astype(jnp.float32))
            index, factor = doubled((place & 127).astype(jnp.float32)), doubled(factor)
            tiles = [jnp.where(chunk == upper_half + float(2 * a), main, zero16) for a in range(CHUNKS // 2)]
            lhs.append(tiles + [jnp.where(chunk == sub16, tail, zero16)])
            rhs.append([jnp.where(index == sub16 + float(16 * b), factor, zero16) for b in range(LANES // 16)])
        lhs = [jnp.concatenate(both, axis=1) for both in zip(*lhs)]
        rhs = [jnp.concatenate(both, axis=1) for both in zip(*rhs)]
        values = lax.dot_general(
            jnp.concatenate(lhs, axis=0),
            jnp.concatenate(rhs, axis=0),
            (((1,), (1,)), ((), ())),
            preferred_element_type=jnp.float32,
        )
        return values[0 : CHUNKS * 8 + 8]

    places = [(s, j) for s in sources for j in range(capacity)]
    made = [one(s, j) for s, j in places]
    for (s, j), values in zip(places, made):
        slot = s * capacity + j
        earlier = links[lax.div(slot, LANES), lax.rem(slot, LANES)]
        chain[slot, 0 : CHUNKS * 8 + 8] = values + chain[earlier, 0 : CHUNKS * 8 + 8]


def assemble(bands, total, chain, links, hi, lo):
    first_row = lax.broadcasted_iota(jnp.int32, (8, LANES), 0) == 0

    def last_of(band):
        inside = (band >= 0) & (band < bands)
        return jnp.where(inside, links[8, jnp.clip(band, 0, bands - 1)], total)

    def rows_of(band):
        mine, above = last_of(band), last_of(band - 1)
        tiles = []
        for a in range(CHUNKS):
            extra = chain[above, pl.ds(CHUNKS * 8 + a, 8, stride=0)]
            tiles.append(chain[mine, a * 8 : a * 8 + 8] + jnp.where(first_row, extra, 0.0))
        return jnp.concatenate(tiles, axis=1)

    def pair(q, carry):
        high, low = split(jnp.concatenate([rows_of(2 * q), rows_of(2 * q + 1)], axis=0))
        at = pl.ds(pl.multiple_of(q * 16, 16), 16)
        hi[at, :] = high
        lo[at, :] = low
        return carry

    lax.fori_loop(0, bands // 2, pair, 0, unroll=4)
    pair(bands // 2, 0)


def transform(rows, hi, lo, table_high, table_low, lines, spectrum, sums, nexts, lasts):
    width = 256
    for n in range(NG // width):
        cols = slice(n * width, (n + 1) * width)
        values = dot3(hi[...], lo[...], table_high[:, cols], table_low[:, cols])
        spectrum[:, cols] = values[:rows]
        sums[2, 0:1, cols] = values[rows : rows + 1]
    eight = lines[T_EIGHT * 8 : T_EIGHT * 8 + 8]
    tiles = rows // 8

    def fold(t, carry):
        fwd, bwd = carry
        fwd = eight * fwd + spectrum[pl.ds(pl.multiple_of(t * 8, 8), 8), :]
        bwd = eight * bwd + spectrum[pl.ds(pl.multiple_of((tiles - 1 - t) * 8, 8), 8), :]
        return fwd, bwd

    nothing = jnp.zeros((8, NG), jnp.float32)
    fwd, bwd = lax.fori_loop(0, tiles, fold, (nothing, nothing), unroll=4)
    sums[0] = jnp.sum(fwd * lines[T_FEND * 8 : T_FEND * 8 + 8], axis=0, keepdims=True)
    sums[1] = jnp.sum(bwd * lines[T_BEND * 8 : T_BEND * 8 + 8], axis=0, keepdims=True)
    nexts[0] = spectrum[0:1]
    nexts[1] = spectrum[1:2]
    lasts[0] = spectrum[rows - 1 : rows]


def wave_tile(wave, row, height=8):
    return jnp.concatenate([wave[a, pl.ds(row, height), :] for a in range(CHUNKS)], axis=1)


def put_wave(wave, row, values):
    for a in range(CHUNKS):
        wave[a, pl.ds(row, values.shape[0]), :] = values[:, a * LANES : (a + 1) * LANES]


def local_scans(rows, spectrum, lines, wave):
    tiles = rows // 8

    def table(which):
        return lines[which * 8 : which * 8 + 8]

    def backward(i, carry):
        t = tiles - 1 - i
        where = pl.ds(pl.multiple_of(t * 8, 8), 8)
        x = spectrum[where, :]
        x = x + table(T_B1) * pltpu.roll(x, 7, 0)
        x = x + table(T_B2) * pltpu.roll(x, 6, 0)
        x = x + table(T_B4) * pltpu.roll(x, 4, 0)
        x = x + table(T_BC) * carry
        put_wave(wave, pl.multiple_of(t * 8 + 8, 8), x)
        return x[0:1]

    nothing = jnp.zeros((1, NG), jnp.float32)
    lax.fori_loop(0, tiles, backward, nothing)

    def forward(t, carry):
        where = pl.ds(pl.multiple_of(t * 8, 8), 8)
        d = spectrum[where, :]
        x = d + table(T_F1) * pltpu.roll(d, 1, 0)
        x = x + table(T_F2) * pltpu.roll(x, 2, 0)
        x = x + table(T_F4) * pltpu.roll(x, 4, 0)
        x = x + table(T_FC) * carry
        row = pl.multiple_of(t * 8 + 8, 8)
        put_wave(wave, row, x + wave_tile(wave, row) - d)
        return x[7:8]

    lax.fori_loop(0, tiles, forward, nothing)


def finish_solve(rows, mine, sums_of, nexts_of, lasts_of, lines, wave, stack):
    pens = sums_of.shape[0]
    tiles = rows // 8

    def table(which):
        return lines[which * 8 : which * 8 + 8]

    def row_of(pen, which):
        return sums_of[lax.rem(pen + 2 * pens, pens), which]

    last_power = table(T_LAST)[0:1]
    before = jnp.zeros((1, NG), jnp.float32)
    beyond = jnp.zeros((1, NG), jnp.float32)
    for j in range(pens):
        lag = lines[T_LAG * 8 + j : T_LAG * 8 + j + 1]
        behind, ahead = mine - 1 - j, mine + 1 + j
        before += lag * (row_of(behind, 0) + last_power * row_of(behind - 1, 2))
        beyond += lag * (row_of(ahead, 1) + row_of(ahead - 1, 2))
    incoming = row_of(mine - 1, 2)
    next_zero = nexts_of[0] + row_of(mine, 2)
    next_one = nexts_of[1]
    last_before = lasts_of[0]
    norm = table(T_NORM)[0:1]
    root = table(T_FC)[0:1]
    eight = table(T_EIGHT)
    ramp_down = norm * (root * before + incoming)
    ramp_up = norm * beyond
    first_back = row_of(mine, 1) + incoming + root * last_power * beyond
    final = row_of(mine, 0) + last_power * incoming + root * last_power * before

    def add_beyond(i, ramp):
        row = pl.multiple_of((tiles - 1 - i) * 8 + 8, 8)
        put_wave(wave, row, table(T_NORM) * wave_tile(wave, row) + ramp)
        return ramp * eight

    lax.fori_loop(0, tiles, add_beyond, table(T_BC) * ramp_up, unroll=4)

    def add_before(q, ramp):
        row = pl.multiple_of(q * 16 + 8, 8)
        then = ramp * eight
        values = wave_tile(wave, row, 16) + jnp.concatenate([ramp, then], axis=0)
        put_wave(wave, row, values)
        stack[pl.ds(pl.multiple_of(q * 16, 16), 16), :] = values.astype(jnp.bfloat16)
        return then * eight

    lax.fori_loop(0, tiles // 2, add_before, table(T_BEND) * ramp_down, unroll=4)
    diagonal = table(T_DIAG)[0:1]
    scale = 1.0 / NG
    up1 = norm * (before + root * first_back)
    up2 = diagonal * up1 - wave_tile(wave, 8, 1) - scale * last_before
    down0 = norm * (root * final + beyond)
    down1 = diagonal * down0 - wave_tile(wave, rows + 7, 1) - scale * next_zero
    down2 = diagonal * down1 - down0 - scale * next_one
    put_wave(wave, 0, jnp.concatenate([jnp.zeros((6, NG), jnp.float32), up2, up1], axis=0))
    below = jnp.concatenate([down0, down1, down2, jnp.zeros((21, NG), jnp.float32)], axis=0)
    put_wave(wave, rows + 8, below)
    stack[rows : rows + 16] = below[0:16].astype(jnp.bfloat16)

    def slope(q, carry):
        row = q * 16 + 8

        def at(shift):
            return wave_tile(wave, row + shift, 16)

        along_y = (8.0 * (at(1) - at(-1)) - (at(2) - at(-2))) * (-1.0 / 12.0)
        stack[pl.ds(pl.multiple_of(rows + 16 + q * 16, 16), 16), :] = along_y.astype(jnp.bfloat16)
        return carry

    lax.fori_loop(0, tiles // 2 + 1, slope, 0)


def invert(rows, stack, table_high, table_along, potential, forms, rim, field):
    width = 256
    tiles = rows // 8
    tall = rows + 16
    dot = functools.partial(jnp.dot, preferred_element_type=jnp.float32)
    for n in range(NG // width):
        cols = slice(n * width, (n + 1) * width)
        values = dot(stack[...], table_high[:, cols])
        potential[:, cols] = values[:rows]
        along = dot(stack[0:tall], table_along[:, cols])
        for k in range(width // LANES):
            a = n * (width // LANES) + k
            lanes = slice(k * LANES, (k + 1) * LANES)
            forms[a * tall : (a + 1) * tall] = along[:, lanes]
            forms[(CHUNKS + a) * tall : (CHUNKS + a + 1) * tall] = values[tall:, lanes]

    def gather_tile(t, carry):
        row = pl.multiple_of(t * 8, 8)
        for a in range(CHUNKS):
            both = [forms[pl.ds(pl.multiple_of((c * CHUNKS + a) * tall + row, 8), 8), :] for c in range(2)]
            field[t, :, a * LANES : (a + 1) * LANES] = jnp.concatenate(both, axis=0).astype(jnp.bfloat16)
        ends = [forms[pl.ds(c * CHUNKS * tall + row + 8, CHUNKS, stride=tall), :] for c in range(2)]
        rim[t, :, 0:LANES] = jnp.concatenate(ends, axis=0).astype(jnp.bfloat16)
        ends = [pltpu.roll(e, CHUNKS - 1, 0) for e in ends]
        rim[t, :, LANES : 2 * LANES] = jnp.concatenate(ends, axis=0).astype(jnp.bfloat16)
        return carry

    lax.fori_loop(0, tiles, gather_tile, 0, unroll=4)


def mesh_kernel(planes, pens, capacity, rows, owner_h, owner_row_h, band_h, count_h, cells_h, offsets_h, charges_h,
                table_high_h, table_low_h, table_along_h, lines_h, potential, out, forces, returned, packed, recv, heads_out, heads,
                heads_s, ids, owner, owner_row, band, block_count, cells, offsets, charges, tables_v, tables, links_v,
                links, chain, field, rim, wave, hi, lo, stack, forms, spectrum, sums, nexts, lasts, sums_of,
                nexts_of, lasts_of, table_high, table_low, table_along, lines, sems,
                send_sems, recv_sems, head_send_sems, head_recv_sems, back_send_sems, back_recv_sems, edge_send_sems,
                edge_recv_sems, side_send_sems, side_recv_sems):
    count = planes * pens
    total = count * capacity
    tall = 4 * capacity
    blocks = owner.shape[0]
    plane = lax.axis_index("pln")
    mine = lax.axis_index("pen")
    me = plane * pens + mine
    barrier = pltpu.get_barrier_semaphore()
    copies = fetch(
        (owner_h, owner_row_h, band_h, count_h, cells_h, offsets_h, charges_h, lines_h, table_high_h, table_low_h,
         table_along_h),
        (owner, owner_row, band.at[0:blocks], block_count.at[0:blocks], cells.at[0:blocks], offsets.at[0:blocks],
         charges.at[0:blocks], lines, table_high, table_low, table_along),
        sems,
    )

    def greet(k, carry):
        other = peer(lax.rem(me + k, count), pens)
        pl.semaphore_signal(barrier, inc=1, device_id=other, device_id_type=pl.DeviceIdType.MESH)
        return carry

    def note(s, carry):
        column = exclusive(plane, lax.rem(s, planes), planes)
        ids[s] = column * pens + exclusive(mine, lax.div(s, planes), pens)
        return carry

    lax.fori_loop(1, count, greet, 0, unroll=8)
    lax.fori_loop(0, count, note, 0, unroll=4)
    copies[0].wait()
    copies[1].wait()
    list_blocks(capacity, owner, owner_row, tables_v)
    tables_copy = pltpu.make_async_copy(tables_v, tables, sems.at[11])
    tables_copy.start()
    cells[blocks : blocks + 8] = jnp.zeros((8, LANES), jnp.int32)
    charges[blocks : blocks + 8] = jnp.zeros((8, LANES), jnp.float32)
    offsets[blocks] = jnp.zeros((2, LANES), jnp.float32)
    for copy in copies[2:7]:
        copy.wait()
    band[blocks] = 0
    block_count[blocks] = 0
    tables_copy.wait()

    def fill(s, carry):
        pack(s, ids[s], capacity, tables, band, block_count, cells, offsets, charges, packed, heads_out)
        return carry

    lax.fori_loop(0, count, fill, 0, unroll=4)
    recv[0, 0:tall] = packed[0]
    heads[0] = heads_out[0]
    chain[total] = jnp.zeros(chain.shape[1:], jnp.float32)
    pl.semaphore_wait(barrier, count - 1)

    def remote(s, source, place, send, receive):
        return pltpu.make_async_remote_copy(
            src_ref=source,
            dst_ref=place,
            send_sem=send.at[s],
            recv_sem=receive.at[s],
            device_id=peer(ids[s], pens),
            device_id_type=pl.DeviceIdType.MESH,
        )

    def head_copy(s):
        return remote(s, heads_out.at[s], heads.at[s], head_send_sems, head_recv_sems)

    def block_copy(s):
        return remote(s, packed.at[s], recv.at[s, 0:tall], send_sems, recv_sems)

    def back_copy(s):
        return remote(s, forces.at[s], returned.at[me], back_send_sems, back_recv_sems)

    def send_heads(s, carry):
        head_copy(s).start()
        return carry

    def send_blocks(s, carry):
        block_copy(s).start()
        return carry

    def take_heads(s, carry):
        head_copy(s).wait_recv()
        return carry

    lax.fori_loop(1, count, send_heads, 0, unroll=4)
    lax.fori_loop(1, count, send_blocks, 0, unroll=4)
    lax.fori_loop(1, count, take_heads, 0, unroll=4)
    heads_copy = pltpu.make_async_copy(heads, heads_s, sems.at[11])
    heads_copy.start()
    heads_copy.wait()
    link_blocks(heads_s, links_v, capacity)
    links_copy = pltpu.make_async_copy(links_v, links, sems.at[11])
    links_copy.start()
    links_copy.wait()

    bunch = 4

    def receive(first, number):
        sources = [first + k for k in range(number)]
        for s in sources:
            @pl.when(s > 0)
            def _():
                block_copy(s).wait_recv()

        deposit(sources, capacity, recv, chain, links)

    def receive_bunch(i, carry):
        receive(i * bunch, bunch)
        return carry

    lax.fori_loop(0, count // bunch - 1, receive_bunch, 0)
    for k in range(2):
        receive(count - bunch + k * (bunch // 2), bunch // 2)
    assemble(rows // 8, total, chain, links, hi, lo)
    for copy in copies[7:]:
        copy.wait()
    transform(rows, hi, lo, table_high, table_low, lines, spectrum, sums, nexts, lasts)
    sums_of[mine] = sums[...]

    def edge_copy(k, place, other):
        return pltpu.make_async_remote_copy(
            src_ref=sums,
            dst_ref=sums_of.at[place],
            send_sem=edge_send_sems.at[k],
            recv_sem=edge_recv_sems.at[k],
            device_id=(plane, other),
            device_id_type=pl.DeviceIdType.MESH,
        )

    def side_copy(n, source, place, other):
        return pltpu.make_async_remote_copy(
            src_ref=source,
            dst_ref=place,
            send_sem=side_send_sems.at[n],
            recv_sem=side_recv_sems.at[n],
            device_id=(plane, other),
            device_id_type=pl.DeviceIdType.MESH,
        )

    up_copy = side_copy(0, nexts, nexts_of, lax.rem(mine + pens - 1, pens))
    down_copy = side_copy(1, lasts, lasts_of, lax.rem(mine + 1, pens))
    for k in range(1, pens):
        edge_copy(k, mine, lax.rem(mine + k, pens)).start()
    up_copy.start()
    down_copy.start()
    local_scans(rows, spectrum, lines, wave)
    for k in range(1, pens):
        behind = lax.rem(mine - k + pens, pens)
        edge_copy(k, mine, lax.rem(mine + k, pens)).wait_send()
        edge_copy(k, behind, behind).wait_recv()
    up_copy.wait()
    down_copy.wait()
    finish_solve(rows, mine, sums_of, nexts_of, lasts_of, lines, wave, stack)
    invert(rows, stack, table_high, table_along, potential, forms, rim, field)
    sub8 = lax.broadcasted_iota(jnp.int32, (8, LANES), 0)
    sub16 = iota16()
    zero16 = jnp.zeros((16, LANES), jnp.bfloat16)

    def one(d, j):
        def spread(which):
            return recv[d, pl.ds(which * capacity + j, 8, stride=0), :]

        band = heads_s[d, 0, j]
        frac_y, weight, row, column, after, left, right = factors(
            spread(0), spread(1), spread(2), spread(3)
        )
        chunk = column >> 7
        index = (column & 127).astype(jnp.float32)
        spot, left16, right16 = doubled(index), doubled(left), doubled(right)
        next_spot = doubled(index + 1.0)
        picks = []
        for b in range(LANES // 16 + 1):
            here = sub16 + float(16 * b)
            picks.append(jnp.where(here == spot, left16, jnp.where(here == next_spot, right16, zero16)))
        picks += [zero16] * (2 * LANES // 16 - len(picks))
        rows_of = field[band]
        windows = [
            jnp.concatenate(
                [
                    rows_of[:, a * LANES : (a + 1) * LANES],
                    rows_of[:, (a + 1) % CHUNKS * LANES : ((a + 1) % CHUNKS + 1) * LANES],
                ],
                axis=1,
            )
            for a in range(CHUNKS)
        ]
        values = jnp.dot(
            jnp.concatenate(windows + [rim[band]], axis=0),
            jnp.concatenate(picks, axis=0),
            preferred_element_type=jnp.float32,
        )
        row_weight = weight * jnp.where(row == sub8, 1.0 - frac_y, jnp.where(row + 1 == sub8, frac_y, 0.0))
        mixed = [values[0:8], values[8:16]]
        for a in range(1, CHUNKS):
            held = chunk == a
            mixed = [jnp.where(held, values[a * 16 + c * 8 : a * 16 + c * 8 + 8], mixed[c]) for c in range(2)]
        edge = weight * jnp.where(row == 7, frac_y, 0.0)
        at_edge = sub8 == chunk
        rims = [jnp.where(at_edge, values[CHUNKS * 16 + c * 8 : CHUNKS * 16 + c * 8 + 8], 0.0) for c in range(2)]
        return [jnp.sum(row_weight * mixed[c] + edge * rims[c], axis=0, keepdims=True) for c in range(2)]

    def pull(sources):
        made = [[one(d, j) for j in range(capacity)] for d in sources]
        for d, results in zip(sources, made):
            keep(d, results)

    def keep(d, made):
        for c in range(2):
            for j in range(capacity):
                forces[d, c * capacity + j : c * capacity + j + 1, :] = made[j][c]
        if forces.shape[1] > 2 * capacity:
            forces[d, 2 * capacity :, :] = jnp.zeros((forces.shape[1] - 2 * capacity, LANES), jnp.float32)

    group = 4

    def step(i, carry):
        sources = [count - 1 - i * group - k for k in range(group)]
        pull(sources)
        for s in sources:
            back_copy(s).start()
        return carry

    lax.fori_loop(0, count // group - 1, step, 0)
    pull(list(range(group)))
    for s in range(1, group):
        back_copy(s).start()
    returned[me] = forces[0]

    def finish(i, carry):
        s = count - i
        head_copy(s).wait_send()
        block_copy(s).wait_send()
        back_copy(s).wait_send()
        back_copy(s).wait_recv()
        return carry

    lax.fori_loop(1, count, finish, 0, unroll=4)

    def take(n, carry):
        for k in range(8):
            i = n * 8 + k
            d, j = owner[i], tables[8, i]
            out[i, 0:1, :] = returned[d, pl.ds(j, 1), :]
            out[i, 1:2, :] = returned[d, pl.ds(capacity + j, 1), :]
        return carry

    lax.fori_loop(0, blocks // 8, take, 0, unroll=2)


def copy_kernel(potential_v, forces_v, potential, forces, sems):
    copies = fetch((potential_v, forces_v), (potential, forces), sems)
    for copy in copies:
        copy.wait()


def shards(block_owner, block_band, block_count, cells, offsets, charges):
    plane_count = lax.axis_size("pln")
    pen_count = lax.axis_size("pen")
    devices = plane_count * pen_count
    local_blocks, block_len = charges.shape
    capacity = max(2, 2 * local_blocks // devices)
    total = devices * capacity
    rows = NG // pen_count
    tall = 4 * capacity
    tall_back = round_up(2 * capacity, 8)
    vmem = pl.BlockSpec(memory_space=pltpu.VMEM)
    far = pl.BlockSpec(memory_space=pltpu.HBM)
    table_high, table_low, table_along = (jnp.asarray(t) for t in hartley_tables())
    lines = jnp.asarray(line_tables(pen_count))
    pairs = pltpu.SemaphoreType.DMA((devices,))
    potential, forces = pl.pallas_call(
        functools.partial(mesh_kernel, plane_count, pen_count, capacity, rows),
        out_shape=(
            pltpu.VMEM((rows, NG), jnp.float32),
            pltpu.VMEM((local_blocks, 2, block_len), jnp.float32),
        ),
        in_specs=[far] * 11,
        out_specs=(vmem, vmem),
        scratch_shapes=[
            pltpu.VMEM((devices, tall_back, LANES), jnp.float32),
            pltpu.VMEM((devices, tall_back, LANES), jnp.float32),
            pltpu.VMEM((devices, tall, LANES), jnp.float32),
            pltpu.VMEM((devices, tall + 8, LANES), jnp.float32),
            pltpu.VMEM((devices, 1, LANES), jnp.int32),
            pltpu.VMEM((devices, 1, LANES), jnp.int32),
            pltpu.SMEM((devices, 1, LANES), jnp.int32),
            pltpu.SMEM((devices,), jnp.int32),
            pltpu.SMEM((local_blocks,), jnp.int32),
            pltpu.VMEM((1, local_blocks), jnp.int32),
            pltpu.SMEM((local_blocks + 8,), jnp.int32),
            pltpu.SMEM((local_blocks + 8,), jnp.int32),
            pltpu.VMEM((local_blocks + 8, block_len), jnp.int32),
            pltpu.VMEM((local_blocks + 8, 2, block_len), jnp.float32),
            pltpu.VMEM((local_blocks + 8, block_len), jnp.float32),
            pltpu.VMEM((16, LANES), jnp.int32),
            pltpu.SMEM((16, LANES), jnp.int32),
            pltpu.VMEM((16, LANES), jnp.int32),
            pltpu.SMEM((16, LANES), jnp.int32),
            pltpu.VMEM((total + 1, CHUNKS * 8 + 16, LANES), jnp.float32),
            pltpu.VMEM((rows // 8, 16, NG), jnp.bfloat16),
            pltpu.VMEM((rows // 8, 16, 2 * LANES), jnp.bfloat16),
            pltpu.VMEM((CHUNKS, rows + 32, LANES), jnp.float32),
            pltpu.VMEM((rows + 16, NG), jnp.bfloat16),
            pltpu.VMEM((rows + 16, NG), jnp.bfloat16),
            pltpu.VMEM((2 * rows + 32, NG), jnp.bfloat16),
            pltpu.VMEM((2 * CHUNKS * (rows + 16), LANES), jnp.float32),
            pltpu.VMEM((rows, NG), jnp.float32),
            pltpu.VMEM((3, 1, NG), jnp.float32),
            pltpu.VMEM((2, 1, NG), jnp.float32),
            pltpu.VMEM((1, 1, NG), jnp.float32),
            pltpu.VMEM((pen_count, 3, 1, NG), jnp.float32),
            pltpu.VMEM((2, 1, NG), jnp.float32),
            pltpu.VMEM((1, 1, NG), jnp.float32),
            pltpu.VMEM((NG, NG), jnp.bfloat16),
            pltpu.VMEM((NG, NG), jnp.bfloat16),
            pltpu.VMEM((NG, NG), jnp.bfloat16),
            pltpu.VMEM(lines.shape, jnp.float32),
            pltpu.SemaphoreType.DMA((13,)),
            pairs,
            pairs,
            pairs,
            pairs,
            pairs,
            pairs,
            pltpu.SemaphoreType.DMA((pen_count,)),
            pltpu.SemaphoreType.DMA((pen_count,)),
            pltpu.SemaphoreType.DMA((2,)),
            pltpu.SemaphoreType.DMA((2,)),
        ],
        compiler_params=pltpu.CompilerParams(
            collective_id=0, has_side_effects=True, vmem_limit_bytes=VMEM_LIMIT
        ),
        name="mesh",
    )(
        block_owner[:, 0],
        block_owner.reshape(1, local_blocks),
        block_band,
        block_count,
        cells,
        offsets,
        charges,
        table_high,
        table_low,
        table_along,
        lines,
    )
    potential = pltpu.with_memory_space_constraint(potential, pltpu.VMEM)
    forces = pltpu.with_memory_space_constraint(forces, pltpu.VMEM)
    potential, forces = pl.pallas_call(
        copy_kernel,
        out_shape=(
            jax.ShapeDtypeStruct(potential.shape, jnp.float32),
            jax.ShapeDtypeStruct(forces.shape, jnp.float32),
        ),
        in_specs=[pl.BlockSpec(memory_space=pl.ANY)] * 2,
        out_specs=(far, far),
        scratch_shapes=[pltpu.SemaphoreType.DMA((2,))],
        name="copy",
    )(potential, forces)
    return (potential[None], forces)


def solution(mesh):
    placed = (
        P(("pln", "pen"), None),
        P(("pln", "pen")),
        P(("pln", "pen")),
        P(("pln", "pen"), None),
        P(("pln", "pen"), None, None),
        P(("pln", "pen"), None),
    )
    return jax.shard_map(
        shards,
        mesh=mesh,
        in_specs=placed,
        out_specs=(P("pln", "pen", None), P(("pln", "pen"), None, None)),
        check_vma=False,
    )
```
